512 devices in a mesh: grp: 4 (over x), gx: 8 (over y_hi, core), gy: 16 (over z, y_lo).
Axes of the slice: x: 4, y: 8 (y_hi: 4, y_lo: 2; y = y_hi * 2 + y_lo), z: 8, core: 2. Of those that a mesh axis runs over, the one named last changes fastest.
Arguments:
- source_term: float32 [64, 256, 1024], P('gx', 'gy', 'grp'), may hold values from -6 to 6
- conductivity: float32 [64, 256, 1024], P('gx', 'gy', 'grp'), may hold values from 0.5 to 4
- initial_field: float32 [64, 256, 1024], P('gx', 'gy', 'grp'), may hold values from -6 to 6
Outputs:
- solution: float32 [64, 256, 1024], P('gx', 'gy', 'grp')
The draws below stay inside these ranges and needn't reach their ends.
All inputs are finite; a program needn't handle non-finite values.
Results may differ from the reference program's by a relative error of at most 0.0001.
Values sent between devices are 32-bit elements; how exact they have to be, the bound alone decides.
A program may use at most 64 MiB of HBM per device.

```python
import math
import jax
import jax.numpy as jnp

ITERS = 2
NX = 64
NY = 256
NZ = 1024


def shard_levels(key, dims, cuts, least, largest):
    loudness = 1.0
    for dim, blocks in cuts:
        draws = jax.random.uniform(jax.random.fold_in(jax.random.fold_in(key, 6), dim), (blocks,), jnp.float32, least / len(cuts), largest / len(cuts))
        loudness = loudness * jnp.repeat(jnp.exp(draws), dims[dim] // blocks).reshape((-1,) + (1,) * (len(dims) - 1 - dim))
    return loudness


def normal_values(own_key, shape, scale, bound, cuts=(), dtype=jnp.bfloat16):
    loudness = shard_levels(own_key, shape, cuts, -0.22, 0.18) if cuts else 1.0
    array = jax.random.normal(own_key, shape, jnp.float32) * scale * loudness
    return jnp.minimum(jnp.maximum(array, -bound), bound).astype(dtype)


def setup_inputs(seed: int = 0) -> dict:
    arg_keys = jax.random.split(jax.random.key(seed), 4)
    return {
        "source_term": normal_values(arg_keys[0], (NX, NY, NZ), 1.0, 6.0, ((0, 8), (1, 16), (2, 4)), jnp.float32),
        "conductivity": jnp.clip(jnp.exp(math.log(4.0) - 2.0794415 * jax.random.uniform(arg_keys[1], (NX, NY, NZ), jnp.float32) ** shard_levels(arg_keys[1], (NX, NY, NZ), ((0, 8), (1, 16), (2, 4)), -0.2, 0.2)), 0.5, 4.0),
        "initial_field": normal_values(arg_keys[2], (NX, NY, NZ), 1.0, 6.0, ((0, 8), (1, 16), (2, 4)), jnp.float32),
    }


FIRST_RATE = 0.8
CARRY_RATE = 9.0 / 41.0
FRESH_RATE = 40.0 / 41.0


def neighbours(padded):
    return [padded[:-2, 1:-1, 1:-1], padded[2:, 1:-1, 1:-1],
            padded[1:-1, :-2, 1:-1], padded[1:-1, 2:, 1:-1],
            padded[1:-1, 1:-1, :-2], padded[1:-1, 1:-1, 2:]]


def apply_operator(field_pad, cond_pad):
    center_field = field_pad[1:-1, 1:-1, 1:-1]
    center_cond = cond_pad[1:-1, 1:-1, 1:-1]
    result = jnp.zeros_like(center_field)
    for near_field, near_cond in zip(neighbours(field_pad), neighbours(cond_pad)):
        result = result + 0.5 * (center_cond + near_cond) * (center_field - near_field)
    return result


def diagonal_of(cond_pad):
    center_cond = cond_pad[1:-1, 1:-1, 1:-1]
    result = jnp.zeros_like(center_cond)
    for near_cond in neighbours(cond_pad):
        result = result + 0.5 * (center_cond + near_cond)
    return result


def block_mean(field):
    sizea, sizeb, sizec = field.shape
    return field.reshape(sizea // 2, 2, sizeb // 2, 2, sizec // 2, 2).mean(axis=(1, 3, 5))


def prolong(coarse):
    sizea, sizeb, sizec = coarse.shape
    spread = jnp.broadcast_to(coarse[:, None, :, None, :, None], (sizea, 2, sizeb, 2, sizec, 2))
    return spread.reshape(2 * sizea, 2 * sizeb, 2 * sizec)


def smooth(residual, cond_pad, scale):
    diagonal = scale * diagonal_of(cond_pad)
    first = FIRST_RATE * residual / diagonal
    image = scale * apply_operator(jnp.pad(first, 1), cond_pad)
    second = CARRY_RATE * first + FRESH_RATE * (residual - image) / diagonal
    return first + second


def reference(source_term, conductivity, initial_field):
    cond_pad = jnp.pad(conductivity, 1)
    coarse_pad = jnp.pad(block_mean(conductivity), 1)
    field = initial_field
    for iteration in range(ITERS):
        residual = source_term - apply_operator(jnp.pad(field, 1), cond_pad)
        fine_corr = smooth(residual, cond_pad, 1.0)
        coarse_corr = smooth(block_mean(residual), coarse_pad, 0.25)
        field = field + fine_corr + prolong(coarse_corr)
    return field
```

```python
import functools

import jax
import jax.numpy as jnp
from jax import lax
from jax.experimental import pallas as pl
from jax.experimental.pallas import tpu as pltpu
from jax.sharding import PartitionSpec as P

MESH = pl.DeviceIdType.MESH
F32 = jnp.float32

NX, NY, NZ = 8, 16, 256
CX = NX // 2
ROWS = NX * NY
HALVES = (0, 1)
TILES = (0, 1)

FIRST_RATE = 0.8
KEEP = 60.0 / 41.0
FRESH = 40.0 / 41.0

FACES = (("gx", -1), ("gx", 1), ("gy", -1), ("gy", 1), ("grp", -1), ("grp", 1))
SIZES = (9, 9, 5, 5, 2, 2)
ROUND_SIZES = (SIZES, (5, 5, 3, 3, 1, 1), (4, 4, 2, 2, 1, 1), (5, 5, 3, 3, 1, 1))
OFFSETS = (0, 9, 18, 23, 28, 30)
SLOTS = 32
SECOND = (5, 5, 3, 3, 1, 1)


def iota(shape, dim):
    return lax.broadcasted_iota(jnp.int32, shape, dim)


def kernel(source_hbm, cond_hbm, field_hbm, out_hbm, source, half_cond, field, first, out, ky_lo, ky_hi, kz_lo, kz_hi,
           diag, inverse, partial, coarse_half, cky_lo, cky_hi, ckz_lo, ckz_hi, coarse_diag, coarse_inverse, coarse_first,
           faces, gains, sent, received, in_sem, out_sem, send_sem, recv_sem):
    sub, lane = iota((2, 8, 128), 1), iota((2, 8, 128), 2)
    sub2, lane2 = iota((8, 128), 0), iota((8, 128), 1)
    even_sub, even_lane = sub % 2 == 0, lane % 2 == 0
    even_sub2, even_lane2 = sub2 % 2 == 0, lane2 % 2 == 0
    zero = jnp.zeros((1, 8, 128), F32)
    zero2 = jnp.zeros((2, 8, 128), F32)

    place = {name: lax.axis_index(name) for name in ("grp", "gx", "gy")}
    size = {name: lax.axis_size(name) for name in ("grp", "gx", "gy")}
    present = []
    for name, step in FACES:
        present.append(place[name] > 0 if step < 0 else place[name] < size[name] - 1)

    def plane(ref, half, x):
        return ref[half, NY * x : NY * (x + 1), :].reshape(2, 8, 128)

    def put(ref, half, x, value):
        ref[half, NY * x : NY * (x + 1), :] = value.reshape(16, 128)

    def y_lower(p, width=1):
        rolled = pltpu.roll(p, width, 1)
        return jnp.where(sub < width, jnp.concatenate([zero, rolled[:1]], axis=0), rolled)

    def y_upper(p, width=1):
        rolled = pltpu.roll(p, 8 - width, 1)
        return jnp.where(sub >= 8 - width, jnp.concatenate([rolled[1:], zero], axis=0), rolled)

    def z_lower(p0, p1, width=1):
        r0, r1 = pltpu.roll(p0, width, 2), pltpu.roll(p1, width, 2)
        return jnp.where(lane < width, 0.0, r0), jnp.where(lane < width, r0, r1)

    def z_upper(p0, p1, width=1):
        r0, r1 = pltpu.roll(p0, 128 - width, 2), pltpu.roll(p1, 128 - width, 2)
        return jnp.where(lane >= 128 - width, r1, r0), jnp.where(lane >= 128 - width, 0.0, r1)

    def neighbour_sum(ref, half_ref, kyl, kyh, kzl, kzh, x, count, width):
        p = [plane(ref, h, x) for h in HALVES]
        zl, zh = z_lower(p[0], p[1], width), z_upper(p[0], p[1], width)
        here = [plane(half_ref, h, x) for h in HALVES]
        total = []
        for h in HALVES:
            s = plane(kyl, h, x) * y_lower(p[h], width) + plane(kyh, h, x) * y_upper(p[h], width)
            s = s + (plane(kzl, h, x) * zl[h] + plane(kzh, h, x) * zh[h])
            if x > 0:
                s = s + (here[h] + plane(half_ref, h, x - 1)) * plane(ref, h, x - 1)
            if x < count - 1:
                s = s + (here[h] + plane(half_ref, h, x + 1)) * plane(ref, h, x + 1)
            total.append(s)
        return total

    def fine_neighbours(ref, x):
        return neighbour_sum(ref, half_cond, ky_lo, ky_hi, kz_lo, kz_hi, x, NX, 1)

    def coarse_neighbours(ref, x):
        return neighbour_sum(ref, coarse_half, cky_lo, cky_hi, ckz_lo, ckz_hi, x, CX, 2)

    def coefficients(ref, kyl, kyh, kzl, kzh, diag_ref, x, count, width):
        p = [plane(ref, h, x) for h in HALVES]
        zl, zh = z_lower(p[0], p[1], width), z_upper(p[0], p[1], width)
        for h in HALVES:
            yl, yh = y_lower(p[h], width), y_upper(p[h], width)
            put(kyl, h, x, p[h] + yl)
            put(kyh, h, x, p[h] + yh)
            put(kzl, h, x, p[h] + zl[h])
            put(kzh, h, x, p[h] + zh[h])
            s = 6.0 * p[h] + ((yl + yh) + (zl[h] + zh[h]))
            if x > 0:
                s = s + plane(ref, h, x - 1)
            if x < count - 1:
                s = s + plane(ref, h, x + 1)
            put(diag_ref, h, x, s)

    def restrict(lower, upper):
        s = lower + upper
        s = s + jnp.where(even_sub, pltpu.roll(s, 7, 1), pltpu.roll(s, 1, 1))
        s = s + jnp.where(even_lane, pltpu.roll(s, 127, 2), pltpu.roll(s, 1, 2))
        return 0.125 * s

    def message(store, turn, face):
        return store.at[turn, pl.ds(OFFSETS[face], ROUND_SIZES[turn][face])]

    def slot(face, index):
        return OFFSETS[face] + index

    def pack_fine(ref, turn, second):
        for face, x in ((0, 0), (1, NX - 1)):
            base = slot(face, SECOND[face] if second else 0)
            for h in HALVES:
                sent[turn, base + 2 * h : base + 2 * h + 2] = plane(ref, h, x)
        for face, row in ((2, 0), (3, NY - 1)):
            base = slot(face, SECOND[face] if second else 0)
            for h in HALVES:
                sent[turn, base + h] = ref[h, pl.ds(row, NX, stride=NY), :]
        columns = []
        for face, h, source_lane in ((4, 0, 0), (5, 1, 127)):
            packed = jnp.zeros((8, 128), F32)
            for x in range(NX):
                p = plane(ref, h, x)
                for t in TILES:
                    m = 2 * x + t
                    packed = jnp.where(lane2 == m, pltpu.roll(p[t], (m - source_lane) % 128, 1), packed)
            columns.append(packed)
        return columns

    def pack_coarse(ref, turn, columns):
        for face, x in ((0, 0), (1, CX - 1)):
            p = [plane(ref, h, x) for h in HALVES]
            sent[turn, slot(face, 4)] = jnp.where(
                even_sub2, jnp.where(even_lane2, p[0][0], p[1][0]), jnp.where(even_lane2, p[0][1], p[1][1]))
        for face, row in ((2, 0), (3, NY - 1)):
            for h in HALVES:
                sent[turn, slot(face, 2), CX * h : CX * (h + 1), :] = ref[h, pl.ds(row, CX, stride=NY), :]
        packed_columns = []
        for packed, (face, h, source_lane) in zip(columns, ((4, 0, 0), (5, 1, 127))):
            for x in range(CX):
                p = plane(ref, h, x)
                for t in TILES:
                    m = 16 + 2 * x + t
                    packed = jnp.where(lane2 == m, pltpu.roll(p[t], (m - source_lane) % 128, 1), packed)
            packed_columns.append(packed)
        return packed_columns

    def store_columns(turn, columns, index):
        for face, packed in zip((4, 5), columns):
            sent[turn, slot(face, index)] = packed

    def spread_fine(q, half, x):
        rows = jnp.concatenate([
            jnp.broadcast_to(q[slot(2, half), x : x + 1, :], (8, 128))[None],
            jnp.broadcast_to(q[slot(3, half), x : x + 1, :], (8, 128))[None],
        ], axis=0)
        tile = iota((2, 8, 128), 0)
        out_ = jnp.where(sub == 7 * tile, rows, 0.0)
        column = q[slot(4 + half, 0)]
        columns = jnp.concatenate([
            jnp.broadcast_to(column[:, 2 * x + t : 2 * x + t + 1], (8, 128))[None] for t in TILES], axis=0)
        out_ = out_ + jnp.where(lane == 127 * half, columns, 0.0)
        if x == 0:
            out_ = out_ + q[slot(0, 2 * half) : slot(0, 2 * half) + 2]
        if x == NX - 1:
            out_ = out_ + q[slot(1, 2 * half) : slot(1, 2 * half) + 2]
        return out_

    def spread_coarse_plane(q, face):
        packed = q[slot(face, 4)]
        by_half = (jnp.where(even_lane2, packed, pltpu.roll(packed, 1, 1)),
                   jnp.where(even_lane2, pltpu.roll(packed, 127, 1), packed))
        return [jnp.concatenate([jnp.where(even_sub2, p, pltpu.roll(p, 1, 0))[None],
                                 jnp.where(even_sub2, pltpu.roll(p, 7, 0), p)[None]], axis=0) for p in by_half]

    def spread_coarse(q, half, x, planes):
        rows = jnp.concatenate([
            jnp.broadcast_to(q[slot(face, 2), CX * half + x : CX * half + x + 1, :], (8, 128))[None] for face in (2, 3)],
            axis=0)
        tile = iota((2, 8, 128), 0)
        out_ = jnp.where((sub // 2) == 3 * tile, rows, 0.0)
        column = q[slot(4 + half, 0)]
        columns = jnp.concatenate([
            jnp.broadcast_to(column[:, 16 + 2 * x + t : 17 + 2 * x + t], (8, 128))[None] for t in TILES], axis=0)
        out_ = out_ + jnp.where((lane // 2) == 63 * half, columns, 0.0)
        if x == 0:
            out_ = out_ + planes[0][half]
        if x == CX - 1:
            out_ = out_ + planes[1][half]
        return out_

    def peer(face):
        name, step = FACES[face]
        return {name: place[name] + step}

    def copy(turn, face):
        return pltpu.make_async_remote_copy(
            src_ref=message(sent, turn, face),
            dst_ref=message(received, turn, face ^ 1),
            send_sem=send_sem.at[turn, face],
            recv_sem=recv_sem.at[turn, face ^ 1],
            device_id=peer(face),
            device_id_type=MESH,
        )

    def arrival(turn, face):
        return pltpu.make_async_remote_copy(
            src_ref=message(sent, turn, face),
            dst_ref=message(received, turn, face),
            send_sem=send_sem.at[turn, face],
            recv_sem=recv_sem.at[turn, face],
            device_id=peer(face),
            device_id_type=MESH,
        )

    ORDER = (1, 0, 3, 2, 5, 4)

    def send(turn):
        for face in ORDER:
            @pl.when(present[face])
            def _():
                copy(turn, face).start()

    def wait(turn):
        for face in (5, 4, 3, 2, 1, 0):
            @pl.when(present[face])
            def _():
                arrival(turn, face).wait_recv()

    barrier = pltpu.get_barrier_semaphore()
    for face in range(6):
        @pl.when(present[face])
        def _():
            pl.semaphore_signal(barrier, inc=1, device_id=peer(face), device_id_type=MESH)

    loads = []
    for index, (hbm, ref) in enumerate(((cond_hbm, half_cond), (field_hbm, field), (source_hbm, source))):
        pair = []
        for h in HALVES:
            load = pltpu.make_async_copy(hbm.at[:, pl.ds(128 * h, 128)], ref.at[h], in_sem.at[index, h])
            load.start()
            pair.append(load)
        loads.append(pair)

    for face in range(6):
        @pl.when(jnp.logical_not(present[face]))
        def _():
            for turn in range(4):
                count = ROUND_SIZES[turn][face]
                received[turn, OFFSETS[face] : OFFSETS[face] + count] = jnp.zeros((count, 8, 128), F32)

    for load in loads[0]:
        load.wait()
    for x in range(NX):
        for h in HALVES:
            put(half_cond, h, x, 0.5 * plane(half_cond, h, x))
    for x in range(CX):
        for h in HALVES:
            put(coarse_half, h, x, restrict(plane(half_cond, h, 2 * x), plane(half_cond, h, 2 * x + 1)))
    store_columns(0, pack_coarse(coarse_half, 0, pack_fine(half_cond, 0, False)), 0)
    for load in loads[1]:
        load.wait()
    store_columns(0, pack_fine(field, 0, True), 1)

    pl.semaphore_wait(barrier, sum(p.astype(jnp.int32) for p in present))
    send(0)

    for x in range(NX):
        coefficients(half_cond, ky_lo, ky_hi, kz_lo, kz_hi, diag, x, NX, 1)
    for x in range(CX):
        coefficients(coarse_half, cky_lo, cky_hi, ckz_lo, ckz_hi, coarse_diag, x, CX, 2)
    for load in loads[2]:
        load.wait()

    def residual_part():
        for x in range(NX):
            total = fine_neighbours(field, x)
            for h in HALVES:
                put(partial, h, x, plane(source, h, x) - plane(diag, h, x) * plane(field, h, x) + total[h])

    residual_part()

    wait(0)
    for face in range(6):
        base, own, two = OFFSETS[face], SECOND[face], SECOND[face] - 1
        for i in range(own):
            gain = sent[0, base + i] + received[0, base + i]
            gains[base + i] = gain
        for i in range(SIZES[face] - own):
            faces[base + i] = (gains[base + i] * received[0, base + own + i]
                               - received[0, base + i] * sent[0, base + own + i])

    jplanes = (spread_coarse_plane(received.at[0], 0), spread_coarse_plane(received.at[0], 1))
    for x in range(CX):
        for h in HALVES:
            total = plane(coarse_diag, h, x) + spread_coarse(received.at[0], h, x, jplanes)
            put(coarse_inverse, h, x, 1.0 / total)
    for x in range(NX):
        for h in HALVES:
            total = plane(diag, h, x) + spread_fine(received.at[0], h, x)
            put(diag, h, x, total)
            put(inverse, h, x, 1.0 / total)

    for iteration in range(2):
        turn = 2 * iteration + 1
        if iteration > 0:
            wait(2)
            for face in range(6):
                base = OFFSETS[face]
                for i in range(ROUND_SIZES[2][face]):
                    faces[base + i] = gains[base + i] * received[2, base + i]
        for x in range(CX):
            for h in HALVES:
                pair = []
                for fx in (2 * x, 2 * x + 1):
                    r = plane(partial, h, fx) + spread_fine(faces, h, fx)
                    put(first, h, fx, FIRST_RATE * plane(inverse, h, fx) * r)
                    pair.append(r)
                put(coarse_first, h, x, 4.0 * FIRST_RATE * plane(coarse_inverse, h, x) * restrict(*pair))
        store_columns(turn, pack_coarse(coarse_first, turn, pack_fine(first, turn, False)), 0)
        send(turn)

        for x in range(CX):
            total = coarse_neighbours(coarse_first, x)
            coarse = [KEEP * plane(coarse_first, h, x) + FRESH * plane(coarse_inverse, h, x) * total[h] for h in HALVES]
            for fx in (2 * x, 2 * x + 1):
                total = fine_neighbours(first, fx)
                for h in HALVES:
                    fine = KEEP * plane(first, h, fx) + FRESH * plane(inverse, h, fx) * total[h]
                    put(partial, h, fx, plane(field, h, fx) + fine + coarse[h])

        wait(turn)
        for face in range(6):
            base = OFFSETS[face]
            for i in range(ROUND_SIZES[turn][face]):
                faces[base + i] = (FRESH * gains[base + i]) * received[turn, base + i]
        planes = (spread_coarse_plane(faces, 0), spread_coarse_plane(faces, 1))
        target = out if iteration == 1 else field
        for x in range(CX):
            for h in HALVES:
                coarse = plane(coarse_inverse, h, x) * spread_coarse(faces, h, x, planes)
                for fx in (2 * x, 2 * x + 1):
                    fine = plane(inverse, h, fx) * spread_fine(faces, h, fx)
                    put(target, h, fx, plane(partial, h, fx) + fine + coarse)
        if iteration == 0:
            store_columns(2, pack_fine(field, 2, False), 0)
            send(2)
            residual_part()

    stores = [pltpu.make_async_copy(out.at[h], out_hbm.at[:, pl.ds(128 * h, 128)], out_sem.at[h]) for h in HALVES]
    for store in stores:
        store.start()
    for turn in range(4):
        for face in range(6):
            @pl.when(present[face])
            def _():
                copy(turn, face).wait_send()
    for store in stores:
        store.wait()


def block(source_term, conductivity, initial_field):
    def fine():
        return pltpu.VMEM((2, ROWS, 128), F32)

    def coarse():
        return pltpu.VMEM((2, CX * NY, 128), F32)

    hbm = pl.BlockSpec(memory_space=pltpu.HBM)
    result = pl.pallas_call(
        kernel,
        out_shape=jax.ShapeDtypeStruct((ROWS, NZ), F32),
        in_specs=[hbm] * 3,
        out_specs=hbm,
        scratch_shapes=[
            *(fine() for _ in range(12)),
            *(coarse() for _ in range(8)),
            pltpu.VMEM((SLOTS, 8, 128), F32),
            pltpu.VMEM((SLOTS, 8, 128), F32),
            pltpu.VMEM((4, SLOTS, 8, 128), F32),
            pltpu.VMEM((4, SLOTS, 8, 128), F32),
            pltpu.SemaphoreType.DMA((3, 2)),
            pltpu.SemaphoreType.DMA((2,)),
            pltpu.SemaphoreType.DMA((4, 6)),
            pltpu.SemaphoreType.DMA((4, 6)),
        ],
        compiler_params=pltpu.CompilerParams(collective_id=0, has_side_effects=True),
    )(*(a.reshape(ROWS, NZ) for a in (source_term, conductivity, initial_field)))
    return result.reshape(NX, NY, NZ)


def solution(mesh):
    spec = P("gx", "gy", "grp")
    return jax.shard_map(block, mesh=mesh, in_specs=(spec,) * 3, out_specs=spec, check_vma=False)
```

```python
import functools

import jax
import jax.numpy as jnp
from jax import lax
from jax.experimental import pallas as pl
from jax.experimental.pallas import tpu as pltpu
from jax.sharding import PartitionSpec as P

MESH = pl.DeviceIdType.MESH
F32 = jnp.float32

NX, NY, NZ = 8, 16, 256
CX = NX // 2
ROWS = NX * NY
HALVES = (0, 1)
TILES = (0, 1)

FIRST_RATE = 0.8
KEEP = 60.0 / 41.0
FRESH = 40.0 / 41.0

FACES = (("gx", -1), ("gx", 1), ("gy", -1), ("gy", 1), ("grp", -1), ("grp", 1))
SIZES = (9, 9, 5, 5, 2, 2)
ROUND_SIZES = (SIZES, (5, 5, 3, 3, 1, 1), (4, 4, 2, 2, 1, 1), (5, 5, 3, 3, 1, 1))
OFFSETS = (0, 9, 18, 23, 28, 30)
SLOTS = 32
SECOND = (5, 5, 3, 3, 1, 1)


def iota(shape, dim):
    return lax.broadcasted_iota(jnp.int32, shape, dim)


def kernel(source_hbm, cond_hbm, field_hbm, out, source, half_cond, field, first, ky_lo, ky_hi, kz_lo, kz_hi,
           diag, inverse, partial, coarse_half, cky_lo, cky_hi, ckz_lo, ckz_hi, coarse_diag, coarse_inverse, coarse_first,
           faces, gains, sent, received, in_sem, send_sem, recv_sem):
    sub, lane = iota((2, 8, 128), 1), iota((2, 8, 128), 2)
    sub2, lane2 = iota((8, 128), 0), iota((8, 128), 1)
    even_sub, even_lane = sub % 2 == 0, lane % 2 == 0
    even_sub2, even_lane2 = sub2 % 2 == 0, lane2 % 2 == 0
    zero = jnp.zeros((1, 8, 128), F32)
    zero2 = jnp.zeros((2, 8, 128), F32)

    place = {name: lax.axis_index(name) for name in ("grp", "gx", "gy")}
    size = {name: lax.axis_size(name) for name in ("grp", "gx", "gy")}
    present = []
    for name, step in FACES:
        present.append(place[name] > 0 if step < 0 else place[name] < size[name] - 1)

    def plane(ref, half, x):
        return ref[half, NY * x : NY * (x + 1), :].reshape(2, 8, 128)

    def put(ref, half, x, value):
        ref[half, NY * x : NY * (x + 1), :] = value.reshape(16, 128)

    def y_lower(p, width=1):
        rolled = pltpu.roll(p, width, 1)
        return jnp.where(sub < width, jnp.concatenate([zero, rolled[:1]], axis=0), rolled)

    def y_upper(p, width=1):
        rolled = pltpu.roll(p, 8 - width, 1)
        return jnp.where(sub >= 8 - width, jnp.concatenate([rolled[1:], zero], axis=0), rolled)

    def z_lower(p0, p1, width=1):
        r0, r1 = pltpu.roll(p0, width, 2), pltpu.roll(p1, width, 2)
        return jnp.where(lane < width, 0.0, r0), jnp.where(lane < width, r0, r1)

    def z_upper(p0, p1, width=1):
        r0, r1 = pltpu.roll(p0, 128 - width, 2), pltpu.roll(p1, 128 - width, 2)
        return jnp.where(lane >= 128 - width, r1, r0), jnp.where(lane >= 128 - width, 0.0, r1)

    def neighbour_sum(ref, half_ref, kyl, kyh, kzl, kzh, x, count, width):
        p = [plane(ref, h, x) for h in HALVES]
        zl, zh = z_lower(p[0], p[1], width), z_upper(p[0], p[1], width)
        here = [plane(half_ref, h, x) for h in HALVES]
        total = []
        for h in HALVES:
            s = plane(kyl, h, x) * y_lower(p[h], width) + plane(kyh, h, x) * y_upper(p[h], width)
            s = s + (plane(kzl, h, x) * zl[h] + plane(kzh, h, x) * zh[h])
            if x > 0:
                s = s + (here[h] + plane(half_ref, h, x - 1)) * plane(ref, h, x - 1)
            if x < count - 1:
                s = s + (here[h] + plane(half_ref, h, x + 1)) * plane(ref, h, x + 1)
            total.append(s)
        return total

    def fine_neighbours(ref, x):
        return neighbour_sum(ref, half_cond, ky_lo, ky_hi, kz_lo, kz_hi, x, NX, 1)

    def coarse_neighbours(ref, x):
        return neighbour_sum(ref, coarse_half, cky_lo, cky_hi, ckz_lo, ckz_hi, x, CX, 2)

    def coefficients(ref, kyl, kyh, kzl, kzh, diag_ref, x, count, width):
        p = [plane(ref, h, x) for h in HALVES]
        zl, zh = z_lower(p[0], p[1], width), z_upper(p[0], p[1], width)
        for h in HALVES:
            yl, yh = y_lower(p[h], width), y_upper(p[h], width)
            put(kyl, h, x, p[h] + yl)
            put(kyh, h, x, p[h] + yh)
            put(kzl, h, x, p[h] + zl[h])
            put(kzh, h, x, p[h] + zh[h])
            s = 6.0 * p[h] + ((yl + yh) + (zl[h] + zh[h]))
            if x > 0:
                s = s + plane(ref, h, x - 1)
            if x < count - 1:
                s = s + plane(ref, h, x + 1)
            put(diag_ref, h, x, s)

    def restrict(lower, upper):
        s = lower + upper
        s = s + jnp.where(even_sub, pltpu.roll(s, 7, 1), pltpu.roll(s, 1, 1))
        s = s + jnp.where(even_lane, pltpu.roll(s, 127, 2), pltpu.roll(s, 1, 2))
        return 0.125 * s

    def message(store, turn, face):
        return store.at[turn, pl.ds(OFFSETS[face], ROUND_SIZES[turn][face])]

    def slot(face, index):
        return OFFSETS[face] + index

    def pack_fine(ref, turn, second):
        for face, x in ((0, 0), (1, NX - 1)):
            base = slot(face, SECOND[face] if second else 0)
            for h in HALVES:
                sent[turn, base + 2 * h : base + 2 * h + 2] = plane(ref, h, x)
        for face, row in ((2, 0), (3, NY - 1)):
            base = slot(face, SECOND[face] if second else 0)
            for h in HALVES:
                sent[turn, base + h] = ref[h, pl.ds(row, NX, stride=NY), :]
        columns = []
        for face, h, source_lane in ((4, 0, 0), (5, 1, 127)):
            packed = jnp.zeros((8, 128), F32)
            for x in range(NX):
                p = plane(ref, h, x)
                for t in TILES:
                    m = 2 * x + t
                    packed = jnp.where(lane2 == m, pltpu.roll(p[t], (m - source_lane) % 128, 1), packed)
            columns.append(packed)
        return columns

    def pack_coarse(ref, turn, columns):
        for face, x in ((0, 0), (1, CX - 1)):
            p = [plane(ref, h, x) for h in HALVES]
            sent[turn, slot(face, 4)] = jnp.where(
                even_sub2, jnp.where(even_lane2, p[0][0], p[1][0]), jnp.where(even_lane2, p[0][1], p[1][1]))
        for face, row in ((2, 0), (3, NY - 1)):
            for h in HALVES:
                sent[turn, slot(face, 2), CX * h : CX * (h + 1), :] = ref[h, pl.ds(row, CX, stride=NY), :]
        packed_columns = []
        for packed, (face, h, source_lane) in zip(columns, ((4, 0, 0), (5, 1, 127))):
            for x in range(CX):
                p = plane(ref, h, x)
                for t in TILES:
                    m = 16 + 2 * x + t
                    packed = jnp.where(lane2 == m, pltpu.roll(p[t], (m - source_lane) % 128, 1), packed)
            packed_columns.append(packed)
        return packed_columns

    def store_columns(turn, columns, index):
        for face, packed in zip((4, 5), columns):
            sent[turn, slot(face, index)] = packed

    def spread_fine(q, half, x):
        rows = jnp.concatenate([
            jnp.broadcast_to(q[slot(2, half), x : x + 1, :], (8, 128))[None],
            jnp.broadcast_to(q[slot(3, half), x : x + 1, :], (8, 128))[None],
        ], axis=0)
        tile = iota((2, 8, 128), 0)
        out_ = jnp.where(sub == 7 * tile, rows, 0.0)
        column = q[slot(4 + half, 0)]
        columns = jnp.concatenate([
            jnp.broadcast_to(column[:, 2 * x + t : 2 * x + t + 1], (8, 128))[None] for t in TILES], axis=0)
        out_ = out_ + jnp.where(lane == 127 * half, columns, 0.0)
        if x == 0:
            out_ = out_ + q[slot(0, 2 * half) : slot(0, 2 * half) + 2]
        if x == NX - 1:
            out_ = out_ + q[slot(1, 2 * half) : slot(1, 2 * half) + 2]
        return out_

    def spread_coarse_plane(q, face):
        packed = q[slot(face, 4)]
        by_half = (jnp.where(even_lane2, packed, pltpu.roll(packed, 1, 1)),
                   jnp.where(even_lane2, pltpu.roll(packed, 127, 1), packed))
        return [jnp.concatenate([jnp.where(even_sub2, p, pltpu.roll(p, 1, 0))[None],
                                 jnp.where(even_sub2, pltpu.roll(p, 7, 0), p)[None]], axis=0) for p in by_half]

    def spread_coarse(q, half, x, planes):
        rows = jnp.concatenate([
            jnp.broadcast_to(q[slot(face, 2), CX * half + x : CX * half + x + 1, :], (8, 128))[None] for face in (2, 3)],
            axis=0)
        tile = iota((2, 8, 128), 0)
        out_ = jnp.where((sub // 2) == 3 * tile, rows, 0.0)
        column = q[slot(4 + half, 0)]
        columns = jnp.concatenate([
            jnp.broadcast_to(column[:, 16 + 2 * x + t : 17 + 2 * x + t], (8, 128))[None] for t in TILES], axis=0)
        out_ = out_ + jnp.where((lane // 2) == 63 * half, columns, 0.0)
        if x == 0:
            out_ = out_ + planes[0][half]
        if x == CX - 1:
            out_ = out_ + planes[1][half]
        return out_

    def peer(face):
        name, step = FACES[face]
        return {name: place[name] + step}

    def copy(turn, face):
        return pltpu.make_async_remote_copy(
            src_ref=message(sent, turn, face),
            dst_ref=message(received, turn, face ^ 1),
            send_sem=send_sem.at[turn, face],
            recv_sem=recv_sem.at[turn, face ^ 1],
            device_id=peer(face),
            device_id_type=MESH,
        )

    def arrival(turn, face):
        return pltpu.make_async_remote_copy(
            src_ref=message(sent, turn, face),
            dst_ref=message(received, turn, face),
            send_sem=send_sem.at[turn, face],
            recv_sem=recv_sem.at[turn, face],
            device_id=peer(face),
            device_id_type=MESH,
        )

    ORDER = (1, 0, 3, 2, 5, 4)

    def send(turn):
        for face in ORDER:
            @pl.when(present[face])
            def _():
                copy(turn, face).start()

    def wait(turn):
        for face in (5, 4, 3, 2, 1, 0):
            @pl.when(present[face])
            def _():
                arrival(turn, face).wait_recv()

    barrier = pltpu.get_barrier_semaphore()
    for face in range(6):
        @pl.when(present[face])
        def _():
            pl.semaphore_signal(barrier, inc=1, device_id=peer(face), device_id_type=MESH)

    loads = []
    for index, (hbm, ref) in enumerate(((cond_hbm, half_cond), (field_hbm, field), (source_hbm, source))):
        pair = []
        for h in HALVES:
            load = pltpu.make_async_copy(hbm.at[:, pl.ds(128 * h, 128)], ref.at[h], in_sem.at[index, h])
            load.start()
            pair.append(load)
        loads.append(pair)

    for face in range(6):
        @pl.when(jnp.logical_not(present[face]))
        def _():
            for turn in range(4):
                count = ROUND_SIZES[turn][face]
                received[turn, OFFSETS[face] : OFFSETS[face] + count] = jnp.zeros((count, 8, 128), F32)

    for load in loads[0]:
        load.wait()
    for x in range(NX):
        for h in HALVES:
            put(half_cond, h, x, 0.5 * plane(half_cond, h, x))
    for x in range(CX):
        for h in HALVES:
            put(coarse_half, h, x, restrict(plane(half_cond, h, 2 * x), plane(half_cond, h, 2 * x + 1)))
    store_columns(0, pack_coarse(coarse_half, 0, pack_fine(half_cond, 0, False)), 0)
    for load in loads[1]:
        load.wait()
    store_columns(0, pack_fine(field, 0, True), 1)

    pl.semaphore_wait(barrier, sum(p.astype(jnp.int32) for p in present))
    send(0)

    for x in range(NX):
        coefficients(half_cond, ky_lo, ky_hi, kz_lo, kz_hi, diag, x, NX, 1)
    for x in range(CX):
        coefficients(coarse_half, cky_lo, cky_hi, ckz_lo, ckz_hi, coarse_diag, x, CX, 2)
    for load in loads[2]:
        load.wait()

    def residual_part():
        for x in range(NX):
            total = fine_neighbours(field, x)
            for h in HALVES:
                put(partial, h, x, plane(source, h, x) - plane(diag, h, x) * plane(field, h, x) + total[h])

    residual_part()

    wait(0)
    for face in range(6):
        base, own, two = OFFSETS[face], SECOND[face], SECOND[face] - 1
        for i in range(own):
            gain = sent[0, base + i] + received[0, base + i]
            gains[base + i] = gain
        for i in range(SIZES[face] - own):
            faces[base + i] = (gains[base + i] * received[0, base + own + i]
                               - received[0, base + i] * sent[0, base + own + i])

    jplanes = (spread_coarse_plane(received.at[0], 0), spread_coarse_plane(received.at[0], 1))
    for x in range(CX):
        for h in HALVES:
            total = plane(coarse_diag, h, x) + spread_coarse(received.at[0], h, x, jplanes)
            put(coarse_inverse, h, x, 1.0 / total)
    for x in range(NX):
        for h in HALVES:
            total = plane(diag, h, x) + spread_fine(received.at[0], h, x)
            put(diag, h, x, total)
            put(inverse, h, x, 1.0 / total)

    for iteration in range(2):
        turn = 2 * iteration + 1
        if iteration > 0:
            wait(2)
            for face in range(6):
                base = OFFSETS[face]
                for i in range(ROUND_SIZES[2][face]):
                    faces[base + i] = gains[base + i] * received[2, base + i]
        for x in range(CX):
            for h in HALVES:
                pair = []
                for fx in (2 * x, 2 * x + 1):
                    r = plane(partial, h, fx) + spread_fine(faces, h, fx)
                    put(first, h, fx, FIRST_RATE * plane(inverse, h, fx) * r)
                    pair.append(r)
                put(coarse_first, h, x, 4.0 * FIRST_RATE * plane(coarse_inverse, h, x) * restrict(*pair))
        store_columns(turn, pack_coarse(coarse_first, turn, pack_fine(first, turn, False)), 0)
        send(turn)

        for x in range(CX):
            total = coarse_neighbours(coarse_first, x)
            coarse = [KEEP * plane(coarse_first, h, x) + FRESH * plane(coarse_inverse, h, x) * total[h] for h in HALVES]
            for fx in (2 * x, 2 * x + 1):
                total = fine_neighbours(first, fx)
                for h in HALVES:
                    fine = KEEP * plane(first, h, fx) + FRESH * plane(inverse, h, fx) * total[h]
                    put(partial, h, fx, plane(field, h, fx) + fine + coarse[h])

        wait(turn)
        for face in range(6):
            base = OFFSETS[face]
            for i in range(ROUND_SIZES[turn][face]):
                faces[base + i] = (FRESH * gains[base + i]) * received[turn, base + i]
        planes = (spread_coarse_plane(faces, 0), spread_coarse_plane(faces, 1))
        for x in range(CX):
            for h in HALVES:
                coarse = plane(coarse_inverse, h, x) * spread_coarse(faces, h, x, planes)
                for fx in (2 * x, 2 * x + 1):
                    fine = plane(inverse, h, fx) * spread_fine(faces, h, fx)
                    value = plane(partial, h, fx) + fine + coarse
                    if iteration == 0:
                        put(field, h, fx, value)
                    else:
                        out[NY * fx : NY * (fx + 1), 128 * h : 128 * (h + 1)] = value.reshape(16, 128)
        if iteration == 0:
            store_columns(2, pack_fine(field, 2, False), 0)
            send(2)
            residual_part()

    for turn in range(4):
        for face in range(6):
            @pl.when(present[face])
            def _():
                copy(turn, face).wait_send()


def block(source_term, conductivity, initial_field):
    def fine():
        return pltpu.VMEM((2, ROWS, 128), F32)

    def coarse():
        return pltpu.VMEM((2, CX * NY, 128), F32)

    hbm = pl.BlockSpec(memory_space=pltpu.HBM)
    result = pl.pallas_call(
        kernel,
        out_shape=pltpu.VMEM((ROWS, NZ), F32),
        in_specs=[hbm] * 3,
        out_specs=pl.BlockSpec(memory_space=pltpu.VMEM),
        scratch_shapes=[
            *(fine() for _ in range(11)),
            *(coarse() for _ in range(8)),
            pltpu.VMEM((SLOTS, 8, 128), F32),
            pltpu.VMEM((SLOTS, 8, 128), F32),
            pltpu.VMEM((4, SLOTS, 8, 128), F32),
            pltpu.VMEM((4, SLOTS, 8, 128), F32),
            pltpu.SemaphoreType.DMA((3, 2)),
            pltpu.SemaphoreType.DMA((4, 6)),
            pltpu.SemaphoreType.DMA((4, 6)),
        ],
        compiler_params=pltpu.CompilerParams(collective_id=0, has_side_effects=True),
    )(*(a.reshape(ROWS, NZ) for a in (source_term, conductivity, initial_field)))
    return result.reshape(NX, NY, NZ)


def solution(mesh):
    spec = P("gx", "gy", "grp")
    return jax.shard_map(block, mesh=mesh, in_specs=(spec,) * 3, out_specs=spec, check_vma=False)
```

```python
import functools

import jax
import jax.numpy as jnp
from jax import lax
from jax.experimental import pallas as pl
from jax.experimental.pallas import tpu as pltpu
from jax.sharding import PartitionSpec as P

MESH = pl.DeviceIdType.MESH
F32 = jnp.float32

NX, NY, NZ = 8, 16, 256
CX = NX // 2
ROWS = NX * NY
HALVES = (0, 1)
TILES = (0, 1)

FIRST_RATE = 0.8
KEEP = 60.0 / 41.0
FRESH = 40.0 / 41.0

FACES = (("gx", -1), ("gx", 1), ("gy", -1), ("gy", 1), ("grp", -1), ("grp", 1))
BOTH = (5, 5, 3, 3, 1, 1)
FINE = (4, 4, 2, 2, 1, 1)
TURN_SIZES = (BOTH, FINE, BOTH, FINE, BOTH)
TURNS = len(TURN_SIZES)
OFFSETS = (0, 5, 10, 13, 16, 17)
SLOTS = 18
AXES = ((0, 1), (2, 3), (4, 5))


def iota(shape, dim):
    return lax.broadcasted_iota(jnp.int32, shape, dim)


def kernel(source_hbm, cond_hbm, field_hbm, out, source, half_cond, field, first, ky_lo, ky_hi, kz_lo, kz_hi,
           diag, inverse, partial, coarse_half, cky_lo, cky_hi, ckz_lo, ckz_hi, coarse_diag, coarse_inverse, coarse_first,
           faces, gains, scaled_gains, sent, received, in_sem, send_sem, recv_sem):
    sub, lane = iota((2, 8, 128), 1), iota((2, 8, 128), 2)
    sub2, lane2 = iota((8, 128), 0), iota((8, 128), 1)
    even_sub, even_lane = sub % 2 == 0, lane % 2 == 0
    even_sub2, even_lane2 = sub2 % 2 == 0, lane2 % 2 == 0
    zero = jnp.zeros((1, 8, 128), F32)
    tile = iota((2, 8, 128), 0)

    place = {name: lax.axis_index(name) for name in ("grp", "gx", "gy")}
    size = {name: lax.axis_size(name) for name in ("grp", "gx", "gy")}
    present = []
    for name, step in FACES:
        present.append(place[name] > 0 if step < 0 else place[name] < size[name] - 1)

    def plane(ref, half, x):
        return ref[half, NY * x : NY * (x + 1), :].reshape(2, 8, 128)

    def put(ref, half, x, value):
        ref[half, NY * x : NY * (x + 1), :] = value.reshape(16, 128)

    def y_lower(p, width=1):
        rolled = pltpu.roll(p, width, 1)
        return jnp.where(sub < width, jnp.concatenate([zero, rolled[:1]], axis=0), rolled)

    def y_upper(p, width=1):
        rolled = pltpu.roll(p, 8 - width, 1)
        return jnp.where(sub >= 8 - width, jnp.concatenate([rolled[1:], zero], axis=0), rolled)

    def z_lower(p0, p1, width=1):
        r0, r1 = pltpu.roll(p0, width, 2), pltpu.roll(p1, width, 2)
        return jnp.where(lane < width, 0.0, r0), jnp.where(lane < width, r0, r1)

    def z_upper(p0, p1, width=1):
        r0, r1 = pltpu.roll(p0, 128 - width, 2), pltpu.roll(p1, 128 - width, 2)
        return jnp.where(lane >= 128 - width, r1, r0), jnp.where(lane >= 128 - width, 0.0, r1)

    def neighbour_sum(ref, half_ref, kyl, kyh, kzl, kzh, x, count, width):
        p = [plane(ref, h, x) for h in HALVES]
        zl, zh = z_lower(p[0], p[1], width), z_upper(p[0], p[1], width)
        here = [plane(half_ref, h, x) for h in HALVES]
        total = []
        for h in HALVES:
            s = plane(kyl, h, x) * y_lower(p[h], width) + plane(kyh, h, x) * y_upper(p[h], width)
            s = s + (plane(kzl, h, x) * zl[h] + plane(kzh, h, x) * zh[h])
            if x > 0:
                s = s + (here[h] + plane(half_ref, h, x - 1)) * plane(ref, h, x - 1)
            if x < count - 1:
                s = s + (here[h] + plane(half_ref, h, x + 1)) * plane(ref, h, x + 1)
            total.append(s)
        return total

    def fine_neighbours(ref, x):
        return neighbour_sum(ref, half_cond, ky_lo, ky_hi, kz_lo, kz_hi, x, NX, 1)

    def coarse_neighbours(ref, x):
        return neighbour_sum(ref, coarse_half, cky_lo, cky_hi, ckz_lo, ckz_hi, x, CX, 2)

    def coefficients(ref, kyl, kyh, kzl, kzh, diag_ref, x, count, width):
        p = [plane(ref, h, x) for h in HALVES]
        zl, zh = z_lower(p[0], p[1], width), z_upper(p[0], p[1], width)
        for h in HALVES:
            yl, yh = y_lower(p[h], width), y_upper(p[h], width)
            put(kyl, h, x, p[h] + yl)
            put(kyh, h, x, p[h] + yh)
            put(kzl, h, x, p[h] + zl[h])
            put(kzh, h, x, p[h] + zh[h])
            s = 6.0 * p[h] + ((yl + yh) + (zl[h] + zh[h]))
            if x > 0:
                s = s + plane(ref, h, x - 1)
            if x < count - 1:
                s = s + plane(ref, h, x + 1)
            put(diag_ref, h, x, s)

    def restrict(lower, upper):
        s = lower + upper
        s = s + jnp.where(even_sub, pltpu.roll(s, 7, 1), pltpu.roll(s, 1, 1))
        s = s + jnp.where(even_lane, pltpu.roll(s, 127, 2), pltpu.roll(s, 1, 2))
        return 0.125 * s

    def slot(face, index):
        return OFFSETS[face] + index

    def message(store, turn, face):
        return store.at[turn, pl.ds(OFFSETS[face], TURN_SIZES[turn][face])]

    def pack_x(dest, fine, coarse=None):
        for face, x in ((0, 0), (1, NX - 1)):
            for h in HALVES:
                dest[slot(face, 2 * h) : slot(face, 2 * h) + 2] = plane(fine, h, x)
        if coarse is not None:
            for face, x in ((0, 0), (1, CX - 1)):
                p = [plane(coarse, h, x) for h in HALVES]
                dest[slot(face, 4)] = jnp.where(
                    even_sub2, jnp.where(even_lane2, p[0][0], p[1][0]), jnp.where(even_lane2, p[0][1], p[1][1]))

    def pack_y(dest, fine, coarse=None):
        for face, row in ((2, 0), (3, NY - 1)):
            for h in HALVES:
                dest[slot(face, h)] = fine[h, pl.ds(row, NX, stride=NY), :]
                if coarse is not None:
                    dest[slot(face, 2), CX * h : CX * (h + 1), :] = coarse[h, pl.ds(row, CX, stride=NY), :]

    def pack_z(dest, fine, coarse=None):
        for face, h, source_lane in ((4, 0, 0), (5, 1, 127)):
            packed = jnp.zeros((8, 128), F32)
            for ref, count, start in ((fine, NX, 0), (coarse, CX, 16)):
                if ref is None:
                    continue
                for x in range(count):
                    p = plane(ref, h, x)
                    for t in TILES:
                        m = start + 2 * x + t
                        packed = jnp.where(lane2 == m, pltpu.roll(p[t], (m - source_lane) % 128, 1), packed)
            dest[slot(face, 0)] = packed

    def two(a, b):
        return jnp.concatenate([a[None], b[None]], axis=0)

    def fine_z(q, half, x):
        column = q[slot(4 + half, 0)]
        return jnp.where(lane == 127 * half, two(*(
            jnp.broadcast_to(column[:, 2 * x + t : 2 * x + t + 1], (8, 128)) for t in TILES)), 0.0)

    def coarse_z(q, half, x):
        column = q[slot(4 + half, 0)]
        return jnp.where(lane // 2 == 63 * half, two(*(
            jnp.broadcast_to(column[:, 16 + 2 * x + t : 17 + 2 * x + t], (8, 128)) for t in TILES)), 0.0)

    def fine_xy(q, half, x):
        added = jnp.where(sub == 7 * tile, two(*(
            jnp.broadcast_to(q[slot(face, half), x : x + 1, :], (8, 128)) for face in (2, 3))), 0.0)
        if x == 0:
            added = added + q[slot(0, 2 * half) : slot(0, 2 * half) + 2]
        if x == NX - 1:
            added = added + q[slot(1, 2 * half) : slot(1, 2 * half) + 2]
        return added

    def coarse_plane(q, half, face):
        packed = q[slot(face, 4)]
        if half == 0:
            p = jnp.where(even_lane2, packed, pltpu.roll(packed, 1, 1))
        else:
            p = jnp.where(even_lane2, pltpu.roll(packed, 127, 1), packed)
        return two(jnp.where(even_sub2, p, pltpu.roll(p, 1, 0)), jnp.where(even_sub2, pltpu.roll(p, 7, 0), p))

    def coarse_xy(q, half, x):
        row = CX * half + x
        added = jnp.where(sub // 2 == 3 * tile, two(*(
            jnp.broadcast_to(q[slot(face, 2), row : row + 1, :], (8, 128)) for face in (2, 3))), 0.0)
        if x == 0:
            added = added + coarse_plane(q, half, 0)
        if x == CX - 1:
            added = added + coarse_plane(q, half, 1)
        return added

    def peer(face):
        name, step = FACES[face]
        return {name: place[name] + step}

    def copy(turn, face):
        return pltpu.make_async_remote_copy(
            src_ref=message(sent, turn, face),
            dst_ref=message(received, turn, face ^ 1),
            send_sem=send_sem.at[turn, face],
            recv_sem=recv_sem.at[turn, face ^ 1],
            device_id=peer(face),
            device_id_type=MESH,
        )

    def arrival(turn, face):
        return pltpu.make_async_remote_copy(
            src_ref=message(sent, turn, face),
            dst_ref=message(received, turn, face),
            send_sem=send_sem.at[turn, face],
            recv_sem=recv_sem.at[turn, face],
            device_id=peer(face),
            device_id_type=MESH,
        )

    def send(turn, axis):
        for face in reversed(AXES[axis]):
            @pl.when(present[face])
            def _():
                copy(turn, face).start()

    def wait(turn, axes):
        for axis in axes:
            for face in AXES[axis]:
                @pl.when(present[face])
                def _():
                    arrival(turn, face).wait_recv()

    def wait_sent(turn):
        for face in range(6):
            @pl.when(present[face])
            def _():
                copy(turn, face).wait_send()

    barrier = pltpu.get_barrier_semaphore()
    for face in range(6):
        @pl.when(present[face])
        def _():
            pl.semaphore_signal(barrier, inc=1, device_id=peer(face), device_id_type=MESH)

    loads = []
    for index, (hbm, ref) in enumerate(((cond_hbm, half_cond), (field_hbm, field), (source_hbm, source))):
        pair = []
        for h in HALVES:
            load = pltpu.make_async_copy(hbm.at[:, pl.ds(128 * h, 128)], ref.at[h], in_sem.at[index, h])
            load.start()
            pair.append(load)
        loads.append(pair)

    for face in range(6):
        @pl.when(jnp.logical_not(present[face]))
        def _():
            for turn in range(TURNS):
                count = TURN_SIZES[turn][face]
                received[turn, OFFSETS[face] : OFFSETS[face] + count] = jnp.zeros((count, 8, 128), F32)

    for load in loads[0]:
        load.wait()
    for x in range(NX):
        for h in HALVES:
            put(half_cond, h, x, 0.5 * plane(half_cond, h, x))
    for x in range(CX):
        for h in HALVES:
            put(coarse_half, h, x, restrict(plane(half_cond, h, 2 * x), plane(half_cond, h, 2 * x + 1)))
    for pack in (pack_x, pack_y, pack_z):
        pack(sent.at[0], half_cond, coarse_half)
    pl.semaphore_wait(barrier, sum(p.astype(jnp.int32) for p in present))
    for axis in range(3):
        send(0, axis)
    for load in loads[1]:
        load.wait()
    for axis, pack in enumerate((pack_x, pack_y, pack_z)):
        pack(sent.at[1], field)
        send(1, axis)

    for x in range(NX):
        coefficients(half_cond, ky_lo, ky_hi, kz_lo, kz_hi, diag, x, NX, 1)
    for x in range(CX):
        coefficients(coarse_half, cky_lo, cky_hi, ckz_lo, ckz_hi, coarse_diag, x, CX, 2)
    for load in loads[2]:
        load.wait()

    def residual_part():
        for x in range(NX):
            total = fine_neighbours(field, x)
            for h in HALVES:
                put(partial, h, x, plane(source, h, x) - plane(diag, h, x) * plane(field, h, x) + total[h])

    residual_part()

    wait(0, (2, 0, 1))
    for i in range(SLOTS):
        gains[i] = sent[0, i] + received[0, i]
    outside = received.at[0]
    for x in range(NX):
        for h in HALVES:
            total = plane(diag, h, x) + fine_z(outside, h, x) + fine_xy(outside, h, x)
            put(diag, h, x, total)
            put(inverse, h, x, 1.0 / total)
    for x in range(CX):
        for h in HALVES:
            put(coarse_inverse, h, x, 1.0 / (plane(coarse_diag, h, x) + coarse_z(outside, h, x) + coarse_xy(outside, h, x)))

    def residual_terms(turn, axis):
        for face in AXES[axis]:
            for i in range(OFFSETS[face], OFFSETS[face] + FINE[face]):
                term = gains[i] * received[turn, i]
                if turn == 1:
                    term = term - received[0, i] * sent[1, i]
                faces[i] = term

    def field_terms(turn, axis):
        for face in AXES[axis]:
            for i in range(OFFSETS[face], OFFSETS[face] + BOTH[face]):
                faces[i] = scaled_gains[i] * received[turn, i]

    for iteration in range(2):
        last = iteration == 1
        turn = 2 * iteration + 1
        wait(turn, (2,))
        residual_terms(turn, 2)
        for x in range(NX):
            for h in HALVES:
                put(partial, h, x, plane(partial, h, x) + fine_z(faces, h, x))
        wait(turn, (0, 1))
        residual_terms(turn, 0)
        residual_terms(turn, 1)

        def smooth(x):
            for h in HALVES:
                pair = []
                for fx in (2 * x, 2 * x + 1):
                    r = plane(partial, h, fx) + fine_xy(faces, h, fx)
                    put(first, h, fx, FIRST_RATE * plane(inverse, h, fx) * r)
                    pair.append(r)
                put(coarse_first, h, x, 4.0 * FIRST_RATE * plane(coarse_inverse, h, x) * restrict(*pair))

        turn += 1
        smooth(0)
        smooth(CX - 1)
        pack_x(sent.at[turn], first, coarse_first)
        send(turn, 0)
        for x in range(1, CX - 1):
            smooth(x)
        pack_y(sent.at[turn], first, coarse_first)
        send(turn, 1)
        pack_z(sent.at[turn], first, coarse_first)
        send(turn, 2)

        if not last:
            for pack in (pack_x, pack_y, pack_z):
                pack(scaled_gains, inverse, coarse_inverse)
            for i in range(SLOTS):
                scaled_gains[i] = FRESH * scaled_gains[i] * gains[i]
        for x in range(CX):
            total = coarse_neighbours(coarse_first, x)
            coarse = [KEEP * plane(coarse_first, h, x) + FRESH * plane(coarse_inverse, h, x) * total[h] for h in HALVES]
            for fx in (2 * x, 2 * x + 1):
                total = fine_neighbours(first, fx)
                for h in HALVES:
                    fine = KEEP * plane(first, h, fx) + FRESH * plane(inverse, h, fx) * total[h]
                    put(partial, h, fx, plane(field, h, fx) + fine + coarse[h])
        wait_sent(turn - 1)
        if not last:
            wait_sent(0)

        wait(turn, (2,))
        field_terms(turn, 2)
        for x in range(CX):
            for h in HALVES:
                coarse = coarse_z(faces, h, x)
                for fx in (2 * x, 2 * x + 1):
                    put(partial, h, fx, plane(partial, h, fx) + coarse + fine_z(faces, h, fx))
        wait(turn, (0, 1))
        field_terms(turn, 0)
        field_terms(turn, 1)

        def update(x):
            for h in HALVES:
                coarse = coarse_xy(faces, h, x)
                for fx in (2 * x, 2 * x + 1):
                    value = plane(partial, h, fx) + coarse + fine_xy(faces, h, fx)
                    if last:
                        out[NY * fx : NY * (fx + 1), 128 * h : 128 * (h + 1)] = value.reshape(16, 128)
                    else:
                        put(field, h, fx, value)

        update(0)
        update(CX - 1)
        if not last:
            pack_x(sent.at[turn + 1], field)
            send(turn + 1, 0)
        for x in range(1, CX - 1):
            update(x)
        if not last:
            pack_y(sent.at[turn + 1], field)
            send(turn + 1, 1)
            pack_z(sent.at[turn + 1], field)
            send(turn + 1, 2)
            residual_part()
            wait_sent(turn)
    wait_sent(TURNS - 1)


def block(source_term, conductivity, initial_field):
    def fine():
        return pltpu.VMEM((2, ROWS, 128), F32)

    def coarse():
        return pltpu.VMEM((2, CX * NY, 128), F32)

    hbm = pl.BlockSpec(memory_space=pltpu.HBM)
    result = pl.pallas_call(
        kernel,
        out_shape=pltpu.VMEM((ROWS, NZ), F32),
        in_specs=[hbm] * 3,
        out_specs=pl.BlockSpec(memory_space=pltpu.VMEM),
        scratch_shapes=[
            *(fine() for _ in range(11)),
            *(coarse() for _ in range(8)),
            *(pltpu.VMEM((SLOTS, 8, 128), F32) for _ in range(3)),
            *(pltpu.VMEM((TURNS, SLOTS, 8, 128), F32) for _ in range(2)),
            pltpu.SemaphoreType.DMA((3, 2)),
            *(pltpu.SemaphoreType.DMA((TURNS, 6)) for _ in range(2)),
        ],
        compiler_params=pltpu.CompilerParams(collective_id=0, has_side_effects=True),
    )(*(a.reshape(ROWS, NZ) for a in (source_term, conductivity, initial_field)))
    return result.reshape(NX, NY, NZ)


def solution(mesh):
    spec = P("gx", "gy", "grp")
    return jax.shard_map(block, mesh=mesh, in_specs=(spec,) * 3, out_specs=spec, check_vma=False)
```

```python
import functools

import jax
import jax.numpy as jnp
from jax import lax
from jax.experimental import pallas as pl
from jax.experimental.pallas import tpu as pltpu
from jax.sharding import PartitionSpec as P

MESH = pl.DeviceIdType.MESH
F32 = jnp.float32

NX, NY, NZ = 8, 16, 256
CX = NX // 2
ROWS = NX * NY
HALVES = (0, 1)
TILES = (0, 1)

FIRST_RATE = 0.8
KEEP = 60.0 / 41.0
FRESH = 40.0 / 41.0

FACES = (("gx", -1), ("gx", 1), ("gy", -1), ("gy", 1), ("grp", -1), ("grp", 1))
BOTH = (5, 5, 3, 3, 1, 1)
FINE = (4, 4, 2, 2, 1, 1)
TURN_SIZES = (BOTH, FINE, BOTH, FINE, BOTH)
TURNS = len(TURN_SIZES)
OFFSETS = (0, 5, 10, 13, 16, 17)
SLOTS = 18
AXES = ((0, 1), (2, 3), (4, 5))


def iota(shape, dim):
    return lax.broadcasted_iota(jnp.int32, shape, dim)


def kernel(source_hbm, cond_hbm, field_hbm, out, source, half_cond, field, first, ky_lo, ky_hi, kz_lo, kz_hi,
           diag, inverse, partial, coarse_half, cky_lo, cky_hi, ckz_lo, ckz_hi, coarse_diag, coarse_inverse, coarse_first,
           faces, gains, scaled_gains, sent, received, in_sem, send_sem, recv_sem):
    sub, lane = iota((2, 8, 128), 1), iota((2, 8, 128), 2)
    sub2, lane2 = iota((8, 128), 0), iota((8, 128), 1)
    even_sub2, even_lane2 = sub2 % 2 == 0, lane2 % 2 == 0
    zero = jnp.zeros((1, 8, 128), F32)

    place = {name: lax.axis_index(name) for name in ("grp", "gx", "gy")}
    size = {name: lax.axis_size(name) for name in ("grp", "gx", "gy")}
    present = []
    for name, step in FACES:
        present.append(place[name] > 0 if step < 0 else place[name] < size[name] - 1)

    def plane(ref, half, x):
        return ref[half, NY * x : NY * (x + 1), :].reshape(2, 8, 128)

    def put(ref, half, x, value):
        ref[half, NY * x : NY * (x + 1), :] = value.reshape(16, 128)

    def part(ref, half, x, t):
        return ref[half, NY * x + 8 * t : NY * x + 8 * t + 8, :]

    def put_part(ref, half, x, t, value):
        ref[half, NY * x + 8 * t : NY * x + 8 * t + 8, :] = value

    def y_lower(p, width=1):
        rolled = pltpu.roll(p, width, 1)
        return jnp.where(sub < width, jnp.concatenate([zero, rolled[:1]], axis=0), rolled)

    def y_upper(p, width=1):
        rolled = pltpu.roll(p, 8 - width, 1)
        return jnp.where(sub >= 8 - width, jnp.concatenate([rolled[1:], zero], axis=0), rolled)

    def z_lower(p0, p1, width=1):
        r0, r1 = pltpu.roll(p0, width, 2), pltpu.roll(p1, width, 2)
        return jnp.where(lane < width, 0.0, r0), jnp.where(lane < width, r0, r1)

    def z_upper(p0, p1, width=1):
        r0, r1 = pltpu.roll(p0, 128 - width, 2), pltpu.roll(p1, 128 - width, 2)
        return jnp.where(lane >= 128 - width, r1, r0), jnp.where(lane >= 128 - width, 0.0, r1)

    def neighbour_sum(ref, half_ref, kyl, kyh, kzl, kzh, x, count, width):
        p = [plane(ref, h, x) for h in HALVES]
        zl, zh = z_lower(p[0], p[1], width), z_upper(p[0], p[1], width)
        here = [plane(half_ref, h, x) for h in HALVES]
        total = []
        for h in HALVES:
            s = plane(kyl, h, x) * y_lower(p[h], width) + plane(kyh, h, x) * y_upper(p[h], width)
            s = s + (plane(kzl, h, x) * zl[h] + plane(kzh, h, x) * zh[h])
            if x > 0:
                s = s + (here[h] + plane(half_ref, h, x - 1)) * plane(ref, h, x - 1)
            if x < count - 1:
                s = s + (here[h] + plane(half_ref, h, x + 1)) * plane(ref, h, x + 1)
            total.append(s)
        return total

    def fine_neighbours(ref, x):
        return neighbour_sum(ref, half_cond, ky_lo, ky_hi, kz_lo, kz_hi, x, NX, 1)

    def coarse_neighbours(ref, x):
        return neighbour_sum(ref, coarse_half, cky_lo, cky_hi, ckz_lo, ckz_hi, x, CX, 2)

    def coefficients(ref, kyl, kyh, kzl, kzh, diag_ref, x, count, width):
        p = [plane(ref, h, x) for h in HALVES]
        zl, zh = z_lower(p[0], p[1], width), z_upper(p[0], p[1], width)
        for h in HALVES:
            yl, yh = y_lower(p[h], width), y_upper(p[h], width)
            put(kyl, h, x, p[h] + yl)
            put(kyh, h, x, p[h] + yh)
            put(kzl, h, x, p[h] + zl[h])
            put(kzh, h, x, p[h] + zh[h])
            s = 6.0 * p[h] + ((yl + yh) + (zl[h] + zh[h]))
            if x > 0:
                s = s + plane(ref, h, x - 1)
            if x < count - 1:
                s = s + plane(ref, h, x + 1)
            put(diag_ref, h, x, s)

    def restrict(lower, upper):
        s = lower + upper
        s = s + jnp.where(even_sub2, pltpu.roll(s, 7, 0), pltpu.roll(s, 1, 0))
        s = s + jnp.where(even_lane2, pltpu.roll(s, 127, 1), pltpu.roll(s, 1, 1))
        return 0.125 * s

    def slot(face, index):
        return OFFSETS[face] + index

    def message(store, turn, face):
        return store.at[turn, pl.ds(OFFSETS[face], TURN_SIZES[turn][face])]

    def pack_x(dest, fine, coarse=None):
        for face, x in ((0, 0), (1, NX - 1)):
            for h in HALVES:
                dest[slot(face, 2 * h) : slot(face, 2 * h) + 2] = plane(fine, h, x)
        if coarse is not None:
            for face, x in ((0, 0), (1, CX - 1)):
                p = [plane(coarse, h, x) for h in HALVES]
                dest[slot(face, 4)] = jnp.where(
                    even_sub2, jnp.where(even_lane2, p[0][0], p[1][0]), jnp.where(even_lane2, p[0][1], p[1][1]))

    def pack_face_y(dest, face, fine, coarse=None):
        row = (NY - 1) * (face - 2)
        for h in HALVES:
            dest[slot(face, h)] = fine[h, pl.ds(row, NX, stride=NY), :]
            if coarse is not None:
                dest[slot(face, 2), CX * h : CX * (h + 1), :] = coarse[h, pl.ds(row, CX, stride=NY), :]

    def pack_y(dest, fine, coarse=None):
        for face in AXES[1]:
            pack_face_y(dest, face, fine, coarse)

    def pack_z(dest, fine, coarse=None):
        for face, h, source_lane in ((4, 0, 0), (5, 1, 127)):
            packed = jnp.zeros((8, 128), F32)
            for ref, count, start in ((fine, NX, 0), (coarse, CX, 16)):
                if ref is None:
                    continue
                for x in range(count):
                    p = plane(ref, h, x)
                    for t in TILES:
                        m = start + 2 * x + t
                        packed = jnp.where(lane2 == m, pltpu.roll(p[t], (m - source_lane) % 128, 1), packed)
            dest[slot(face, 0)] = packed

    def fine_z(q, half, x, t):
        lanes = 2 * x + t
        column = q[slot(4 + half, 0)][:, lanes : lanes + 1]
        return jnp.where(lane2 == 127 * half, jnp.broadcast_to(column, (8, 128)), 0.0)

    def coarse_z(q, half, x, t):
        lanes = 16 + 2 * x + t
        column = q[slot(4 + half, 0)][:, lanes : lanes + 1]
        return jnp.where(lane2 // 2 == 63 * half, jnp.broadcast_to(column, (8, 128)), 0.0)

    def fine_y(q, half, x, t):
        return jnp.where(sub2 == 7 * t, jnp.broadcast_to(q[slot(2 + t, half), x : x + 1, :], (8, 128)), 0.0)

    def coarse_y(q, half, x, t):
        row = CX * half + x
        return jnp.where(sub2 // 2 == 3 * t, jnp.broadcast_to(q[slot(2 + t, 2), row : row + 1, :], (8, 128)), 0.0)

    def fine_xz(q, half, x, t):
        added = fine_z(q, half, x, t)
        if x == 0:
            added = added + q[slot(0, 2 * half + t)]
        if x == NX - 1:
            added = added + q[slot(1, 2 * half + t)]
        return added

    def coarse_plane(q, half, face, t):
        packed = q[slot(face, 4)]
        if half == 0:
            p = jnp.where(even_lane2, packed, pltpu.roll(packed, 1, 1))
        else:
            p = jnp.where(even_lane2, pltpu.roll(packed, 127, 1), packed)
        return jnp.where(even_sub2, p, pltpu.roll(p, 1, 0)) if t == 0 else jnp.where(even_sub2, pltpu.roll(p, 7, 0), p)

    def coarse_xz(q, half, x, t):
        added = coarse_z(q, half, x, t)
        if x == 0:
            added = added + coarse_plane(q, half, 0, t)
        if x == CX - 1:
            added = added + coarse_plane(q, half, 1, t)
        return added

    def peer(face):
        name, step = FACES[face]
        return {name: place[name] + step}

    def copy(turn, face):
        return pltpu.make_async_remote_copy(
            src_ref=message(sent, turn, face),
            dst_ref=message(received, turn, face ^ 1),
            send_sem=send_sem.at[turn, face],
            recv_sem=recv_sem.at[turn, face ^ 1],
            device_id=peer(face),
            device_id_type=MESH,
        )

    def arrival(turn, face):
        return pltpu.make_async_remote_copy(
            src_ref=message(sent, turn, face),
            dst_ref=message(received, turn, face),
            send_sem=send_sem.at[turn, face],
            recv_sem=recv_sem.at[turn, face],
            device_id=peer(face),
            device_id_type=MESH,
        )

    def send(turn, faces_):
        for face in faces_:
            @pl.when(present[face])
            def _():
                copy(turn, face).start()

    def wait(turn, faces_):
        for face in faces_:
            @pl.when(present[face])
            def _():
                arrival(turn, face).wait_recv()

    def wait_sent(turn):
        for face in range(6):
            @pl.when(present[face])
            def _():
                copy(turn, face).wait_send()

    barrier = pltpu.get_barrier_semaphore()
    for face in range(6):
        @pl.when(present[face])
        def _():
            pl.semaphore_signal(barrier, inc=1, device_id=peer(face), device_id_type=MESH)

    loads = []
    for index, (hbm, ref) in enumerate(((cond_hbm, half_cond), (field_hbm, field), (source_hbm, source))):
        pair = []
        for h in HALVES:
            load = pltpu.make_async_copy(hbm.at[:, pl.ds(128 * h, 128)], ref.at[h], in_sem.at[index, h])
            load.start()
            pair.append(load)
        loads.append(pair)

    for face in range(6):
        @pl.when(jnp.logical_not(present[face]))
        def _():
            for turn in range(TURNS):
                count = TURN_SIZES[turn][face]
                received[turn, OFFSETS[face] : OFFSETS[face] + count] = jnp.zeros((count, 8, 128), F32)

    for load in loads[0]:
        load.wait()
    for x in range(NX):
        for h in HALVES:
            put(half_cond, h, x, 0.5 * plane(half_cond, h, x))
    for x in range(CX):
        for h in HALVES:
            for t in TILES:
                put_part(coarse_half, h, x, t, restrict(part(half_cond, h, 2 * x, t), part(half_cond, h, 2 * x + 1, t)))
    for pack in (pack_x, pack_y, pack_z):
        pack(sent.at[0], half_cond, coarse_half)
    pl.semaphore_wait(barrier, sum(p.astype(jnp.int32) for p in present))
    send(0, (3, 2, 1, 0, 5, 4))
    for load in loads[1]:
        load.wait()
    for axis, pack in ((1, pack_y), (0, pack_x), (2, pack_z)):
        pack(sent.at[1], field)
        send(1, AXES[axis])

    for x in range(NX):
        coefficients(half_cond, ky_lo, ky_hi, kz_lo, kz_hi, diag, x, NX, 1)
    for x in range(CX):
        coefficients(coarse_half, cky_lo, cky_hi, ckz_lo, ckz_hi, coarse_diag, x, CX, 2)
    for load in loads[2]:
        load.wait()

    def residual_part():
        for x in range(NX):
            total = fine_neighbours(field, x)
            for h in HALVES:
                put(partial, h, x, plane(source, h, x) - plane(diag, h, x) * plane(field, h, x) + total[h])

    residual_part()

    wait(0, (4, 5, 0, 1, 2, 3))
    for i in range(SLOTS):
        gains[i] = sent[0, i] + received[0, i]
    outside = received.at[0]
    for x in range(NX):
        for h in HALVES:
            for t in TILES:
                total = part(diag, h, x, t) + fine_xz(outside, h, x, t) + fine_y(outside, h, x, t)
                put_part(diag, h, x, t, total)
                put_part(inverse, h, x, t, 1.0 / total)
    for x in range(CX):
        for h in HALVES:
            for t in TILES:
                total = part(coarse_diag, h, x, t) + coarse_xz(outside, h, x, t) + coarse_y(outside, h, x, t)
                put_part(coarse_inverse, h, x, t, 1.0 / total)

    def residual_terms(turn, faces_):
        for face in faces_:
            for i in range(OFFSETS[face], OFFSETS[face] + FINE[face]):
                term = gains[i] * received[turn, i]
                if turn == 1:
                    term = term - received[0, i] * sent[1, i]
                faces[i] = term

    def field_terms(turn, faces_):
        for face in faces_:
            for i in range(OFFSETS[face], OFFSETS[face] + BOTH[face]):
                faces[i] = scaled_gains[i] * received[turn, i]

    for iteration in range(2):
        last = iteration == 1
        turn = 2 * iteration + 1
        near = (4, 5, 0, 1)
        wait(turn, near)
        residual_terms(turn, near)
        for x in range(NX):
            for h in HALVES:
                for t in TILES:
                    put_part(partial, h, x, t, part(partial, h, x, t) + fine_xz(faces, h, x, t))

        def smooth(x, t):
            for h in HALVES:
                pair = []
                for fx in (2 * x, 2 * x + 1):
                    r = part(partial, h, fx, t) + fine_y(faces, h, fx, t)
                    put_part(first, h, fx, t, FIRST_RATE * part(inverse, h, fx, t) * r)
                    pair.append(r)
                put_part(coarse_first, h, x, t, 4.0 * FIRST_RATE * part(coarse_inverse, h, x, t) * restrict(*pair))

        for t in TILES:
            wait(turn, (2 + t,))
            residual_terms(turn, (2 + t,))
            for x in range(CX):
                smooth(x, t)
            pack_face_y(sent.at[turn + 1], 2 + t, first, coarse_first)
            send(turn + 1, (2 + t,))
        turn += 1
        pack_x(sent.at[turn], first, coarse_first)
        send(turn, AXES[0])
        pack_z(sent.at[turn], first, coarse_first)
        send(turn, AXES[2])

        if not last:
            for pack in (pack_x, pack_y, pack_z):
                pack(scaled_gains, inverse, coarse_inverse)
            for i in range(SLOTS):
                scaled_gains[i] = FRESH * scaled_gains[i] * gains[i]
        for x in range(CX):
            total = coarse_neighbours(coarse_first, x)
            coarse = [KEEP * plane(coarse_first, h, x) + FRESH * plane(coarse_inverse, h, x) * total[h] for h in HALVES]
            for fx in (2 * x, 2 * x + 1):
                total = fine_neighbours(first, fx)
                for h in HALVES:
                    fine = KEEP * plane(first, h, fx) + FRESH * plane(inverse, h, fx) * total[h]
                    put(partial, h, fx, plane(field, h, fx) + fine + coarse[h])
        wait_sent(turn - 1)
        if not last:
            wait_sent(0)

        wait(turn, near)
        field_terms(turn, near)
        for x in range(CX):
            for h in HALVES:
                for t in TILES:
                    coarse = coarse_xz(faces, h, x, t)
                    for fx in (2 * x, 2 * x + 1):
                        put_part(partial, h, fx, t, part(partial, h, fx, t) + coarse + fine_xz(faces, h, fx, t))

        for t in TILES:
            wait(turn, (2 + t,))
            field_terms(turn, (2 + t,))
            for x in range(CX):
                for h in HALVES:
                    coarse = coarse_y(faces, h, x, t)
                    for fx in (2 * x, 2 * x + 1):
                        value = part(partial, h, fx, t) + coarse + fine_y(faces, h, fx, t)
                        if last:
                            row = NY * fx + 8 * t
                            out[row : row + 8, 128 * h : 128 * (h + 1)] = value
                        else:
                            put_part(field, h, fx, t, value)
            if not last:
                pack_face_y(sent.at[turn + 1], 2 + t, field)
                send(turn + 1, (2 + t,))
        if not last:
            pack_x(sent.at[turn + 1], field)
            send(turn + 1, AXES[0])
            pack_z(sent.at[turn + 1], field)
            send(turn + 1, AXES[2])
            residual_part()
            wait_sent(turn)
    wait_sent(TURNS - 1)


def block(source_term, conductivity, initial_field):
    def fine():
        return pltpu.VMEM((2, ROWS, 128), F32)

    def coarse():
        return pltpu.VMEM((2, CX * NY, 128), F32)

    hbm = pl.BlockSpec(memory_space=pltpu.HBM)
    result = pl.pallas_call(
        kernel,
        out_shape=pltpu.VMEM((ROWS, NZ), F32),
        in_specs=[hbm] * 3,
        out_specs=pl.BlockSpec(memory_space=pltpu.VMEM),
        scratch_shapes=[
            *(fine() for _ in range(11)),
            *(coarse() for _ in range(8)),
            *(pltpu.VMEM((SLOTS, 8, 128), F32) for _ in range(3)),
            *(pltpu.VMEM((TURNS, SLOTS, 8, 128), F32) for _ in range(2)),
            pltpu.SemaphoreType.DMA((3, 2)),
            *(pltpu.SemaphoreType.DMA((TURNS, 6)) for _ in range(2)),
        ],
        compiler_params=pltpu.CompilerParams(collective_id=0, has_side_effects=True),
    )(*(a.reshape(ROWS, NZ) for a in (source_term, conductivity, initial_field)))
    return result.reshape(NX, NY, NZ)


def solution(mesh):
    spec = P("gx", "gy", "grp")
    return jax.shard_map(block, mesh=mesh, in_specs=(spec,) * 3, out_specs=spec, check_vma=False)
```

```python
import functools

import jax
import jax.numpy as jnp
from jax import lax
from jax.experimental import pallas as pl
from jax.experimental.pallas import tpu as pltpu
from jax.sharding import PartitionSpec as P

MESH = pl.DeviceIdType.MESH
F32 = jnp.float32

NX, NY, NZ = 8, 16, 256
CX = NX // 2
ROWS = NX * NY
HALVES = (0, 1)
TILES = (0, 1)

FIRST_RATE = 0.8
KEEP = 60.0 / 41.0
FRESH = 40.0 / 41.0

FACES = (("gx", -1), ("gx", 1), ("gy", -1), ("gy", 1), ("grp", -1), ("grp", 1))
BOTH = (5, 5, 3, 3, 1, 1)
FINE = (4, 4, 2, 2, 1, 1)
TURN_SIZES = (BOTH, FINE, BOTH, FINE, BOTH, BOTH)
TURNS = len(TURN_SIZES)
OFFSETS = (0, 5, 10, 13, 16, 17)
SLOTS = 18
AXES = ((0, 1), (2, 3), (4, 5))
EDGES = [(a, b) for p, q in ((0, 1), (0, 2), (1, 2)) for a in AXES[p] for b in AXES[q]]


def iota(shape, dim):
    return lax.broadcasted_iota(jnp.int32, shape, dim)


def kernel(source_hbm, cond_hbm, field_hbm, out, source, half_cond, field, first, ky_lo, ky_hi, kz_lo, kz_hi,
           diag, inverse, partial, coarse_half, cky_lo, cky_hi, ckz_lo, ckz_hi, coarse_diag, coarse_inverse, coarse_first,
           faces, gains, scaled_gains, beside, edge_sent, edge_received, sent,
           received, in_sem, send_sem, recv_sem, edge_send_sem, edge_recv_sem):
    sub, lane = iota((2, 8, 128), 1), iota((2, 8, 128), 2)
    sub2, lane2 = iota((8, 128), 0), iota((8, 128), 1)
    even_sub2, even_lane2 = sub2 % 2 == 0, lane2 % 2 == 0
    zero = jnp.zeros((1, 8, 128), F32)

    place = {name: lax.axis_index(name) for name in ("grp", "gx", "gy")}
    size = {name: lax.axis_size(name) for name in ("grp", "gx", "gy")}
    present = []
    for name, step in FACES:
        present.append(place[name] > 0 if step < 0 else place[name] < size[name] - 1)

    def plane(ref, half, x):
        return ref[half, NY * x : NY * (x + 1), :].reshape(2, 8, 128)

    def put(ref, half, x, value):
        ref[half, NY * x : NY * (x + 1), :] = value.reshape(16, 128)

    def part(ref, half, x, t):
        return ref[half, NY * x + 8 * t : NY * x + 8 * t + 8, :]

    def put_part(ref, half, x, t, value):
        ref[half, NY * x + 8 * t : NY * x + 8 * t + 8, :] = value

    def y_lower(p, width=1):
        rolled = pltpu.roll(p, width, 1)
        return jnp.where(sub < width, jnp.concatenate([zero, rolled[:1]], axis=0), rolled)

    def y_upper(p, width=1):
        rolled = pltpu.roll(p, 8 - width, 1)
        return jnp.where(sub >= 8 - width, jnp.concatenate([rolled[1:], zero], axis=0), rolled)

    def z_lower(p0, p1, width=1):
        r0, r1 = pltpu.roll(p0, width, 2), pltpu.roll(p1, width, 2)
        return jnp.where(lane < width, 0.0, r0), jnp.where(lane < width, r0, r1)

    def z_upper(p0, p1, width=1):
        r0, r1 = pltpu.roll(p0, 128 - width, 2), pltpu.roll(p1, 128 - width, 2)
        return jnp.where(lane >= 128 - width, r1, r0), jnp.where(lane >= 128 - width, 0.0, r1)

    def neighbour_sum(ref, half_ref, kyl, kyh, kzl, kzh, x, count, width):
        p = [plane(ref, h, x) for h in HALVES]
        zl, zh = z_lower(p[0], p[1], width), z_upper(p[0], p[1], width)
        here = [plane(half_ref, h, x) for h in HALVES]
        total = []
        for h in HALVES:
            s = plane(kyl, h, x) * y_lower(p[h], width) + plane(kyh, h, x) * y_upper(p[h], width)
            s = s + (plane(kzl, h, x) * zl[h] + plane(kzh, h, x) * zh[h])
            if x > 0:
                s = s + (here[h] + plane(half_ref, h, x - 1)) * plane(ref, h, x - 1)
            if x < count - 1:
                s = s + (here[h] + plane(half_ref, h, x + 1)) * plane(ref, h, x + 1)
            total.append(s)
        return total

    def fine_neighbours(ref, x):
        return neighbour_sum(ref, half_cond, ky_lo, ky_hi, kz_lo, kz_hi, x, NX, 1)

    def coarse_neighbours(ref, x):
        return neighbour_sum(ref, coarse_half, cky_lo, cky_hi, ckz_lo, ckz_hi, x, CX, 2)

    def coefficients(ref, kyl, kyh, kzl, kzh, diag_ref, x, count, width):
        p = [plane(ref, h, x) for h in HALVES]
        zl, zh = z_lower(p[0], p[1], width), z_upper(p[0], p[1], width)
        for h in HALVES:
            yl, yh = y_lower(p[h], width), y_upper(p[h], width)
            put(kyl, h, x, p[h] + yl)
            put(kyh, h, x, p[h] + yh)
            put(kzl, h, x, p[h] + zl[h])
            put(kzh, h, x, p[h] + zh[h])
            s = 6.0 * p[h] + ((yl + yh) + (zl[h] + zh[h]))
            if x > 0:
                s = s + plane(ref, h, x - 1)
            if x < count - 1:
                s = s + plane(ref, h, x + 1)
            put(diag_ref, h, x, s)

    def restrict(lower, upper):
        s = lower + upper
        s = s + jnp.where(even_sub2, pltpu.roll(s, 7, 0), pltpu.roll(s, 1, 0))
        s = s + jnp.where(even_lane2, pltpu.roll(s, 127, 1), pltpu.roll(s, 1, 1))
        return 0.125 * s

    def slot(face, index):
        return OFFSETS[face] + index

    def message(store, turn, face):
        return store.at[turn, pl.ds(OFFSETS[face], TURN_SIZES[turn][face])]

    def pack_x(dest, fine, coarse=None):
        for face, x in ((0, 0), (1, NX - 1)):
            for h in HALVES:
                dest[slot(face, 2 * h) : slot(face, 2 * h) + 2] = plane(fine, h, x)
        if coarse is not None:
            for face, x in ((0, 0), (1, CX - 1)):
                p = [plane(coarse, h, x) for h in HALVES]
                dest[slot(face, 4)] = jnp.where(
                    even_sub2, jnp.where(even_lane2, p[0][0], p[1][0]), jnp.where(even_lane2, p[0][1], p[1][1]))

    def pack_face_y(dest, face, fine, coarse=None):
        row = (NY - 1) * (face - 2)
        for h in HALVES:
            dest[slot(face, h)] = fine[h, pl.ds(row, NX, stride=NY), :]
            if coarse is not None:
                dest[slot(face, 2), CX * h : CX * (h + 1), :] = coarse[h, pl.ds(row, CX, stride=NY), :]

    def pack_y(dest, fine, coarse=None):
        for face in AXES[1]:
            pack_face_y(dest, face, fine, coarse)

    def pack_z(dest, fine, coarse=None):
        for face, h, source_lane in ((4, 0, 0), (5, 1, 127)):
            packed = jnp.zeros((8, 128), F32)
            for ref, count, start in ((fine, NX, 0), (coarse, CX, 16)):
                if ref is None:
                    continue
                for x in range(count):
                    p = plane(ref, h, x)
                    for t in TILES:
                        m = start + 2 * x + t
                        packed = jnp.where(lane2 == m, pltpu.roll(p[t], (m - source_lane) % 128, 1), packed)
            dest[slot(face, 0)] = packed

    def fine_z(q, half, x, t):
        lanes = 2 * x + t
        column = q[slot(4 + half, 0)][:, lanes : lanes + 1]
        return jnp.where(lane2 == 127 * half, jnp.broadcast_to(column, (8, 128)), 0.0)

    def coarse_z(q, half, x, t):
        lanes = 16 + 2 * x + t
        column = q[slot(4 + half, 0)][:, lanes : lanes + 1]
        return jnp.where(lane2 // 2 == 63 * half, jnp.broadcast_to(column, (8, 128)), 0.0)

    def fine_y(q, half, x, t):
        return jnp.where(sub2 == 7 * t, jnp.broadcast_to(q[slot(2 + t, half), x : x + 1, :], (8, 128)), 0.0)

    def coarse_y(q, half, x, t):
        row = CX * half + x
        return jnp.where(sub2 // 2 == 3 * t, jnp.broadcast_to(q[slot(2 + t, 2), row : row + 1, :], (8, 128)), 0.0)

    def fine_xz(q, half, x, t):
        added = fine_z(q, half, x, t)
        if x == 0:
            added = added + q[slot(0, 2 * half + t)]
        if x == NX - 1:
            added = added + q[slot(1, 2 * half + t)]
        return added

    def coarse_plane(q, half, face, t):
        packed = q[slot(face, 4)]
        if half == 0:
            p = jnp.where(even_lane2, packed, pltpu.roll(packed, 1, 1))
        else:
            p = jnp.where(even_lane2, pltpu.roll(packed, 127, 1), packed)
        return jnp.where(even_sub2, p, pltpu.roll(p, 1, 0)) if t == 0 else jnp.where(even_sub2, pltpu.roll(p, 7, 0), p)

    def coarse_xz(q, half, x, t):
        added = coarse_z(q, half, x, t)
        if x == 0:
            added = added + coarse_plane(q, half, 0, t)
        if x == CX - 1:
            added = added + coarse_plane(q, half, 1, t)
        return added

    def peer(face):
        name, step = FACES[face]
        return {name: place[name] + step}

    def copy(turn, face):
        return pltpu.make_async_remote_copy(
            src_ref=message(sent, turn, face),
            dst_ref=message(received, turn, face ^ 1),
            send_sem=send_sem.at[turn, face],
            recv_sem=recv_sem.at[turn, face ^ 1],
            device_id=peer(face),
            device_id_type=MESH,
        )

    def arrival(turn, face):
        return pltpu.make_async_remote_copy(
            src_ref=message(sent, turn, face),
            dst_ref=message(received, turn, face),
            send_sem=send_sem.at[turn, face],
            recv_sem=recv_sem.at[turn, face],
            device_id=peer(face),
            device_id_type=MESH,
        )

    def send(turn, faces_):
        for face in faces_:
            @pl.when(present[face])
            def _():
                copy(turn, face).start()

    def wait(turn, faces_):
        for face in faces_:
            @pl.when(present[face])
            def _():
                arrival(turn, face).wait_recv()

    def edge_copy(k, landing):
        return pltpu.make_async_remote_copy(
            src_ref=edge_sent.at[k],
            dst_ref=edge_received.at[landing],
            send_sem=edge_send_sem.at[k],
            recv_sem=edge_recv_sem.at[landing],
            device_id={**peer(EDGES[k][0]), **peer(EDGES[k][1])},
            device_id_type=MESH,
        )

    edge_present = [jnp.logical_and(present[a], present[b]) for a, b in EDGES]

    def send_edges(ks):
        for k in ks:
            a, b = EDGES[k]

            @pl.when(edge_present[k])
            def _():
                edge_copy(k, EDGES.index((a ^ 1, b ^ 1))).start()

    def wait_edges(ks):
        for k in ks:
            @pl.when(edge_present[k])
            def _():
                edge_copy(k, k).wait_recv()

    def wait_sent_edges():
        for k in range(len(EDGES)):
            @pl.when(edge_present[k])
            def _():
                edge_copy(k, k).wait_send()

    def row(ref, *index):
        return jnp.broadcast_to(ref[index[0], index[1] : index[1] + 1, :], (8, 128))

    def column(value, lane_):
        return jnp.broadcast_to(value[:, lane_ : lane_ + 1], (8, 128))

    def pack_edges(ks, turn):
        cond, update = sent.at[0], sent.at[turn]
        for k in ks:
            a, b = EDGES[k]
            if a < 2 and b < 4:
                for h in HALVES:
                    for j, ref in ((0, cond), (2, update)):
                        x, i = (NX - 1) * a, CX * h + (CX - 1) * a
                        edge_sent[k, j + h : j + h + 1, :] = ref[slot(b, h), x : x + 1, :]
                        edge_sent[k, j + h + 4 : j + h + 5, :] = ref[slot(b, 2), i : i + 1, :]
            elif a < 2:
                c, u = cond[slot(b, 0)], update[slot(b, 0)]
                fine, coarse = 2 * (NX - 1) * a, 16 + 2 * (CX - 1) * a
                packed = pltpu.roll(u, (6 - coarse) % 128, 1)
                packed = jnp.where(lane2 < 6, pltpu.roll(c, (4 - coarse) % 128, 1), packed)
                packed = jnp.where(lane2 < 4, pltpu.roll(u, (2 - fine) % 128, 1), packed)
                edge_sent[k] = jnp.where(lane2 < 2, pltpu.roll(c, (-fine) % 128, 1) if fine else c, packed)
            else:
                h, t = b - 4, a - 2
                packed = pltpu.roll(update[slot(a, 2)], (35 - 127 * h) % 128, 1)
                packed = jnp.where(lane2 < 35, pltpu.roll(cond[slot(a, 2)], (34 - 127 * h) % 128, 1), packed)
                packed = jnp.where(lane2 < 34, pltpu.roll(update[slot(a, h)], (33 - 127 * h) % 128, 1), packed)
                packed = jnp.where(lane2 < 33, pltpu.roll(cond[slot(a, h)], (32 - 127 * h) % 128, 1), packed)
                rows = jnp.where(sub2 == 0, row(cond, slot(b, 0), 7 * t), row(update, slot(b, 0), 7 * t))
                edge_sent[k] = jnp.where(lane2 < 32, rows, packed)

    def add_edges(face):
        def add(index, mask, c, u):
            i = slot(face, index)
            beside[i] = beside[i] + jnp.where(mask, (received[0, i] + c) * u, 0.0)

        for side in range(6):
            if side // 2 == face // 2:
                continue
            k = EDGES.index((min(face, side), max(face, side)))
            if face < 2 and side < 4:
                t = side - 2
                r = [row(edge_received, k, j) for j in range(8)]
                for h in HALVES:
                    add(2 * h + t, sub2 == 7 * t, r[h], r[2 + h])
                add(4, sub2 == 7 * t, jnp.where(even_lane2, r[4], r[5]), jnp.where(even_lane2, r[6], r[7]))
            elif face < 2:
                h = side - 4
                lines = edge_received[k]
                r = [column(lines, j) for j in range(8)]
                for t in TILES:
                    add(2 * h + t, lane2 == 127 * h, r[t], r[2 + t])
                add(4, lane2 == 127 * h, jnp.where(even_sub2, r[4], r[5]), jnp.where(even_sub2, r[6], r[7]))
            elif face < 4 and side < 2:
                for h in HALVES:
                    add(h, sub2 == 7 * side, row(edge_received, k, h), row(edge_received, k, 2 + h))
                    add(2, sub2 == CX * h + (CX - 1) * side, row(edge_received, k, 4 + h), row(edge_received, k, 6 + h))
            elif face < 4:
                h = side - 4
                lines = edge_received[k]
                other = pltpu.roll(lines, 4, 0)
                add(h, lane2 == 127 * h, column(lines, 32), column(lines, 33))
                add(2, jnp.logical_and(lane2 // 2 == 63 * h, sub2 // 4 == h), column(other, 34), column(other, 35))
            elif side < 2:
                lines = edge_received[k]
                for t in TILES:
                    add(0, lane2 == 14 * side + t, column(lines, t), column(lines, 2 + t))
                    add(0, lane2 == 16 + 6 * side + t, column(lines, 4 + t), column(lines, 6 + t))
            else:
                t = side - 2
                shift = 1 if t else 127
                c, u = (pltpu.roll(row(edge_received, k, j), shift, 1) for j in (0, 1))
                fine = jnp.logical_and(sub2 == 7 * t, lane2 < 16)
                coarse = jnp.logical_and(sub2 // 2 == 3 * t, jnp.logical_and(lane2 >= 16, lane2 < 24))
                add(0, jnp.logical_and(jnp.logical_or(fine, coarse), lane2 % 2 == t), c, u)

    def neighbour_field(face):
        base = OFFSETS[face]
        for i in range(base, base + BOTH[face]):
            beside[i] = FRESH * received[4, i] * beside[i]
        if face < 2:
            for h in HALVES:
                for t in TILES:
                    i = slot(face, 2 * h + t)
                    beside[i] = received[3, i] + beside[i] + coarse_plane(beside, h, face, t)
        elif face < 4:
            for h in HALVES:
                spread = row(beside, slot(face, 2), CX * h)
                for x in range(1, CX):
                    spread = jnp.where(sub2 // 2 == x, row(beside, slot(face, 2), CX * h + x), spread)
                beside[slot(face, h)] = received[3, slot(face, h)] + beside[slot(face, h)] + spread
        else:
            i = slot(face, 0)
            value = beside[i]
            spread = jnp.zeros((8, 128), F32)
            for x in range(NX):
                spread = jnp.where(lane2 // 2 == x, pltpu.roll(value, (2 * x - 16 - 2 * (x // 2)) % 128, 1), spread)
            beside[i] = received[3, i] + value + spread

    def wait_sent(turn):
        for face in range(6):
            @pl.when(present[face])
            def _():
                copy(turn, face).wait_send()

    barrier = pltpu.get_barrier_semaphore()
    for face in range(6):
        @pl.when(present[face])
        def _():
            pl.semaphore_signal(barrier, inc=1, device_id=peer(face), device_id_type=MESH)

    loads = []
    for index, (hbm, ref) in enumerate(((cond_hbm, half_cond), (field_hbm, field), (source_hbm, source))):
        pair = []
        for h in HALVES:
            load = pltpu.make_async_copy(hbm.at[:, pl.ds(128 * h, 128)], ref.at[h], in_sem.at[index, h])
            load.start()
            pair.append(load)
        loads.append(pair)

    for face in range(6):
        @pl.when(jnp.logical_not(present[face]))
        def _():
            for turn in range(TURNS):
                count = TURN_SIZES[turn][face]
                received[turn, OFFSETS[face] : OFFSETS[face] + count] = jnp.zeros((count, 8, 128), F32)

    for k in range(len(EDGES)):
        @pl.when(jnp.logical_not(edge_present[k]))
        def _():
            edge_received[k] = jnp.zeros((8, 128), F32)

    for load in loads[0]:
        load.wait()
    for x in range(NX):
        for h in HALVES:
            put(half_cond, h, x, 0.5 * plane(half_cond, h, x))
    for x in range(CX):
        for h in HALVES:
            for t in TILES:
                put_part(coarse_half, h, x, t, restrict(part(half_cond, h, 2 * x, t), part(half_cond, h, 2 * x + 1, t)))
    for pack in (pack_x, pack_y, pack_z):
        pack(sent.at[0], half_cond, coarse_half)
    pl.semaphore_wait(barrier, sum(p.astype(jnp.int32) for p in present))
    send(0, (3, 2, 1, 0, 5, 4))
    for load in loads[1]:
        load.wait()
    for axis, pack in ((1, pack_y), (0, pack_x), (2, pack_z)):
        pack(sent.at[1], field)
        send(1, AXES[axis])

    for x in range(NX):
        coefficients(half_cond, ky_lo, ky_hi, kz_lo, kz_hi, diag, x, NX, 1)
    for x in range(CX):
        coefficients(coarse_half, cky_lo, cky_hi, ckz_lo, ckz_hi, coarse_diag, x, CX, 2)
    for load in loads[2]:
        load.wait()

    def residual_part():
        for x in range(NX):
            total = fine_neighbours(field, x)
            for h in HALVES:
                put(partial, h, x, plane(source, h, x) - plane(diag, h, x) * plane(field, h, x) + total[h])

    residual_part()

    wait(0, (4, 5, 0, 1, 2, 3))
    for i in range(SLOTS):
        gains[i] = sent[0, i] + received[0, i]
    outside = received.at[0]
    for x in range(NX):
        for h in HALVES:
            for t in TILES:
                total = part(diag, h, x, t) + fine_xz(outside, h, x, t) + fine_y(outside, h, x, t)
                put_part(diag, h, x, t, total)
                put_part(inverse, h, x, t, 1.0 / total)
    for x in range(CX):
        for h in HALVES:
            for t in TILES:
                total = part(coarse_diag, h, x, t) + coarse_xz(outside, h, x, t) + coarse_y(outside, h, x, t)
                put_part(coarse_inverse, h, x, t, 1.0 / total)

    def add_near(ref):
        for x in range(NX):
            for h in HALVES:
                for t in TILES:
                    put_part(ref, h, x, t, part(ref, h, x, t) + fine_xz(faces, h, x, t))

    def smooth(x, t):
        for h in HALVES:
            pair = []
            for fx in (2 * x, 2 * x + 1):
                r = part(partial, h, fx, t) + fine_y(faces, h, fx, t)
                put_part(first, h, fx, t, FIRST_RATE * part(inverse, h, fx, t) * r)
                pair.append(r)
            put_part(coarse_first, h, x, t, 4.0 * FIRST_RATE * part(coarse_inverse, h, x, t) * restrict(*pair))

    def own_update():
        for x in range(CX):
            total = coarse_neighbours(coarse_first, x)
            coarse = [KEEP * plane(coarse_first, h, x) + FRESH * plane(coarse_inverse, h, x) * total[h] for h in HALVES]
            for fx in (2 * x, 2 * x + 1):
                total = fine_neighbours(first, fx)
                for h in HALVES:
                    fine = KEEP * plane(first, h, fx) + FRESH * plane(inverse, h, fx) * total[h]
                    put(partial, h, fx, plane(field, h, fx) + fine + coarse[h])

    def update_terms(turn, faces_):
        for face in faces_:
            for i in range(OFFSETS[face], OFFSETS[face] + BOTH[face]):
                faces[i] = scaled_gains[i] * received[turn, i]

    def finish(turn, last):
        wait(turn, near)
        update_terms(turn, near)
        for x in range(CX):
            for h in HALVES:
                for t in TILES:
                    coarse = coarse_xz(faces, h, x, t)
                    for fx in (2 * x, 2 * x + 1):
                        put_part(partial, h, fx, t, part(partial, h, fx, t) + coarse + fine_xz(faces, h, fx, t))
        for t in TILES:
            wait(turn, (2 + t,))
            update_terms(turn, (2 + t,))
            for x in range(CX):
                for h in HALVES:
                    coarse = coarse_y(faces, h, x, t)
                    for fx in (2 * x, 2 * x + 1):
                        value = part(partial, h, fx, t) + coarse + fine_y(faces, h, fx, t)
                        if last:
                            at = NY * fx + 8 * t
                            out[at : at + 8, 128 * h : 128 * (h + 1)] = value
                        else:
                            put_part(field, h, fx, t, value)

    near = (4, 5, 0, 1)
    every = near + (2, 3)

    def first_terms(faces_):
        for face in faces_:
            for i in range(OFFSETS[face], OFFSETS[face] + FINE[face]):
                faces[i] = gains[i] * received[1, i] - received[0, i] * sent[1, i]

    wait(1, near)
    first_terms(near)
    add_near(partial)
    for t in TILES:
        wait(1, (2 + t,))
        first_terms((2 + t,))
        for x in range(CX):
            smooth(x, t)
        pack_face_y(sent.at[2], 2 + t, first, coarse_first)
        send(2, (2 + t,))
    pack_edges(range(4), 2)
    send_edges(range(4))
    pack_z(sent.at[2], first, coarse_first)
    pack_edges(range(4, 12), 2)
    send_edges(range(4, 12))
    pack_x(sent.at[2], first, coarse_first)
    send(2, near)

    own_update()
    pack_y(sent.at[3], partial)
    send(3, AXES[1])
    pack_x(sent.at[3], partial)
    send(3, AXES[0])
    pack_z(sent.at[3], partial)
    send(3, AXES[2])
    for axis, pack in ((1, pack_y), (0, pack_x), (2, pack_z)):
        pack(sent.at[4], inverse, coarse_inverse)
        send(4, AXES[axis])
    for i in range(SLOTS):
        scaled_gains[i] = FRESH * sent[4, i] * gains[i]
        beside[i] = gains[i] * sent[2, i]
    wait_sent(0)
    wait_sent(1)
    finish(2, False)
    residual_part()

    wait(3, every)
    wait(4, every)
    wait_edges(range(12))
    for face in every:
        add_edges(face)
        neighbour_field(face)
        for i in range(OFFSETS[face], OFFSETS[face] + FINE[face]):
            faces[i] = gains[i] * beside[i]
    add_near(partial)
    for t in TILES:
        for x in range(CX):
            smooth(x, t)
        pack_face_y(sent.at[5], 2 + t, first, coarse_first)
        send(5, (2 + t,))
    pack_x(sent.at[5], first, coarse_first)
    send(5, AXES[0])
    pack_z(sent.at[5], first, coarse_first)
    send(5, AXES[2])
    own_update()
    for turn in (2, 3, 4):
        wait_sent(turn)
    wait_sent_edges()
    finish(5, True)
    wait_sent(TURNS - 1)


def block(source_term, conductivity, initial_field):
    def fine():
        return pltpu.VMEM((2, ROWS, 128), F32)

    def coarse():
        return pltpu.VMEM((2, CX * NY, 128), F32)

    hbm = pl.BlockSpec(memory_space=pltpu.HBM)
    result = pl.pallas_call(
        kernel,
        out_shape=pltpu.VMEM((ROWS, NZ), F32),
        in_specs=[hbm] * 3,
        out_specs=pl.BlockSpec(memory_space=pltpu.VMEM),
        scratch_shapes=[
            *(fine() for _ in range(11)),
            *(coarse() for _ in range(8)),
            *(pltpu.VMEM((SLOTS, 8, 128), F32) for _ in range(4)),
            *(pltpu.VMEM((len(EDGES), 8, 128), F32) for _ in range(2)),
            *(pltpu.VMEM((TURNS, SLOTS, 8, 128), F32) for _ in range(2)),
            pltpu.SemaphoreType.DMA((3, 2)),
            *(pltpu.SemaphoreType.DMA((TURNS, 6)) for _ in range(2)),
            *(pltpu.SemaphoreType.DMA((len(EDGES),)) for _ in range(2)),
        ],
        compiler_params=pltpu.CompilerParams(collective_id=0, has_side_effects=True),
    )(*(a.reshape(ROWS, NZ) for a in (source_term, conductivity, initial_field)))
    return result.reshape(NX, NY, NZ)


def solution(mesh):
    spec = P("gx", "gy", "grp")
    return jax.shard_map(block, mesh=mesh, in_specs=(spec,) * 3, out_specs=spec, check_vma=False)
```

```python
import functools

import jax
import jax.numpy as jnp
from jax import lax
from jax.experimental import pallas as pl
from jax.experimental.pallas import tpu as pltpu
from jax.sharding import PartitionSpec as P

MESH = pl.DeviceIdType.MESH
F32 = jnp.float32

NX, NY, NZ = 8, 16, 256
CX = NX // 2
ROWS = NX * NY
HALVES = (0, 1)
TILES = (0, 1)

FIRST_RATE = 0.8
KEEP = 60.0 / 41.0
FRESH = 40.0 / 41.0

FACES = (("gx", -1), ("gx", 1), ("gy", -1), ("gy", 1), ("grp", -1), ("grp", 1))
BOTH = (5, 5, 3, 3, 1, 1)
FINE = (4, 4, 2, 2, 1, 1)
TURN_SIZES = (BOTH, FINE, BOTH, FINE, BOTH, BOTH)
TURNS = len(TURN_SIZES)
OFFSETS = (0, 5, 10, 13, 16, 17)
SLOTS = 18
AXES = ((0, 1), (2, 3), (4, 5))
EDGES = [(a, b) for p, q in ((0, 1), (0, 2), (1, 2)) for a in AXES[p] for b in AXES[q]]


def iota(shape, dim):
    return lax.broadcasted_iota(jnp.int32, shape, dim)


def kernel(source_hbm, cond_hbm, field_hbm, out, source, half_cond, field, first, ky_lo, ky_hi, kz_lo, kz_hi,
           diag, inverse, partial, coarse_half, cky_lo, cky_hi, ckz_lo, ckz_hi, coarse_diag, coarse_inverse, coarse_first,
           faces, gains, scaled_gains, beside, edge_sent, edge_received, sent,
           received, in_sem, send_sem, recv_sem, edge_send_sem, edge_recv_sem):
    sub, lane = iota((2, 8, 128), 1), iota((2, 8, 128), 2)
    sub2, lane2 = iota((8, 128), 0), iota((8, 128), 1)
    even_sub2, even_lane2 = sub2 % 2 == 0, lane2 % 2 == 0
    zero = jnp.zeros((1, 8, 128), F32)

    place = {name: lax.axis_index(name) for name in ("grp", "gx", "gy")}
    size = {name: lax.axis_size(name) for name in ("grp", "gx", "gy")}
    present = []
    for name, step in FACES:
        present.append(place[name] > 0 if step < 0 else place[name] < size[name] - 1)

    def plane(ref, half, x):
        return ref[half, NY * x : NY * (x + 1), :].reshape(2, 8, 128)

    def put(ref, half, x, value):
        ref[half, NY * x : NY * (x + 1), :] = value.reshape(16, 128)

    def part(ref, half, x, t):
        return ref[half, NY * x + 8 * t : NY * x + 8 * t + 8, :]

    def put_part(ref, half, x, t, value):
        ref[half, NY * x + 8 * t : NY * x + 8 * t + 8, :] = value

    def y_lower(p, width=1):
        rolled = pltpu.roll(p, width, 1)
        return jnp.where(sub < width, jnp.concatenate([zero, rolled[:1]], axis=0), rolled)

    def y_upper(p, width=1):
        rolled = pltpu.roll(p, 8 - width, 1)
        return jnp.where(sub >= 8 - width, jnp.concatenate([rolled[1:], zero], axis=0), rolled)

    def z_lower(p0, p1, width=1):
        r0, r1 = pltpu.roll(p0, width, 2), pltpu.roll(p1, width, 2)
        return jnp.where(lane < width, 0.0, r0), jnp.where(lane < width, r0, r1)

    def z_upper(p0, p1, width=1):
        r0, r1 = pltpu.roll(p0, 128 - width, 2), pltpu.roll(p1, 128 - width, 2)
        return jnp.where(lane >= 128 - width, r1, r0), jnp.where(lane >= 128 - width, 0.0, r1)

    def neighbour_sum(ref, half_ref, kyl, kyh, kzl, kzh, x, count, width):
        p = [plane(ref, h, x) for h in HALVES]
        zl, zh = z_lower(p[0], p[1], width), z_upper(p[0], p[1], width)
        here = [plane(half_ref, h, x) for h in HALVES]
        total = []
        for h in HALVES:
            s = plane(kyl, h, x) * y_lower(p[h], width) + plane(kyh, h, x) * y_upper(p[h], width)
            s = s + (plane(kzl, h, x) * zl[h] + plane(kzh, h, x) * zh[h])
            if x > 0:
                s = s + (here[h] + plane(half_ref, h, x - 1)) * plane(ref, h, x - 1)
            if x < count - 1:
                s = s + (here[h] + plane(half_ref, h, x + 1)) * plane(ref, h, x + 1)
            total.append(s)
        return total

    def fine_neighbours(ref, x):
        return neighbour_sum(ref, half_cond, ky_lo, ky_hi, kz_lo, kz_hi, x, NX, 1)

    def coarse_neighbours(ref, x):
        return neighbour_sum(ref, coarse_half, cky_lo, cky_hi, ckz_lo, ckz_hi, x, CX, 2)

    def coefficients(ref, kyl, kyh, kzl, kzh, diag_ref, x, count, width):
        p = [plane(ref, h, x) for h in HALVES]
        zl, zh = z_lower(p[0], p[1], width), z_upper(p[0], p[1], width)
        for h in HALVES:
            yl, yh = y_lower(p[h], width), y_upper(p[h], width)
            put(kyl, h, x, p[h] + yl)
            put(kyh, h, x, p[h] + yh)
            put(kzl, h, x, p[h] + zl[h])
            put(kzh, h, x, p[h] + zh[h])
            s = 6.0 * p[h] + ((yl + yh) + (zl[h] + zh[h]))
            if x > 0:
                s = s + plane(ref, h, x - 1)
            if x < count - 1:
                s = s + plane(ref, h, x + 1)
            put(diag_ref, h, x, s)

    def restrict(lower, upper):
        s = lower + upper
        s = s + jnp.where(even_sub2, pltpu.roll(s, 7, 0), pltpu.roll(s, 1, 0))
        s = s + jnp.where(even_lane2, pltpu.roll(s, 127, 1), pltpu.roll(s, 1, 1))
        return 0.125 * s

    def slot(face, index):
        return OFFSETS[face] + index

    def message(store, turn, face):
        return store.at[turn, pl.ds(OFFSETS[face], TURN_SIZES[turn][face])]

    def pack_x(dest, fine, coarse=None):
        for face, x in ((0, 0), (1, NX - 1)):
            for h in HALVES:
                dest[slot(face, 2 * h) : slot(face, 2 * h) + 2] = plane(fine, h, x)
        if coarse is not None:
            for face, x in ((0, 0), (1, CX - 1)):
                p = [plane(coarse, h, x) for h in HALVES]
                dest[slot(face, 4)] = jnp.where(
                    even_sub2, jnp.where(even_lane2, p[0][0], p[1][0]), jnp.where(even_lane2, p[0][1], p[1][1]))

    def pack_face_y(dest, face, fine, coarse=None):
        row = (NY - 1) * (face - 2)
        for h in HALVES:
            dest[slot(face, h)] = fine[h, pl.ds(row, NX, stride=NY), :]
            if coarse is not None:
                dest[slot(face, 2), CX * h : CX * (h + 1), :] = coarse[h, pl.ds(row, CX, stride=NY), :]

    def pack_y(dest, fine, coarse=None):
        for face in AXES[1]:
            pack_face_y(dest, face, fine, coarse)

    def pack_z(dest, fine, coarse=None):
        for face, h, source_lane in ((4, 0, 0), (5, 1, 127)):
            packed = jnp.zeros((8, 128), F32)
            for ref, count, start in ((fine, NX, 0), (coarse, CX, 16)):
                if ref is None:
                    continue
                for x in range(count):
                    p = plane(ref, h, x)
                    for t in TILES:
                        m = start + 2 * x + t
                        packed = jnp.where(lane2 == m, pltpu.roll(p[t], (m - source_lane) % 128, 1), packed)
            dest[slot(face, 0)] = packed

    def fine_z(q, half, x, t):
        lanes = 2 * x + t
        column = q[slot(4 + half, 0)][:, lanes : lanes + 1]
        return jnp.where(lane2 == 127 * half, jnp.broadcast_to(column, (8, 128)), 0.0)

    def coarse_z(q, half, x, t):
        lanes = 16 + 2 * x + t
        column = q[slot(4 + half, 0)][:, lanes : lanes + 1]
        return jnp.where(lane2 // 2 == 63 * half, jnp.broadcast_to(column, (8, 128)), 0.0)

    def fine_y(q, half, x, t):
        return jnp.where(sub2 == 7 * t, jnp.broadcast_to(q[slot(2 + t, half), x : x + 1, :], (8, 128)), 0.0)

    def coarse_y(q, half, x, t):
        row = CX * half + x
        return jnp.where(sub2 // 2 == 3 * t, jnp.broadcast_to(q[slot(2 + t, 2), row : row + 1, :], (8, 128)), 0.0)

    def fine_xz(q, half, x, t):
        added = fine_z(q, half, x, t)
        if x == 0:
            added = added + q[slot(0, 2 * half + t)]
        if x == NX - 1:
            added = added + q[slot(1, 2 * half + t)]
        return added

    def coarse_plane(q, half, face, t):
        packed = q[slot(face, 4)]
        if half == 0:
            p = jnp.where(even_lane2, packed, pltpu.roll(packed, 1, 1))
        else:
            p = jnp.where(even_lane2, pltpu.roll(packed, 127, 1), packed)
        return jnp.where(even_sub2, p, pltpu.roll(p, 1, 0)) if t == 0 else jnp.where(even_sub2, pltpu.roll(p, 7, 0), p)

    def coarse_xz(q, half, x, t):
        added = coarse_z(q, half, x, t)
        if x == 0:
            added = added + coarse_plane(q, half, 0, t)
        if x == CX - 1:
            added = added + coarse_plane(q, half, 1, t)
        return added

    def peer(face):
        name, step = FACES[face]
        return {name: place[name] + step}

    def copy(turn, face):
        return pltpu.make_async_remote_copy(
            src_ref=message(sent, turn, face),
            dst_ref=message(received, turn, face ^ 1),
            send_sem=send_sem.at[turn, face],
            recv_sem=recv_sem.at[turn, face ^ 1],
            device_id=peer(face),
            device_id_type=MESH,
        )

    def arrival(turn, face):
        return pltpu.make_async_remote_copy(
            src_ref=message(sent, turn, face),
            dst_ref=message(received, turn, face),
            send_sem=send_sem.at[turn, face],
            recv_sem=recv_sem.at[turn, face],
            device_id=peer(face),
            device_id_type=MESH,
        )

    def send(turn, faces_):
        for face in faces_:
            @pl.when(present[face])
            def _():
                copy(turn, face).start()

    def wait(turn, faces_):
        for face in faces_:
            @pl.when(present[face])
            def _():
                arrival(turn, face).wait_recv()

    def edge_copy(k, landing):
        return pltpu.make_async_remote_copy(
            src_ref=edge_sent.at[k],
            dst_ref=edge_received.at[landing],
            send_sem=edge_send_sem.at[k],
            recv_sem=edge_recv_sem.at[landing],
            device_id={**peer(EDGES[k][0]), **peer(EDGES[k][1])},
            device_id_type=MESH,
        )

    edge_present = [jnp.logical_and(present[a], present[b]) for a, b in EDGES]

    def send_edges(ks):
        for k in ks:
            a, b = EDGES[k]

            @pl.when(edge_present[k])
            def _():
                edge_copy(k, EDGES.index((a ^ 1, b ^ 1))).start()

    def wait_edges(ks):
        for k in ks:
            @pl.when(edge_present[k])
            def _():
                edge_copy(k, k).wait_recv()

    def wait_sent_edges():
        for k in range(len(EDGES)):
            @pl.when(edge_present[k])
            def _():
                edge_copy(k, k).wait_send()

    def row(ref, *index):
        return jnp.broadcast_to(ref[index[0], index[1] : index[1] + 1, :], (8, 128))

    def column(value, lane_):
        return jnp.broadcast_to(value[:, lane_ : lane_ + 1], (8, 128))

    def pack_edges(ks, turn):
        cond, update = sent.at[0], sent.at[turn]
        for k in ks:
            a, b = EDGES[k]
            if a < 2 and b < 4:
                for h in HALVES:
                    for j, ref in ((0, cond), (2, update)):
                        x, i = (NX - 1) * a, CX * h + (CX - 1) * a
                        edge_sent[k, j + h : j + h + 1, :] = ref[slot(b, h), x : x + 1, :]
                        edge_sent[k, j + h + 4 : j + h + 5, :] = ref[slot(b, 2), i : i + 1, :]
            elif a < 2:
                c, u = cond[slot(b, 0)], update[slot(b, 0)]
                fine, coarse = 2 * (NX - 1) * a, 16 + 2 * (CX - 1) * a
                packed = pltpu.roll(u, (6 - coarse) % 128, 1)
                packed = jnp.where(lane2 < 6, pltpu.roll(c, (4 - coarse) % 128, 1), packed)
                packed = jnp.where(lane2 < 4, pltpu.roll(u, (2 - fine) % 128, 1), packed)
                edge_sent[k] = jnp.where(lane2 < 2, pltpu.roll(c, (-fine) % 128, 1) if fine else c, packed)
            else:
                h, t = b - 4, a - 2
                packed = pltpu.roll(update[slot(a, 2)], (35 - 127 * h) % 128, 1)
                packed = jnp.where(lane2 < 35, pltpu.roll(cond[slot(a, 2)], (34 - 127 * h) % 128, 1), packed)
                packed = jnp.where(lane2 < 34, pltpu.roll(update[slot(a, h)], (33 - 127 * h) % 128, 1), packed)
                packed = jnp.where(lane2 < 33, pltpu.roll(cond[slot(a, h)], (32 - 127 * h) % 128, 1), packed)
                rows = jnp.where(sub2 == 0, row(cond, slot(b, 0), 7 * t), row(update, slot(b, 0), 7 * t))
                edge_sent[k] = jnp.where(lane2 < 32, rows, packed)

    def add_edges(face, sides):
        def add(index, mask, c, u):
            i = slot(face, index)
            beside[i] = beside[i] + jnp.where(mask, (received[0, i] + c) * u, 0.0)

        for side in sides:
            k = EDGES.index((min(face, side), max(face, side)))
            if face < 2 and side < 4:
                t = side - 2
                r = [row(edge_received, k, j) for j in range(8)]
                for h in HALVES:
                    add(2 * h + t, sub2 == 7 * t, r[h], r[2 + h])
                add(4, sub2 == 7 * t, jnp.where(even_lane2, r[4], r[5]), jnp.where(even_lane2, r[6], r[7]))
            elif face < 2:
                h = side - 4
                lines = edge_received[k]
                r = [column(lines, j) for j in range(8)]
                for t in TILES:
                    add(2 * h + t, lane2 == 127 * h, r[t], r[2 + t])
                add(4, lane2 == 127 * h, jnp.where(even_sub2, r[4], r[5]), jnp.where(even_sub2, r[6], r[7]))
            elif face < 4 and side < 2:
                for h in HALVES:
                    add(h, sub2 == 7 * side, row(edge_received, k, h), row(edge_received, k, 2 + h))
                    add(2, sub2 == CX * h + (CX - 1) * side, row(edge_received, k, 4 + h), row(edge_received, k, 6 + h))
            elif face < 4:
                h = side - 4
                lines = edge_received[k]
                other = pltpu.roll(lines, 4, 0)
                add(h, lane2 == 127 * h, column(lines, 32), column(lines, 33))
                add(2, jnp.logical_and(lane2 // 2 == 63 * h, sub2 // 4 == h), column(other, 34), column(other, 35))
            elif side < 2:
                lines = edge_received[k]
                for t in TILES:
                    add(0, lane2 == 14 * side + t, column(lines, t), column(lines, 2 + t))
                    add(0, lane2 == 16 + 6 * side + t, column(lines, 4 + t), column(lines, 6 + t))
            else:
                t = side - 2
                shift = 1 if t else 127
                c, u = (pltpu.roll(row(edge_received, k, j), shift, 1) for j in (0, 1))
                fine = jnp.logical_and(sub2 == 7 * t, lane2 < 16)
                coarse = jnp.logical_and(sub2 // 2 == 3 * t, jnp.logical_and(lane2 >= 16, lane2 < 24))
                add(0, jnp.logical_and(jnp.logical_or(fine, coarse), lane2 % 2 == t), c, u)

    def neighbour_field(face):
        base = OFFSETS[face]
        for i in range(base, base + BOTH[face]):
            beside[i] = FRESH * received[4, i] * beside[i]
        if face < 2:
            for h in HALVES:
                for t in TILES:
                    i = slot(face, 2 * h + t)
                    beside[i] = received[3, i] + beside[i] + coarse_plane(beside, h, face, t)
        elif face < 4:
            for h in HALVES:
                spread = row(beside, slot(face, 2), CX * h)
                for x in range(1, CX):
                    spread = jnp.where(sub2 // 2 == x, row(beside, slot(face, 2), CX * h + x), spread)
                beside[slot(face, h)] = received[3, slot(face, h)] + beside[slot(face, h)] + spread
        else:
            i = slot(face, 0)
            value = beside[i]
            spread = jnp.zeros((8, 128), F32)
            for x in range(NX):
                spread = jnp.where(lane2 // 2 == x, pltpu.roll(value, (2 * x - 16 - 2 * (x // 2)) % 128, 1), spread)
            beside[i] = received[3, i] + value + spread

    def wait_sent(turn):
        for face in range(6):
            @pl.when(present[face])
            def _():
                copy(turn, face).wait_send()

    barrier = pltpu.get_barrier_semaphore()
    for face in range(6):
        @pl.when(present[face])
        def _():
            pl.semaphore_signal(barrier, inc=1, device_id=peer(face), device_id_type=MESH)

    loads = []
    for index, (hbm, ref) in enumerate(((cond_hbm, half_cond), (field_hbm, field), (source_hbm, source))):
        pair = []
        for h in HALVES:
            load = pltpu.make_async_copy(hbm.at[:, pl.ds(128 * h, 128)], ref.at[h], in_sem.at[index, h])
            load.start()
            pair.append(load)
        loads.append(pair)

    for face in range(6):
        @pl.when(jnp.logical_not(present[face]))
        def _():
            for turn in range(TURNS):
                count = TURN_SIZES[turn][face]
                received[turn, OFFSETS[face] : OFFSETS[face] + count] = jnp.zeros((count, 8, 128), F32)

    for k in range(len(EDGES)):
        @pl.when(jnp.logical_not(edge_present[k]))
        def _():
            edge_received[k] = jnp.zeros((8, 128), F32)

    for load in loads[0]:
        load.wait()
    for x in range(NX):
        for h in HALVES:
            put(half_cond, h, x, 0.5 * plane(half_cond, h, x))
    for x in range(CX):
        for h in HALVES:
            for t in TILES:
                put_part(coarse_half, h, x, t, restrict(part(half_cond, h, 2 * x, t), part(half_cond, h, 2 * x + 1, t)))
    for pack in (pack_x, pack_y, pack_z):
        pack(sent.at[0], half_cond, coarse_half)
    pl.semaphore_wait(barrier, sum(p.astype(jnp.int32) for p in present))
    send(0, (3, 2, 1, 0, 5, 4))
    for load in loads[1]:
        load.wait()
    for axis, pack in ((1, pack_y), (0, pack_x), (2, pack_z)):
        pack(sent.at[1], field)
        send(1, AXES[axis])

    for x in range(NX):
        coefficients(half_cond, ky_lo, ky_hi, kz_lo, kz_hi, diag, x, NX, 1)
    for x in range(CX):
        coefficients(coarse_half, cky_lo, cky_hi, ckz_lo, ckz_hi, coarse_diag, x, CX, 2)
    for load in loads[2]:
        load.wait()

    def residual_part():
        for x in range(NX):
            total = fine_neighbours(field, x)
            for h in HALVES:
                put(partial, h, x, plane(source, h, x) - plane(diag, h, x) * plane(field, h, x) + total[h])

    residual_part()

    wait(0, (4, 5, 0, 1, 2, 3))
    for i in range(SLOTS):
        gains[i] = sent[0, i] + received[0, i]
    outside = received.at[0]
    for x in range(NX):
        for h in HALVES:
            for t in TILES:
                total = part(diag, h, x, t) + fine_xz(outside, h, x, t) + fine_y(outside, h, x, t)
                put_part(diag, h, x, t, total)
                put_part(inverse, h, x, t, 1.0 / total)
    for x in range(CX):
        for h in HALVES:
            for t in TILES:
                total = part(coarse_diag, h, x, t) + coarse_xz(outside, h, x, t) + coarse_y(outside, h, x, t)
                put_part(coarse_inverse, h, x, t, 1.0 / total)

    def add_near(ref):
        for x in range(NX):
            for h in HALVES:
                for t in TILES:
                    put_part(ref, h, x, t, part(ref, h, x, t) + fine_xz(faces, h, x, t))

    def smooth(x, t):
        for h in HALVES:
            pair = []
            for fx in (2 * x, 2 * x + 1):
                r = part(partial, h, fx, t) + fine_y(faces, h, fx, t)
                put_part(first, h, fx, t, FIRST_RATE * part(inverse, h, fx, t) * r)
                pair.append(r)
            put_part(coarse_first, h, x, t, 4.0 * FIRST_RATE * part(coarse_inverse, h, x, t) * restrict(*pair))

    def own_update():
        for x in range(CX):
            total = coarse_neighbours(coarse_first, x)
            coarse = [KEEP * plane(coarse_first, h, x) + FRESH * plane(coarse_inverse, h, x) * total[h] for h in HALVES]
            for fx in (2 * x, 2 * x + 1):
                total = fine_neighbours(first, fx)
                for h in HALVES:
                    fine = KEEP * plane(first, h, fx) + FRESH * plane(inverse, h, fx) * total[h]
                    put(partial, h, fx, plane(field, h, fx) + fine + coarse[h])

    def update_terms(turn, faces_):
        for face in faces_:
            for i in range(OFFSETS[face], OFFSETS[face] + BOTH[face]):
                faces[i] = scaled_gains[i] * received[turn, i]

    def finish(turn, last):
        wait(turn, near)
        update_terms(turn, near)
        for x in range(CX):
            for h in HALVES:
                for t in TILES:
                    coarse = coarse_xz(faces, h, x, t)
                    for fx in (2 * x, 2 * x + 1):
                        put_part(partial, h, fx, t, part(partial, h, fx, t) + coarse + fine_xz(faces, h, fx, t))
        for t in TILES:
            wait(turn, (2 + t,))
            update_terms(turn, (2 + t,))
            for x in range(CX):
                for h in HALVES:
                    coarse = coarse_y(faces, h, x, t)
                    for fx in (2 * x, 2 * x + 1):
                        value = part(partial, h, fx, t) + coarse + fine_y(faces, h, fx, t)
                        if last:
                            at = NY * fx + 8 * t
                            out[at : at + 8, 128 * h : 128 * (h + 1)] = value
                        else:
                            put_part(field, h, fx, t, value)

    near = (4, 5, 0, 1)
    every = near + (2, 3)

    def first_terms(faces_):
        for face in faces_:
            for i in range(OFFSETS[face], OFFSETS[face] + FINE[face]):
                faces[i] = gains[i] * received[1, i] - received[0, i] * sent[1, i]

    wait(1, near)
    first_terms(near)
    add_near(partial)
    for t in TILES:
        wait(1, (2 + t,))
        first_terms((2 + t,))
        for x in range(CX):
            smooth(x, t)
        pack_face_y(sent.at[2], 2 + t, first, coarse_first)
    pack_edges(range(4), 2)
    send_edges(range(4))
    send(2, AXES[1])
    pack_z(sent.at[2], first, coarse_first)
    pack_edges(range(4, 12), 2)
    send_edges(range(4, 12))
    pack_x(sent.at[2], first, coarse_first)
    send(2, near)

    own_update()
    pack_y(sent.at[3], partial)
    send(3, AXES[1])
    pack_x(sent.at[3], partial)
    send(3, AXES[0])
    pack_z(sent.at[3], partial)
    send(3, AXES[2])
    for axis, pack in ((1, pack_y), (0, pack_x), (2, pack_z)):
        pack(sent.at[4], inverse, coarse_inverse)
        send(4, AXES[axis])
    for i in range(SLOTS):
        scaled_gains[i] = FRESH * sent[4, i] * gains[i]
        beside[i] = gains[i] * sent[2, i]
    wait_sent(0)
    wait_sent(1)
    finish(2, False)
    residual_part()

    wait_edges(range(4, 12))
    for face in near:
        add_edges(face, (2, 3) if face >= 4 else (4, 5))
    for face in AXES[1]:
        add_edges(face, (4, 5))
    for face in AXES[2]:
        add_edges(face, (0, 1))
    wait(3, every)
    wait(4, every)
    def second_terms(faces_):
        for face in faces_:
            neighbour_field(face)
            for i in range(OFFSETS[face], OFFSETS[face] + FINE[face]):
                faces[i] = gains[i] * beside[i]

    second_terms(AXES[2])
    for x in range(NX):
        for h in HALVES:
            for t in TILES:
                put_part(partial, h, x, t, part(partial, h, x, t) + fine_z(faces, h, x, t))
    wait_edges(range(4))
    for face in AXES[1]:
        add_edges(face, (0, 1))
    for face in AXES[0]:
        add_edges(face, (2, 3))
    second_terms((2, 3, 0, 1))
    for face, x in ((0, 0), (1, NX - 1)):
        for h in HALVES:
            for t in TILES:
                put_part(partial, h, x, t, part(partial, h, x, t) + faces[slot(face, 2 * h + t)])
    for t in TILES:
        for x in range(CX):
            smooth(x, t)
        pack_face_y(sent.at[5], 2 + t, first, coarse_first)
        send(5, (2 + t,))
    pack_x(sent.at[5], first, coarse_first)
    send(5, AXES[0])
    pack_z(sent.at[5], first, coarse_first)
    send(5, AXES[2])
    own_update()
    for turn in (2, 3, 4):
        wait_sent(turn)
    wait_sent_edges()
    finish(5, True)
    wait_sent(TURNS - 1)


def block(source_term, conductivity, initial_field):
    def fine():
        return pltpu.VMEM((2, ROWS, 128), F32)

    def coarse():
        return pltpu.VMEM((2, CX * NY, 128), F32)

    hbm = pl.BlockSpec(memory_space=pltpu.HBM)
    result = pl.pallas_call(
        kernel,
        out_shape=pltpu.VMEM((ROWS, NZ), F32),
        in_specs=[hbm] * 3,
        out_specs=pl.BlockSpec(memory_space=pltpu.VMEM),
        scratch_shapes=[
            *(fine() for _ in range(11)),
            *(coarse() for _ in range(8)),
            *(pltpu.VMEM((SLOTS, 8, 128), F32) for _ in range(4)),
            *(pltpu.VMEM((len(EDGES), 8, 128), F32) for _ in range(2)),
            *(pltpu.VMEM((TURNS, SLOTS, 8, 128), F32) for _ in range(2)),
            pltpu.SemaphoreType.DMA((3, 2)),
            *(pltpu.SemaphoreType.DMA((TURNS, 6)) for _ in range(2)),
            *(pltpu.SemaphoreType.DMA((len(EDGES),)) for _ in range(2)),
        ],
        compiler_params=pltpu.CompilerParams(collective_id=0, has_side_effects=True),
    )(*(a.reshape(ROWS, NZ) for a in (source_term, conductivity, initial_field)))
    return result.reshape(NX, NY, NZ)


def solution(mesh):
    spec = P("gx", "gy", "grp")
    return jax.shard_map(block, mesh=mesh, in_specs=(spec,) * 3, out_specs=spec, check_vma=False)
```

```python
import functools

import jax
import jax.numpy as jnp
from jax import lax
from jax.experimental import pallas as pl
from jax.experimental.pallas import tpu as pltpu
from jax.sharding import PartitionSpec as P

MESH = pl.DeviceIdType.MESH
F32 = jnp.float32

NX, NY, NZ = 8, 16, 256
CX = NX // 2
ROWS = NX * NY
HALVES = (0, 1)
TILES = (0, 1)

FIRST_RATE = 0.8
KEEP = 60.0 / 41.0
FRESH = 40.0 / 41.0

FACES = (("gx", -1), ("gx", 1), ("gy", -1), ("gy", 1), ("grp", -1), ("grp", 1))
BOTH = (5, 5, 3, 3, 1, 1)
FINE = (4, 4, 2, 2, 1, 1)
TURN_SIZES = (BOTH, FINE, BOTH, FINE, BOTH, BOTH)
TURNS = len(TURN_SIZES)
OFFSETS = (0, 5, 10, 13, 16, 17)
SLOTS = 18
AXES = ((0, 1), (2, 3), (4, 5))
EDGES = [(a, b) for p, q in ((0, 1), (0, 2), (1, 2)) for a in AXES[p] for b in AXES[q]]


def iota(shape, dim):
    return lax.broadcasted_iota(jnp.int32, shape, dim)


def kernel(source_hbm, cond_hbm, field_hbm, out, source, half_cond, field, first, ky_lo, ky_hi, kz_lo, kz_hi,
           diag, inverse, partial, coarse_half, cky_lo, cky_hi, ckz_lo, ckz_hi, coarse_diag, coarse_inverse, coarse_first,
           faces, gains, scaled_gains, beside, edge_sent, edge_received, sent,
           received, in_sem, send_sem, recv_sem, edge_send_sem, edge_recv_sem):
    sub, lane = iota((2, 8, 128), 1), iota((2, 8, 128), 2)
    sub2, lane2 = iota((8, 128), 0), iota((8, 128), 1)
    even_sub2, even_lane2 = sub2 % 2 == 0, lane2 % 2 == 0
    zero = jnp.zeros((1, 8, 128), F32)

    place = {name: lax.axis_index(name) for name in ("grp", "gx", "gy")}
    size = {name: lax.axis_size(name) for name in ("grp", "gx", "gy")}
    present = []
    for name, step in FACES:
        present.append(place[name] > 0 if step < 0 else place[name] < size[name] - 1)

    def plane(ref, half, x):
        return ref[half, NY * x : NY * (x + 1), :].reshape(2, 8, 128)

    def put(ref, half, x, value):
        ref[half, NY * x : NY * (x + 1), :] = value.reshape(16, 128)

    def part(ref, half, x, t):
        return ref[half, NY * x + 8 * t : NY * x + 8 * t + 8, :]

    def put_part(ref, half, x, t, value):
        ref[half, NY * x + 8 * t : NY * x + 8 * t + 8, :] = value

    def y_lower(p, width=1):
        rolled = pltpu.roll(p, width, 1)
        return jnp.where(sub < width, jnp.concatenate([zero, rolled[:1]], axis=0), rolled)

    def y_upper(p, width=1):
        rolled = pltpu.roll(p, 8 - width, 1)
        return jnp.where(sub >= 8 - width, jnp.concatenate([rolled[1:], zero], axis=0), rolled)

    def z_lower(p0, p1, width=1):
        r0, r1 = pltpu.roll(p0, width, 2), pltpu.roll(p1, width, 2)
        return jnp.where(lane < width, 0.0, r0), jnp.where(lane < width, r0, r1)

    def z_upper(p0, p1, width=1):
        r0, r1 = pltpu.roll(p0, 128 - width, 2), pltpu.roll(p1, 128 - width, 2)
        return jnp.where(lane >= 128 - width, r1, r0), jnp.where(lane >= 128 - width, 0.0, r1)

    def neighbour_sum(ref, half_ref, kyl, kyh, kzl, kzh, x, count, width):
        p = [plane(ref, h, x) for h in HALVES]
        zl, zh = z_lower(p[0], p[1], width), z_upper(p[0], p[1], width)
        here = [plane(half_ref, h, x) for h in HALVES]
        total = []
        for h in HALVES:
            s = plane(kyl, h, x) * y_lower(p[h], width) + plane(kyh, h, x) * y_upper(p[h], width)
            s = s + (plane(kzl, h, x) * zl[h] + plane(kzh, h, x) * zh[h])
            if x > 0:
                s = s + (here[h] + plane(half_ref, h, x - 1)) * plane(ref, h, x - 1)
            if x < count - 1:
                s = s + (here[h] + plane(half_ref, h, x + 1)) * plane(ref, h, x + 1)
            total.append(s)
        return total

    def fine_neighbours(ref, x):
        return neighbour_sum(ref, half_cond, ky_lo, ky_hi, kz_lo, kz_hi, x, NX, 1)

    def coarse_neighbours(ref, x):
        return neighbour_sum(ref, coarse_half, cky_lo, cky_hi, ckz_lo, ckz_hi, x, CX, 2)

    def coefficients(ref, kyl, kyh, kzl, kzh, diag_ref, x, count, width):
        p = [plane(ref, h, x) for h in HALVES]
        zl, zh = z_lower(p[0], p[1], width), z_upper(p[0], p[1], width)
        for h in HALVES:
            yl, yh = y_lower(p[h], width), y_upper(p[h], width)
            put(kyl, h, x, p[h] + yl)
            put(kyh, h, x, p[h] + yh)
            put(kzl, h, x, p[h] + zl[h])
            put(kzh, h, x, p[h] + zh[h])
            s = 6.0 * p[h] + ((yl + yh) + (zl[h] + zh[h]))
            if x > 0:
                s = s + plane(ref, h, x - 1)
            if x < count - 1:
                s = s + plane(ref, h, x + 1)
            put(diag_ref, h, x, s)

    def restrict(lower, upper):
        s = lower + upper
        s = s + jnp.where(even_sub2, pltpu.roll(s, 7, 0), pltpu.roll(s, 1, 0))
        s = s + jnp.where(even_lane2, pltpu.roll(s, 127, 1), pltpu.roll(s, 1, 1))
        return 0.125 * s

    def slot(face, index):
        return OFFSETS[face] + index

    def message(store, turn, face):
        return store.at[turn, pl.ds(OFFSETS[face], TURN_SIZES[turn][face])]

    def pack_x(dest, fine, coarse=None):
        for face, x in ((0, 0), (1, NX - 1)):
            for h in HALVES:
                dest[slot(face, 2 * h) : slot(face, 2 * h) + 2] = plane(fine, h, x)
        if coarse is not None:
            for face, x in ((0, 0), (1, CX - 1)):
                p = [plane(coarse, h, x) for h in HALVES]
                dest[slot(face, 4)] = jnp.where(
                    even_sub2, jnp.where(even_lane2, p[0][0], p[1][0]), jnp.where(even_lane2, p[0][1], p[1][1]))

    def pack_face_y(dest, face, fine, coarse=None):
        row = (NY - 1) * (face - 2)
        for h in HALVES:
            dest[slot(face, h)] = fine[h, pl.ds(row, NX, stride=NY), :]
            if coarse is not None:
                dest[slot(face, 2), CX * h : CX * (h + 1), :] = coarse[h, pl.ds(row, CX, stride=NY), :]

    def pack_y(dest, fine, coarse=None):
        for face in AXES[1]:
            pack_face_y(dest, face, fine, coarse)

    def pack_z(dest, fine, coarse=None):
        for face, h, source_lane in ((4, 0, 0), (5, 1, 127)):
            packed = jnp.zeros((8, 128), F32)
            for ref, count, start in ((fine, NX, 0), (coarse, CX, 16)):
                if ref is None:
                    continue
                for x in range(count):
                    p = plane(ref, h, x)
                    for t in TILES:
                        m = start + 2 * x + t
                        packed = jnp.where(lane2 == m, pltpu.roll(p[t], (m - source_lane) % 128, 1), packed)
            dest[slot(face, 0)] = packed

    def fine_z(q, half, x, t):
        lanes = 2 * x + t
        column = q[slot(4 + half, 0)][:, lanes : lanes + 1]
        return jnp.where(lane2 == 127 * half, jnp.broadcast_to(column, (8, 128)), 0.0)

    def coarse_z(q, half, x, t):
        lanes = 16 + 2 * x + t
        column = q[slot(4 + half, 0)][:, lanes : lanes + 1]
        return jnp.where(lane2 // 2 == 63 * half, jnp.broadcast_to(column, (8, 128)), 0.0)

    def fine_y(q, half, x, t):
        return jnp.where(sub2 == 7 * t, jnp.broadcast_to(q[slot(2 + t, half), x : x + 1, :], (8, 128)), 0.0)

    def coarse_y(q, half, x, t):
        row = CX * half + x
        return jnp.where(sub2 // 2 == 3 * t, jnp.broadcast_to(q[slot(2 + t, 2), row : row + 1, :], (8, 128)), 0.0)

    def fine_xz(q, half, x, t):
        added = fine_z(q, half, x, t)
        if x == 0:
            added = added + q[slot(0, 2 * half + t)]
        if x == NX - 1:
            added = added + q[slot(1, 2 * half + t)]
        return added

    def coarse_plane(q, half, face, t):
        packed = q[slot(face, 4)]
        if half == 0:
            p = jnp.where(even_lane2, packed, pltpu.roll(packed, 1, 1))
        else:
            p = jnp.where(even_lane2, pltpu.roll(packed, 127, 1), packed)
        return jnp.where(even_sub2, p, pltpu.roll(p, 1, 0)) if t == 0 else jnp.where(even_sub2, pltpu.roll(p, 7, 0), p)

    def coarse_xz(q, half, x, t):
        added = coarse_z(q, half, x, t)
        if x == 0:
            added = added + coarse_plane(q, half, 0, t)
        if x == CX - 1:
            added = added + coarse_plane(q, half, 1, t)
        return added

    def peer(face):
        name, step = FACES[face]
        return {name: place[name] + step}

    def copy(turn, face):
        return pltpu.make_async_remote_copy(
            src_ref=message(sent, turn, face),
            dst_ref=message(received, turn, face ^ 1),
            send_sem=send_sem.at[turn, face],
            recv_sem=recv_sem.at[turn, face ^ 1],
            device_id=peer(face),
            device_id_type=MESH,
        )

    def arrival(turn, face):
        return pltpu.make_async_remote_copy(
            src_ref=message(sent, turn, face),
            dst_ref=message(received, turn, face),
            send_sem=send_sem.at[turn, face],
            recv_sem=recv_sem.at[turn, face],
            device_id=peer(face),
            device_id_type=MESH,
        )

    def send(turn, faces_):
        for face in faces_:
            @pl.when(present[face])
            def _():
                copy(turn, face).start()

    def wait(turn, faces_):
        for face in faces_:
            @pl.when(present[face])
            def _():
                arrival(turn, face).wait_recv()

    def edge_copy(k, landing):
        return pltpu.make_async_remote_copy(
            src_ref=edge_sent.at[k],
            dst_ref=edge_received.at[landing],
            send_sem=edge_send_sem.at[k],
            recv_sem=edge_recv_sem.at[landing],
            device_id={**peer(EDGES[k][0]), **peer(EDGES[k][1])},
            device_id_type=MESH,
        )

    edge_present = [jnp.logical_and(present[a], present[b]) for a, b in EDGES]

    def send_edges(ks):
        for k in ks:
            a, b = EDGES[k]

            @pl.when(edge_present[k])
            def _():
                edge_copy(k, EDGES.index((a ^ 1, b ^ 1))).start()

    def wait_edges(ks):
        for k in ks:
            @pl.when(edge_present[k])
            def _():
                edge_copy(k, k).wait_recv()

    def wait_sent_edges():
        for k in range(len(EDGES)):
            @pl.when(edge_present[k])
            def _():
                edge_copy(k, k).wait_send()

    def row(ref, *index):
        return jnp.broadcast_to(ref[index[0], index[1] : index[1] + 1, :], (8, 128))

    def column(value, lane_):
        return jnp.broadcast_to(value[:, lane_ : lane_ + 1], (8, 128))

    def pack_edges(ks, turn):
        cond, update = sent.at[0], sent.at[turn]
        for k in ks:
            a, b = EDGES[k]
            if a < 2 and b < 4:
                for h in HALVES:
                    for j, ref in ((0, cond), (2, update)):
                        x, i = (NX - 1) * a, CX * h + (CX - 1) * a
                        edge_sent[k, j + h : j + h + 1, :] = ref[slot(b, h), x : x + 1, :]
                        edge_sent[k, j + h + 4 : j + h + 5, :] = ref[slot(b, 2), i : i + 1, :]
            elif a < 2:
                c, u = cond[slot(b, 0)], update[slot(b, 0)]
                fine, coarse = 2 * (NX - 1) * a, 16 + 2 * (CX - 1) * a
                packed = pltpu.roll(u, (6 - coarse) % 128, 1)
                packed = jnp.where(lane2 < 6, pltpu.roll(c, (4 - coarse) % 128, 1), packed)
                packed = jnp.where(lane2 < 4, pltpu.roll(u, (2 - fine) % 128, 1), packed)
                edge_sent[k] = jnp.where(lane2 < 2, pltpu.roll(c, (-fine) % 128, 1) if fine else c, packed)
            else:
                h, t = b - 4, a - 2
                packed = pltpu.roll(update[slot(a, 2)], (35 - 127 * h) % 128, 1)
                packed = jnp.where(lane2 < 35, pltpu.roll(cond[slot(a, 2)], (34 - 127 * h) % 128, 1), packed)
                packed = jnp.where(lane2 < 34, pltpu.roll(update[slot(a, h)], (33 - 127 * h) % 128, 1), packed)
                packed = jnp.where(lane2 < 33, pltpu.roll(cond[slot(a, h)], (32 - 127 * h) % 128, 1), packed)
                rows = jnp.where(sub2 == 0, row(cond, slot(b, 0), 7 * t), row(update, slot(b, 0), 7 * t))
                edge_sent[k] = jnp.where(lane2 < 32, rows, packed)

    def add_edges(face, sides):
        def add(index, mask, c, u):
            i = slot(face, index)
            beside[i] = beside[i] + jnp.where(mask, (received[0, i] + c) * u, 0.0)

        for side in sides:
            k = EDGES.index((min(face, side), max(face, side)))
            if face < 2 and side < 4:
                t = side - 2
                r = [row(edge_received, k, j) for j in range(8)]
                for h in HALVES:
                    add(2 * h + t, sub2 == 7 * t, r[h], r[2 + h])
                add(4, sub2 == 7 * t, jnp.where(even_lane2, r[4], r[5]), jnp.where(even_lane2, r[6], r[7]))
            elif face < 2:
                h = side - 4
                lines = edge_received[k]
                r = [column(lines, j) for j in range(8)]
                for t in TILES:
                    add(2 * h + t, lane2 == 127 * h, r[t], r[2 + t])
                add(4, lane2 == 127 * h, jnp.where(even_sub2, r[4], r[5]), jnp.where(even_sub2, r[6], r[7]))
            elif face < 4 and side < 2:
                for h in HALVES:
                    add(h, sub2 == 7 * side, row(edge_received, k, h), row(edge_received, k, 2 + h))
                    add(2, sub2 == CX * h + (CX - 1) * side, row(edge_received, k, 4 + h), row(edge_received, k, 6 + h))
            elif face < 4:
                h = side - 4
                lines = edge_received[k]
                other = pltpu.roll(lines, 4, 0)
                add(h, lane2 == 127 * h, column(lines, 32), column(lines, 33))
                add(2, jnp.logical_and(lane2 // 2 == 63 * h, sub2 // 4 == h), column(other, 34), column(other, 35))
            elif side < 2:
                lines = edge_received[k]
                for t in TILES:
                    add(0, lane2 == 14 * side + t, column(lines, t), column(lines, 2 + t))
                    add(0, lane2 == 16 + 6 * side + t, column(lines, 4 + t), column(lines, 6 + t))
            else:
                t = side - 2
                shift = 1 if t else 127
                c, u = (pltpu.roll(row(edge_received, k, j), shift, 1) for j in (0, 1))
                fine = jnp.logical_and(sub2 == 7 * t, lane2 < 16)
                coarse = jnp.logical_and(sub2 // 2 == 3 * t, jnp.logical_and(lane2 >= 16, lane2 < 24))
                add(0, jnp.logical_and(jnp.logical_or(fine, coarse), lane2 % 2 == t), c, u)

    def neighbour_field(face):
        base = OFFSETS[face]
        for i in range(base, base + BOTH[face]):
            beside[i] = FRESH * received[4, i] * beside[i]
        if face < 2:
            for h in HALVES:
                for t in TILES:
                    i = slot(face, 2 * h + t)
                    beside[i] = received[3, i] + beside[i] + coarse_plane(beside, h, face, t)
        elif face < 4:
            for h in HALVES:
                spread = row(beside, slot(face, 2), CX * h)
                for x in range(1, CX):
                    spread = jnp.where(sub2 // 2 == x, row(beside, slot(face, 2), CX * h + x), spread)
                beside[slot(face, h)] = received[3, slot(face, h)] + beside[slot(face, h)] + spread
        else:
            i = slot(face, 0)
            value = beside[i]
            spread = jnp.zeros((8, 128), F32)
            for x in range(NX):
                spread = jnp.where(lane2 // 2 == x, pltpu.roll(value, (2 * x - 16 - 2 * (x // 2)) % 128, 1), spread)
            beside[i] = received[3, i] + value + spread

    def wait_sent(turn):
        for face in range(6):
            @pl.when(present[face])
            def _():
                copy(turn, face).wait_send()

    barrier = pltpu.get_barrier_semaphore()
    for face in range(6):
        @pl.when(present[face])
        def _():
            pl.semaphore_signal(barrier, inc=1, device_id=peer(face), device_id_type=MESH)

    loads = []
    for index, (hbm, ref) in enumerate(((cond_hbm, half_cond), (field_hbm, field), (source_hbm, source))):
        pair = []
        for h in HALVES:
            load = pltpu.make_async_copy(hbm.at[:, pl.ds(128 * h, 128)], ref.at[h], in_sem.at[index, h])
            load.start()
            pair.append(load)
        loads.append(pair)

    for face in range(6):
        @pl.when(jnp.logical_not(present[face]))
        def _():
            for turn in range(TURNS):
                count = TURN_SIZES[turn][face]
                received[turn, OFFSETS[face] : OFFSETS[face] + count] = jnp.zeros((count, 8, 128), F32)

    for k in range(len(EDGES)):
        @pl.when(jnp.logical_not(edge_present[k]))
        def _():
            edge_received[k] = jnp.zeros((8, 128), F32)

    for load in loads[0]:
        load.wait()
    for x in range(NX):
        for h in HALVES:
            put(half_cond, h, x, 0.5 * plane(half_cond, h, x))
    for x in range(CX):
        for h in HALVES:
            for t in TILES:
                put_part(coarse_half, h, x, t, restrict(part(half_cond, h, 2 * x, t), part(half_cond, h, 2 * x + 1, t)))
    for pack in (pack_x, pack_y, pack_z):
        pack(sent.at[0], half_cond, coarse_half)
    pl.semaphore_wait(barrier, sum(p.astype(jnp.int32) for p in present))
    send(0, AXES[1])
    for load in loads[1]:
        load.wait()
    for axis, pack in ((1, pack_y), (0, pack_x), (2, pack_z)):
        if axis != 1:
            send(0, AXES[axis])
        pack(sent.at[1], field)
        send(1, AXES[axis])

    for x in range(NX):
        coefficients(half_cond, ky_lo, ky_hi, kz_lo, kz_hi, diag, x, NX, 1)
    for x in range(CX):
        coefficients(coarse_half, cky_lo, cky_hi, ckz_lo, ckz_hi, coarse_diag, x, CX, 2)
    for load in loads[2]:
        load.wait()

    def residual_part():
        for x in range(NX):
            total = fine_neighbours(field, x)
            for h in HALVES:
                put(partial, h, x, plane(source, h, x) - plane(diag, h, x) * plane(field, h, x) + total[h])

    residual_part()

    wait(0, (4, 5, 0, 1, 2, 3))
    for i in range(SLOTS):
        gains[i] = sent[0, i] + received[0, i]
    outside = received.at[0]
    for x in range(NX):
        for h in HALVES:
            for t in TILES:
                total = part(diag, h, x, t) + fine_xz(outside, h, x, t) + fine_y(outside, h, x, t)
                put_part(diag, h, x, t, total)
                put_part(inverse, h, x, t, 1.0 / total)
    for x in range(CX):
        for h in HALVES:
            for t in TILES:
                total = part(coarse_diag, h, x, t) + coarse_xz(outside, h, x, t) + coarse_y(outside, h, x, t)
                put_part(coarse_inverse, h, x, t, 1.0 / total)

    def add_near(ref):
        for x in range(NX):
            for h in HALVES:
                for t in TILES:
                    put_part(ref, h, x, t, part(ref, h, x, t) + fine_xz(faces, h, x, t))

    def smooth(x, t):
        for h in HALVES:
            pair = []
            for fx in (2 * x, 2 * x + 1):
                r = part(partial, h, fx, t) + fine_y(faces, h, fx, t)
                put_part(first, h, fx, t, FIRST_RATE * part(inverse, h, fx, t) * r)
                pair.append(r)
            put_part(coarse_first, h, x, t, 4.0 * FIRST_RATE * part(coarse_inverse, h, x, t) * restrict(*pair))

    def own_update():
        for x in range(CX):
            total = coarse_neighbours(coarse_first, x)
            coarse = [KEEP * plane(coarse_first, h, x) + FRESH * plane(coarse_inverse, h, x) * total[h] for h in HALVES]
            for fx in (2 * x, 2 * x + 1):
                total = fine_neighbours(first, fx)
                for h in HALVES:
                    fine = KEEP * plane(first, h, fx) + FRESH * plane(inverse, h, fx) * total[h]
                    put(partial, h, fx, plane(field, h, fx) + fine + coarse[h])

    def update_terms(turn, faces_):
        for face in faces_:
            for i in range(OFFSETS[face], OFFSETS[face] + BOTH[face]):
                faces[i] = scaled_gains[i] * received[turn, i]

    def finish(turn, last):
        wait(turn, near)
        update_terms(turn, near)
        for x in range(CX):
            for h in HALVES:
                for t in TILES:
                    coarse = coarse_xz(faces, h, x, t)
                    for fx in (2 * x, 2 * x + 1):
                        put_part(partial, h, fx, t, part(partial, h, fx, t) + coarse + fine_xz(faces, h, fx, t))
        for t in TILES:
            wait(turn, (2 + t,))
            update_terms(turn, (2 + t,))
            for x in range(CX):
                for h in HALVES:
                    coarse = coarse_y(faces, h, x, t)
                    for fx in (2 * x, 2 * x + 1):
                        value = part(partial, h, fx, t) + coarse + fine_y(faces, h, fx, t)
                        if last:
                            at = NY * fx + 8 * t
                            out[at : at + 8, 128 * h : 128 * (h + 1)] = value
                        else:
                            put_part(field, h, fx, t, value)

    near = (4, 5, 0, 1)
    every = near + (2, 3)

    def first_terms(faces_):
        for face in faces_:
            for i in range(OFFSETS[face], OFFSETS[face] + FINE[face]):
                faces[i] = gains[i] * received[1, i] - received[0, i] * sent[1, i]

    wait(1, near)
    first_terms(near)
    add_near(partial)
    for t in TILES:
        wait(1, (2 + t,))
        first_terms((2 + t,))
        for x in range(CX):
            smooth(x, t)
        pack_face_y(sent.at[2], 2 + t, first, coarse_first)
    pack_edges(range(4), 2)
    send_edges(range(4))
    pack_z(sent.at[2], first, coarse_first)
    pack_edges(range(4, 12), 2)
    send_edges((8, 9, 10, 11, 4, 5, 6, 7))
    send(2, AXES[1])
    pack_x(sent.at[2], first, coarse_first)
    send(2, near)

    own_update()
    pack_y(sent.at[3], partial)
    send(3, AXES[1])
    pack_x(sent.at[3], partial)
    send(3, AXES[0])
    pack_z(sent.at[3], partial)
    send(3, AXES[2])
    for axis, pack in ((1, pack_y), (0, pack_x), (2, pack_z)):
        pack(sent.at[4], inverse, coarse_inverse)
        send(4, AXES[axis])
    for i in range(SLOTS):
        scaled_gains[i] = FRESH * sent[4, i] * gains[i]
        beside[i] = gains[i] * sent[2, i]
    wait_sent(0)
    wait_sent(1)
    finish(2, False)
    residual_part()

    wait_edges(range(4, 12))
    for face in near:
        add_edges(face, (2, 3) if face >= 4 else (4, 5))
    for face in AXES[1]:
        add_edges(face, (4, 5))
    for face in AXES[2]:
        add_edges(face, (0, 1))
    wait(3, every)
    wait(4, every)
    def second_terms(faces_):
        for face in faces_:
            neighbour_field(face)
            for i in range(OFFSETS[face], OFFSETS[face] + FINE[face]):
                faces[i] = gains[i] * beside[i]

    second_terms(AXES[2])
    for x in range(NX):
        for h in HALVES:
            for t in TILES:
                put_part(partial, h, x, t, part(partial, h, x, t) + fine_z(faces, h, x, t))
    wait_edges(range(4))
    for face in AXES[1]:
        add_edges(face, (0, 1))
    for face in AXES[0]:
        add_edges(face, (2, 3))
    second_terms((2, 3, 0, 1))
    for face, x in ((0, 0), (1, NX - 1)):
        for h in HALVES:
            for t in TILES:
                put_part(partial, h, x, t, part(partial, h, x, t) + faces[slot(face, 2 * h + t)])
    for t in TILES:
        for x in range(CX):
            smooth(x, t)
        pack_face_y(sent.at[5], 2 + t, first, coarse_first)
        send(5, (2 + t,))
    pack_x(sent.at[5], first, coarse_first)
    send(5, AXES[0])
    pack_z(sent.at[5], first, coarse_first)
    send(5, AXES[2])
    own_update()
    for turn in (2, 3, 4):
        wait_sent(turn)
    wait_sent_edges()
    finish(5, True)
    wait_sent(TURNS - 1)


def block(source_term, conductivity, initial_field):
    def fine():
        return pltpu.VMEM((2, ROWS, 128), F32)

    def coarse():
        return pltpu.VMEM((2, CX * NY, 128), F32)

    hbm = pl.BlockSpec(memory_space=pltpu.HBM)
    result = pl.pallas_call(
        kernel,
        out_shape=pltpu.VMEM((ROWS, NZ), F32),
        in_specs=[hbm] * 3,
        out_specs=pl.BlockSpec(memory_space=pltpu.VMEM),
        scratch_shapes=[
            *(fine() for _ in range(11)),
            *(coarse() for _ in range(8)),
            *(pltpu.VMEM((SLOTS, 8, 128), F32) for _ in range(4)),
            *(pltpu.VMEM((len(EDGES), 8, 128), F32) for _ in range(2)),
            *(pltpu.VMEM((TURNS, SLOTS, 8, 128), F32) for _ in range(2)),
            pltpu.SemaphoreType.DMA((3, 2)),
            *(pltpu.SemaphoreType.DMA((TURNS, 6)) for _ in range(2)),
            *(pltpu.SemaphoreType.DMA((len(EDGES),)) for _ in range(2)),
        ],
        compiler_params=pltpu.CompilerParams(collective_id=0, has_side_effects=True),
    )(*(a.reshape(ROWS, NZ) for a in (source_term, conductivity, initial_field)))
    return result.reshape(NX, NY, NZ)


def solution(mesh):
    spec = P("gx", "gy", "grp")
    return jax.shard_map(block, mesh=mesh, in_specs=(spec,) * 3, out_specs=spec, check_vma=False)
```

```python
import functools

import jax
import jax.numpy as jnp
from jax import lax
from jax.experimental import pallas as pl
from jax.experimental.pallas import tpu as pltpu
from jax.sharding import PartitionSpec as P

MESH = pl.DeviceIdType.MESH
F32 = jnp.float32

NX, NY, NZ = 8, 16, 256
CX = NX // 2
ROWS = NX * NY
HALVES = (0, 1)
TILES = (0, 1)

FIRST_RATE = 0.8
KEEP = 60.0 / 41.0
FRESH = 40.0 / 41.0

FACES = (("gx", -1), ("gx", 1), ("gy", -1), ("gy", 1), ("grp", -1), ("grp", 1))
BOTH = (5, 5, 3, 3, 1, 1)
FINE = (4, 4, 2, 2, 1, 1)
TURN_SIZES = (BOTH, FINE, BOTH, FINE, BOTH, BOTH)
TURNS = len(TURN_SIZES)
OFFSETS = (0, 5, 10, 13, 16, 17)
SLOTS = 18
AXES = ((0, 1), (2, 3), (4, 5))
EDGES = [(a, b) for p, q in ((0, 1), (0, 2), (1, 2)) for a in AXES[p] for b in AXES[q]]


def iota(shape, dim):
    return lax.broadcasted_iota(jnp.int32, shape, dim)


def kernel(source_hbm, cond_hbm, field_hbm, out, source, half_cond, field, first, ky_lo, ky_hi, kz_lo, kz_hi,
           diag, inverse, partial, coarse_half, cky_lo, cky_hi, ckz_lo, ckz_hi, coarse_diag, coarse_inverse, coarse_first,
           faces, gains, scaled_gains, beside, edge_sent, edge_received, sent,
           received, in_sem, send_sem, recv_sem, edge_send_sem, edge_recv_sem):
    sub, lane = iota((2, 8, 128), 1), iota((2, 8, 128), 2)
    sub2, lane2 = iota((8, 128), 0), iota((8, 128), 1)
    even_sub2, even_lane2 = sub2 % 2 == 0, lane2 % 2 == 0
    zero = jnp.zeros((1, 8, 128), F32)

    place = {name: lax.axis_index(name) for name in ("grp", "gx", "gy")}
    size = {name: lax.axis_size(name) for name in ("grp", "gx", "gy")}
    present = []
    for name, step in FACES:
        present.append(place[name] > 0 if step < 0 else place[name] < size[name] - 1)

    def plane(ref, half, x):
        return ref[half, NY * x : NY * (x + 1), :].reshape(2, 8, 128)

    def put(ref, half, x, value):
        ref[half, NY * x : NY * (x + 1), :] = value.reshape(16, 128)

    def part(ref, half, x, t):
        return ref[half, NY * x + 8 * t : NY * x + 8 * t + 8, :]

    def put_part(ref, half, x, t, value):
        ref[half, NY * x + 8 * t : NY * x + 8 * t + 8, :] = value

    def y_lower(p, width=1):
        rolled = pltpu.roll(p, width, 1)
        return jnp.where(sub < width, jnp.concatenate([zero, rolled[:1]], axis=0), rolled)

    def y_upper(p, width=1):
        rolled = pltpu.roll(p, 8 - width, 1)
        return jnp.where(sub >= 8 - width, jnp.concatenate([rolled[1:], zero], axis=0), rolled)

    def z_lower(p0, p1, width=1):
        r0, r1 = pltpu.roll(p0, width, 2), pltpu.roll(p1, width, 2)
        return jnp.where(lane < width, 0.0, r0), jnp.where(lane < width, r0, r1)

    def z_upper(p0, p1, width=1):
        r0, r1 = pltpu.roll(p0, 128 - width, 2), pltpu.roll(p1, 128 - width, 2)
        return jnp.where(lane >= 128 - width, r1, r0), jnp.where(lane >= 128 - width, 0.0, r1)

    def neighbour_sum(ref, half_ref, kyl, kyh, kzl, kzh, x, count, width):
        p = [plane(ref, h, x) for h in HALVES]
        zl, zh = z_lower(p[0], p[1], width), z_upper(p[0], p[1], width)
        here = [plane(half_ref, h, x) for h in HALVES]
        total = []
        for h in HALVES:
            s = plane(kyl, h, x) * y_lower(p[h], width) + plane(kyh, h, x) * y_upper(p[h], width)
            s = s + (plane(kzl, h, x) * zl[h] + plane(kzh, h, x) * zh[h])
            if x > 0:
                s = s + (here[h] + plane(half_ref, h, x - 1)) * plane(ref, h, x - 1)
            if x < count - 1:
                s = s + (here[h] + plane(half_ref, h, x + 1)) * plane(ref, h, x + 1)
            total.append(s)
        return total

    def fine_neighbours(ref, x):
        return neighbour_sum(ref, half_cond, ky_lo, ky_hi, kz_lo, kz_hi, x, NX, 1)

    def coarse_neighbours(ref, x):
        return neighbour_sum(ref, coarse_half, cky_lo, cky_hi, ckz_lo, ckz_hi, x, CX, 2)

    def coefficients(ref, kyl, kyh, kzl, kzh, diag_ref, x, count, width):
        p = [plane(ref, h, x) for h in HALVES]
        zl, zh = z_lower(p[0], p[1], width), z_upper(p[0], p[1], width)
        for h in HALVES:
            yl, yh = y_lower(p[h], width), y_upper(p[h], width)
            put(kyl, h, x, p[h] + yl)
            put(kyh, h, x, p[h] + yh)
            put(kzl, h, x, p[h] + zl[h])
            put(kzh, h, x, p[h] + zh[h])
            s = 6.0 * p[h] + ((yl + yh) + (zl[h] + zh[h]))
            if x > 0:
                s = s + plane(ref, h, x - 1)
            if x < count - 1:
                s = s + plane(ref, h, x + 1)
            put(diag_ref, h, x, s)

    def restrict(lower, upper):
        s = lower + upper
        s = s + jnp.where(even_sub2, pltpu.roll(s, 7, 0), pltpu.roll(s, 1, 0))
        s = s + jnp.where(even_lane2, pltpu.roll(s, 127, 1), pltpu.roll(s, 1, 1))
        return 0.125 * s

    def slot(face, index):
        return OFFSETS[face] + index

    def message(store, turn, face):
        return store.at[turn, pl.ds(OFFSETS[face], TURN_SIZES[turn][face])]

    def pack_x(dest, fine, coarse=None):
        for face, x in ((0, 0), (1, NX - 1)):
            for h in HALVES:
                dest[slot(face, 2 * h) : slot(face, 2 * h) + 2] = plane(fine, h, x)
        if coarse is not None:
            for face, x in ((0, 0), (1, CX - 1)):
                p = [plane(coarse, h, x) for h in HALVES]
                dest[slot(face, 4)] = jnp.where(
                    even_sub2, jnp.where(even_lane2, p[0][0], p[1][0]), jnp.where(even_lane2, p[0][1], p[1][1]))

    def pack_face_y(dest, face, fine, coarse=None):
        row = (NY - 1) * (face - 2)
        for h in HALVES:
            dest[slot(face, h)] = fine[h, pl.ds(row, NX, stride=NY), :]
            if coarse is not None:
                dest[slot(face, 2), CX * h : CX * (h + 1), :] = coarse[h, pl.ds(row, CX, stride=NY), :]

    def pack_y(dest, fine, coarse=None):
        for face in AXES[1]:
            pack_face_y(dest, face, fine, coarse)

    def pack_z(dest, fine, coarse=None):
        for face, h, source_lane in ((4, 0, 0), (5, 1, 127)):
            packed = jnp.zeros((8, 128), F32)
            for ref, count, start in ((fine, NX, 0), (coarse, CX, 16)):
                if ref is None:
                    continue
                for x in range(count):
                    p = plane(ref, h, x)
                    for t in TILES:
                        m = start + 2 * x + t
                        packed = jnp.where(lane2 == m, pltpu.roll(p[t], (m - source_lane) % 128, 1), packed)
            dest[slot(face, 0)] = packed

    def fine_z(q, half, x, t):
        lanes = 2 * x + t
        column = q[slot(4 + half, 0)][:, lanes : lanes + 1]
        return jnp.where(lane2 == 127 * half, jnp.broadcast_to(column, (8, 128)), 0.0)

    def coarse_z(q, half, x, t):
        lanes = 16 + 2 * x + t
        column = q[slot(4 + half, 0)][:, lanes : lanes + 1]
        return jnp.where(lane2 // 2 == 63 * half, jnp.broadcast_to(column, (8, 128)), 0.0)

    def fine_y(q, half, x, t):
        return jnp.where(sub2 == 7 * t, jnp.broadcast_to(q[slot(2 + t, half), x : x + 1, :], (8, 128)), 0.0)

    def coarse_y(q, half, x, t):
        row = CX * half + x
        return jnp.where(sub2 // 2 == 3 * t, jnp.broadcast_to(q[slot(2 + t, 2), row : row + 1, :], (8, 128)), 0.0)

    def fine_xz(q, half, x, t):
        added = fine_z(q, half, x, t)
        if x == 0:
            added = added + q[slot(0, 2 * half + t)]
        if x == NX - 1:
            added = added + q[slot(1, 2 * half + t)]
        return added

    def coarse_plane(q, half, face, t):
        packed = q[slot(face, 4)]
        if half == 0:
            p = jnp.where(even_lane2, packed, pltpu.roll(packed, 1, 1))
        else:
            p = jnp.where(even_lane2, pltpu.roll(packed, 127, 1), packed)
        return jnp.where(even_sub2, p, pltpu.roll(p, 1, 0)) if t == 0 else jnp.where(even_sub2, pltpu.roll(p, 7, 0), p)

    def coarse_xz(q, half, x, t):
        added = coarse_z(q, half, x, t)
        if x == 0:
            added = added + coarse_plane(q, half, 0, t)
        if x == CX - 1:
            added = added + coarse_plane(q, half, 1, t)
        return added

    def peer(face):
        name, step = FACES[face]
        return {name: place[name] + step}

    def copy(turn, face):
        return pltpu.make_async_remote_copy(
            src_ref=message(sent, turn, face),
            dst_ref=message(received, turn, face ^ 1),
            send_sem=send_sem.at[turn, face],
            recv_sem=recv_sem.at[turn, face ^ 1],
            device_id=peer(face),
            device_id_type=MESH,
        )

    def arrival(turn, face):
        return pltpu.make_async_remote_copy(
            src_ref=message(sent, turn, face),
            dst_ref=message(received, turn, face),
            send_sem=send_sem.at[turn, face],
            recv_sem=recv_sem.at[turn, face],
            device_id=peer(face),
            device_id_type=MESH,
        )

    def send(turn, faces_):
        for face in faces_:
            @pl.when(present[face])
            def _():
                copy(turn, face).start()

    def wait(turn, faces_):
        for face in faces_:
            @pl.when(present[face])
            def _():
                arrival(turn, face).wait_recv()

    def edge_copy(k, landing):
        return pltpu.make_async_remote_copy(
            src_ref=edge_sent.at[k],
            dst_ref=edge_received.at[landing],
            send_sem=edge_send_sem.at[k],
            recv_sem=edge_recv_sem.at[landing],
            device_id={**peer(EDGES[k][0]), **peer(EDGES[k][1])},
            device_id_type=MESH,
        )

    edge_present = [jnp.logical_and(present[a], present[b]) for a, b in EDGES]

    def send_edges(ks):
        for k in ks:
            a, b = EDGES[k]

            @pl.when(edge_present[k])
            def _():
                edge_copy(k, EDGES.index((a ^ 1, b ^ 1))).start()

    def wait_edges(ks):
        for k in ks:
            @pl.when(edge_present[k])
            def _():
                edge_copy(k, k).wait_recv()

    def wait_sent_edges():
        for k in range(len(EDGES)):
            @pl.when(edge_present[k])
            def _():
                edge_copy(k, k).wait_send()

    def row(ref, *index):
        return jnp.broadcast_to(ref[index[0], index[1] : index[1] + 1, :], (8, 128))

    def column(value, lane_):
        return jnp.broadcast_to(value[:, lane_ : lane_ + 1], (8, 128))

    def pack_edges(ks, turn):
        cond, update = sent.at[0], sent.at[turn]
        for k in ks:
            a, b = EDGES[k]
            if a < 2 and b < 4:
                for h in HALVES:
                    for j, ref in ((0, cond), (2, update)):
                        x, i = (NX - 1) * a, CX * h + (CX - 1) * a
                        edge_sent[k, j + h : j + h + 1, :] = ref[slot(b, h), x : x + 1, :]
                        edge_sent[k, j + h + 4 : j + h + 5, :] = ref[slot(b, 2), i : i + 1, :]
            elif a < 2:
                c, u = cond[slot(b, 0)], update[slot(b, 0)]
                fine, coarse = 2 * (NX - 1) * a, 16 + 2 * (CX - 1) * a
                packed = pltpu.roll(u, (6 - coarse) % 128, 1)
                packed = jnp.where(lane2 < 6, pltpu.roll(c, (4 - coarse) % 128, 1), packed)
                packed = jnp.where(lane2 < 4, pltpu.roll(u, (2 - fine) % 128, 1), packed)
                edge_sent[k] = jnp.where(lane2 < 2, pltpu.roll(c, (-fine) % 128, 1) if fine else c, packed)
            else:
                h, t = b - 4, a - 2
                packed = pltpu.roll(update[slot(a, 2)], (35 - 127 * h) % 128, 1)
                packed = jnp.where(lane2 < 35, pltpu.roll(cond[slot(a, 2)], (34 - 127 * h) % 128, 1), packed)
                packed = jnp.where(lane2 < 34, pltpu.roll(update[slot(a, h)], (33 - 127 * h) % 128, 1), packed)
                packed = jnp.where(lane2 < 33, pltpu.roll(cond[slot(a, h)], (32 - 127 * h) % 128, 1), packed)
                rows = jnp.where(sub2 == 0, row(cond, slot(b, 0), 7 * t), row(update, slot(b, 0), 7 * t))
                edge_sent[k] = jnp.where(lane2 < 32, rows, packed)

    def add_edges(face, sides):
        def add(index, mask, c, u):
            i = slot(face, index)
            beside[i] = beside[i] + jnp.where(mask, (received[0, i] + c) * u, 0.0)

        for side in sides:
            k = EDGES.index((min(face, side), max(face, side)))
            if face < 2 and side < 4:
                t = side - 2
                r = [row(edge_received, k, j) for j in range(8)]
                for h in HALVES:
                    add(2 * h + t, sub2 == 7 * t, r[h], r[2 + h])
                add(4, sub2 == 7 * t, jnp.where(even_lane2, r[4], r[5]), jnp.where(even_lane2, r[6], r[7]))
            elif face < 2:
                h = side - 4
                lines = edge_received[k]
                r = [column(lines, j) for j in range(8)]
                for t in TILES:
                    add(2 * h + t, lane2 == 127 * h, r[t], r[2 + t])
                add(4, lane2 == 127 * h, jnp.where(even_sub2, r[4], r[5]), jnp.where(even_sub2, r[6], r[7]))
            elif face < 4 and side < 2:
                for h in HALVES:
                    add(h, sub2 == 7 * side, row(edge_received, k, h), row(edge_received, k, 2 + h))
                    add(2, sub2 == CX * h + (CX - 1) * side, row(edge_received, k, 4 + h), row(edge_received, k, 6 + h))
            elif face < 4:
                h = side - 4
                lines = edge_received[k]
                other = pltpu.roll(lines, 4, 0)
                add(h, lane2 == 127 * h, column(lines, 32), column(lines, 33))
                add(2, jnp.logical_and(lane2 // 2 == 63 * h, sub2 // 4 == h), column(other, 34), column(other, 35))
            elif side < 2:
                lines = edge_received[k]
                for t in TILES:
                    add(0, lane2 == 14 * side + t, column(lines, t), column(lines, 2 + t))
                    add(0, lane2 == 16 + 6 * side + t, column(lines, 4 + t), column(lines, 6 + t))
            else:
                t = side - 2
                shift = 1 if t else 127
                c, u = (pltpu.roll(row(edge_received, k, j), shift, 1) for j in (0, 1))
                fine = jnp.logical_and(sub2 == 7 * t, lane2 < 16)
                coarse = jnp.logical_and(sub2 // 2 == 3 * t, jnp.logical_and(lane2 >= 16, lane2 < 24))
                add(0, jnp.logical_and(jnp.logical_or(fine, coarse), lane2 % 2 == t), c, u)

    def neighbour_field(face):
        base = OFFSETS[face]
        for i in range(base, base + BOTH[face]):
            beside[i] = FRESH * received[4, i] * beside[i]
        if face < 2:
            for h in HALVES:
                for t in TILES:
                    i = slot(face, 2 * h + t)
                    beside[i] = received[3, i] + beside[i] + coarse_plane(beside, h, face, t)
        elif face < 4:
            for h in HALVES:
                spread = row(beside, slot(face, 2), CX * h)
                for x in range(1, CX):
                    spread = jnp.where(sub2 // 2 == x, row(beside, slot(face, 2), CX * h + x), spread)
                beside[slot(face, h)] = received[3, slot(face, h)] + beside[slot(face, h)] + spread
        else:
            i = slot(face, 0)
            value = beside[i]
            spread = jnp.zeros((8, 128), F32)
            for x in range(NX):
                spread = jnp.where(lane2 // 2 == x, pltpu.roll(value, (2 * x - 16 - 2 * (x // 2)) % 128, 1), spread)
            beside[i] = received[3, i] + value + spread

    def wait_sent(turn):
        for face in range(6):
            @pl.when(present[face])
            def _():
                copy(turn, face).wait_send()

    barrier = pltpu.get_barrier_semaphore()
    for face in range(6):
        @pl.when(present[face])
        def _():
            pl.semaphore_signal(barrier, inc=1, device_id=peer(face), device_id_type=MESH)

    loads = []
    for index, (hbm, ref) in enumerate(((cond_hbm, half_cond), (field_hbm, field), (source_hbm, source))):
        pair = []
        for h in HALVES:
            load = pltpu.make_async_copy(hbm.at[:, pl.ds(128 * h, 128)], ref.at[h], in_sem.at[index, h])
            load.start()
            pair.append(load)
        loads.append(pair)

    for face in range(6):
        @pl.when(jnp.logical_not(present[face]))
        def _():
            for turn in range(TURNS):
                count = TURN_SIZES[turn][face]
                received[turn, OFFSETS[face] : OFFSETS[face] + count] = jnp.zeros((count, 8, 128), F32)

    for k in range(len(EDGES)):
        @pl.when(jnp.logical_not(edge_present[k]))
        def _():
            edge_received[k] = jnp.zeros((8, 128), F32)

    for load in loads[0]:
        load.wait()
    for x in range(NX):
        for h in HALVES:
            put(half_cond, h, x, 0.5 * plane(half_cond, h, x))
    for x in range(CX):
        for h in HALVES:
            for t in TILES:
                put_part(coarse_half, h, x, t, restrict(part(half_cond, h, 2 * x, t), part(half_cond, h, 2 * x + 1, t)))
    for pack in (pack_x, pack_y, pack_z):
        pack(sent.at[0], half_cond, coarse_half)
    pl.semaphore_wait(barrier, sum(p.astype(jnp.int32) for p in present))
    send(0, AXES[1])
    for load in loads[1]:
        load.wait()
    for axis, pack in ((1, pack_y), (0, pack_x), (2, pack_z)):
        if axis != 1:
            send(0, AXES[axis])
        pack(sent.at[1], field)
        send(1, AXES[axis])

    for x in range(NX):
        coefficients(half_cond, ky_lo, ky_hi, kz_lo, kz_hi, diag, x, NX, 1)
    for x in range(CX):
        coefficients(coarse_half, cky_lo, cky_hi, ckz_lo, ckz_hi, coarse_diag, x, CX, 2)
    for load in loads[2]:
        load.wait()

    def residual_part():
        for x in range(NX):
            total = fine_neighbours(field, x)
            for h in HALVES:
                put(partial, h, x, plane(source, h, x) - plane(diag, h, x) * plane(field, h, x) + total[h])

    residual_part()

    wait(0, (4, 5, 0, 1, 2, 3))
    for i in range(SLOTS):
        gains[i] = sent[0, i] + received[0, i]
    outside = received.at[0]
    for x in range(NX):
        for h in HALVES:
            for t in TILES:
                total = part(diag, h, x, t) + fine_xz(outside, h, x, t) + fine_y(outside, h, x, t)
                put_part(diag, h, x, t, total)
                put_part(inverse, h, x, t, 1.0 / total)
    for x in range(CX):
        for h in HALVES:
            for t in TILES:
                total = part(coarse_diag, h, x, t) + coarse_xz(outside, h, x, t) + coarse_y(outside, h, x, t)
                put_part(coarse_inverse, h, x, t, 1.0 / total)

    def add_near(ref):
        for x in range(NX):
            for h in HALVES:
                for t in TILES:
                    put_part(ref, h, x, t, part(ref, h, x, t) + fine_xz(faces, h, x, t))

    def smooth(x, t):
        for h in HALVES:
            pair = []
            for fx in (2 * x, 2 * x + 1):
                r = part(partial, h, fx, t) + fine_y(faces, h, fx, t)
                put_part(first, h, fx, t, FIRST_RATE * part(inverse, h, fx, t) * r)
                pair.append(r)
            put_part(coarse_first, h, x, t, 4.0 * FIRST_RATE * part(coarse_inverse, h, x, t) * restrict(*pair))

    def own_update():
        for x in range(CX):
            total = coarse_neighbours(coarse_first, x)
            coarse = [KEEP * plane(coarse_first, h, x) + FRESH * plane(coarse_inverse, h, x) * total[h] for h in HALVES]
            for fx in (2 * x, 2 * x + 1):
                total = fine_neighbours(first, fx)
                for h in HALVES:
                    fine = KEEP * plane(first, h, fx) + FRESH * plane(inverse, h, fx) * total[h]
                    put(partial, h, fx, plane(field, h, fx) + fine + coarse[h])

    def update_terms(turn, faces_):
        for face in faces_:
            for i in range(OFFSETS[face], OFFSETS[face] + BOTH[face]):
                faces[i] = scaled_gains[i] * received[turn, i]

    def finish(turn, last):
        wait(turn, near)
        update_terms(turn, near)
        for x in range(CX):
            for h in HALVES:
                for t in TILES:
                    coarse = coarse_xz(faces, h, x, t)
                    for fx in (2 * x, 2 * x + 1):
                        put_part(partial, h, fx, t, part(partial, h, fx, t) + coarse + fine_xz(faces, h, fx, t))
        for t in TILES:
            wait(turn, (2 + t,))
            update_terms(turn, (2 + t,))
            for x in range(CX):
                for h in HALVES:
                    coarse = coarse_y(faces, h, x, t)
                    for fx in (2 * x, 2 * x + 1):
                        value = part(partial, h, fx, t) + coarse + fine_y(faces, h, fx, t)
                        if last:
                            at = NY * fx + 8 * t
                            out[at : at + 8, 128 * h : 128 * (h + 1)] = value
                        else:
                            put_part(field, h, fx, t, value)

    near = (4, 5, 0, 1)
    every = near + (2, 3)

    def first_terms(faces_):
        for face in faces_:
            for i in range(OFFSETS[face], OFFSETS[face] + FINE[face]):
                faces[i] = gains[i] * received[1, i] - received[0, i] * sent[1, i]

    for axis, pack in ((1, pack_y), (0, pack_x)):
        pack(sent.at[4], inverse, coarse_inverse)
        send(4, AXES[axis])
    wait(1, near)
    first_terms(near)
    add_near(partial)
    for t in TILES:
        wait(1, (2 + t,))
        first_terms((2 + t,))
        for x in range(CX):
            smooth(x, t)
        pack_face_y(sent.at[2], 2 + t, first, coarse_first)
    pack_edges(range(4), 2)
    send_edges(range(4))
    pack_z(sent.at[2], first, coarse_first)
    pack_edges(range(4, 12), 2)
    send_edges((8, 9, 10, 11, 4, 5, 6, 7))
    send(2, AXES[1])
    pack_x(sent.at[2], first, coarse_first)
    send(2, near)

    own_update()
    pack_y(sent.at[3], partial)
    send(3, AXES[1])
    pack_x(sent.at[3], partial)
    send(3, AXES[0])
    pack_z(sent.at[3], partial)
    send(3, AXES[2])
    pack_z(sent.at[4], inverse, coarse_inverse)
    send(4, AXES[2])
    for i in range(SLOTS):
        scaled_gains[i] = FRESH * sent[4, i] * gains[i]
        beside[i] = gains[i] * sent[2, i]
    wait_sent(0)
    wait_sent(1)
    finish(2, False)
    residual_part()

    wait_edges(range(4, 12))
    for face in near:
        add_edges(face, (2, 3) if face >= 4 else (4, 5))
    for face in AXES[1]:
        add_edges(face, (4, 5))
    for face in AXES[2]:
        add_edges(face, (0, 1))
    wait(3, every)
    wait(4, every)
    def second_terms(faces_):
        for face in faces_:
            neighbour_field(face)
            for i in range(OFFSETS[face], OFFSETS[face] + FINE[face]):
                faces[i] = gains[i] * beside[i]

    second_terms(AXES[2])
    for x in range(NX):
        for h in HALVES:
            for t in TILES:
                put_part(partial, h, x, t, part(partial, h, x, t) + fine_z(faces, h, x, t))
    wait_edges(range(4))
    for face in AXES[1]:
        add_edges(face, (0, 1))
    for face in AXES[0]:
        add_edges(face, (2, 3))
    second_terms((2, 3, 0, 1))
    for face, x in ((0, 0), (1, NX - 1)):
        for h in HALVES:
            for t in TILES:
                put_part(partial, h, x, t, part(partial, h, x, t) + faces[slot(face, 2 * h + t)])
    for t in TILES:
        for x in range(CX):
            smooth(x, t)
        pack_face_y(sent.at[5], 2 + t, first, coarse_first)
        send(5, (2 + t,))
    pack_x(sent.at[5], first, coarse_first)
    send(5, AXES[0])
    pack_z(sent.at[5], first, coarse_first)
    send(5, AXES[2])
    own_update()
    for turn in (2, 3, 4):
        wait_sent(turn)
    wait_sent_edges()
    finish(5, True)
    wait_sent(TURNS - 1)


def block(source_term, conductivity, initial_field):
    def fine():
        return pltpu.VMEM((2, ROWS, 128), F32)

    def coarse():
        return pltpu.VMEM((2, CX * NY, 128), F32)

    hbm = pl.BlockSpec(memory_space=pltpu.HBM)
    result = pl.pallas_call(
        kernel,
        out_shape=pltpu.VMEM((ROWS, NZ), F32),
        in_specs=[hbm] * 3,
        out_specs=pl.BlockSpec(memory_space=pltpu.VMEM),
        scratch_shapes=[
            *(fine() for _ in range(11)),
            *(coarse() for _ in range(8)),
            *(pltpu.VMEM((SLOTS, 8, 128), F32) for _ in range(4)),
            *(pltpu.VMEM((len(EDGES), 8, 128), F32) for _ in range(2)),
            *(pltpu.VMEM((TURNS, SLOTS, 8, 128), F32) for _ in range(2)),
            pltpu.SemaphoreType.DMA((3, 2)),
            *(pltpu.SemaphoreType.DMA((TURNS, 6)) for _ in range(2)),
            *(pltpu.SemaphoreType.DMA((len(EDGES),)) for _ in range(2)),
        ],
        compiler_params=pltpu.CompilerParams(collective_id=0, has_side_effects=True),
    )(*(a.reshape(ROWS, NZ) for a in (source_term, conductivity, initial_field)))
    return result.reshape(NX, NY, NZ)


def solution(mesh):
    spec = P("gx", "gy", "grp")
    return jax.shard_map(block, mesh=mesh, in_specs=(spec,) * 3, out_specs=spec, check_vma=False)
```

```python
import functools

import jax
import jax.numpy as jnp
from jax import lax
from jax.experimental import pallas as pl
from jax.experimental.pallas import tpu as pltpu
from jax.sharding import PartitionSpec as P

MESH = pl.DeviceIdType.MESH
F32 = jnp.float32

NX, NY, NZ = 8, 16, 256
CX = NX // 2
ROWS = NX * NY
HALVES = (0, 1)
TILES = (0, 1)

FIRST_RATE = 0.8
KEEP = 60.0 / 41.0
FRESH = 40.0 / 41.0

FACES = (("gx", -1), ("gx", 1), ("gy", -1), ("gy", 1), ("grp", -1), ("grp", 1))
BOTH = (5, 5, 3, 3, 1, 1)
FINE = (4, 4, 2, 2, 1, 1)
TURN_SIZES = (BOTH, FINE, BOTH, FINE, BOTH, BOTH)
TURNS = len(TURN_SIZES)
OFFSETS = (0, 5, 10, 13, 16, 17)
SLOTS = 18
AXES = ((0, 1), (2, 3), (4, 5))
EDGES = [(a, b) for p, q in ((0, 1), (0, 2), (1, 2)) for a in AXES[p] for b in AXES[q]]


def iota(shape, dim):
    return lax.broadcasted_iota(jnp.int32, shape, dim)


def kernel(source_hbm, cond_hbm, field_hbm, out, source, half_cond, field, first, ky_lo, ky_hi, kz_lo, kz_hi,
           diag, inverse, partial, coarse_half, cky_lo, cky_hi, ckz_lo, ckz_hi, coarse_diag, coarse_inverse, coarse_first,
           faces, gains, scaled_gains, beside, edge_sent, edge_received, sent,
           received, in_sem, send_sem, recv_sem, edge_send_sem, edge_recv_sem):
    sub, lane = iota((2, 8, 128), 1), iota((2, 8, 128), 2)
    sub2, lane2 = iota((8, 128), 0), iota((8, 128), 1)
    even_sub2, even_lane2 = sub2 % 2 == 0, lane2 % 2 == 0
    zero = jnp.zeros((1, 8, 128), F32)

    place = {name: lax.axis_index(name) for name in ("grp", "gx", "gy")}
    size = {name: lax.axis_size(name) for name in ("grp", "gx", "gy")}
    present = []
    for name, step in FACES:
        present.append(place[name] > 0 if step < 0 else place[name] < size[name] - 1)

    def plane(ref, half, x):
        return ref[half, NY * x : NY * (x + 1), :].reshape(2, 8, 128)

    def put(ref, half, x, value):
        ref[half, NY * x : NY * (x + 1), :] = value.reshape(16, 128)

    def part(ref, half, x, t):
        return ref[half, NY * x + 8 * t : NY * x + 8 * t + 8, :]

    def put_part(ref, half, x, t, value):
        ref[half, NY * x + 8 * t : NY * x + 8 * t + 8, :] = value

    def y_lower(p, width=1):
        rolled = pltpu.roll(p, width, 1)
        return jnp.where(sub < width, jnp.concatenate([zero, rolled[:1]], axis=0), rolled)

    def y_upper(p, width=1):
        rolled = pltpu.roll(p, 8 - width, 1)
        return jnp.where(sub >= 8 - width, jnp.concatenate([rolled[1:], zero], axis=0), rolled)

    def z_lower(p0, p1, width=1):
        r0, r1 = pltpu.roll(p0, width, 2), pltpu.roll(p1, width, 2)
        return jnp.where(lane < width, 0.0, r0), jnp.where(lane < width, r0, r1)

    def z_upper(p0, p1, width=1):
        r0, r1 = pltpu.roll(p0, 128 - width, 2), pltpu.roll(p1, 128 - width, 2)
        return jnp.where(lane >= 128 - width, r1, r0), jnp.where(lane >= 128 - width, 0.0, r1)

    def neighbour_sum(ref, half_ref, kyl, kyh, kzl, kzh, x, count, width):
        p = [plane(ref, h, x) for h in HALVES]
        zl, zh = z_lower(p[0], p[1], width), z_upper(p[0], p[1], width)
        here = [plane(half_ref, h, x) for h in HALVES]
        total = []
        for h in HALVES:
            s = plane(kyl, h, x) * y_lower(p[h], width) + plane(kyh, h, x) * y_upper(p[h], width)
            s = s + (plane(kzl, h, x) * zl[h] + plane(kzh, h, x) * zh[h])
            if x > 0:
                s = s + (here[h] + plane(half_ref, h, x - 1)) * plane(ref, h, x - 1)
            if x < count - 1:
                s = s + (here[h] + plane(half_ref, h, x + 1)) * plane(ref, h, x + 1)
            total.append(s)
        return total

    def fine_neighbours(ref, x):
        return neighbour_sum(ref, half_cond, ky_lo, ky_hi, kz_lo, kz_hi, x, NX, 1)

    def coarse_neighbours(ref, x):
        return neighbour_sum(ref, coarse_half, cky_lo, cky_hi, ckz_lo, ckz_hi, x, CX, 2)

    def coefficients(ref, kyl, kyh, kzl, kzh, diag_ref, x, count, width):
        p = [plane(ref, h, x) for h in HALVES]
        zl, zh = z_lower(p[0], p[1], width), z_upper(p[0], p[1], width)
        for h in HALVES:
            yl, yh = y_lower(p[h], width), y_upper(p[h], width)
            put(kyl, h, x, p[h] + yl)
            put(kyh, h, x, p[h] + yh)
            put(kzl, h, x, p[h] + zl[h])
            put(kzh, h, x, p[h] + zh[h])
            s = 6.0 * p[h] + ((yl + yh) + (zl[h] + zh[h]))
            if x > 0:
                s = s + plane(ref, h, x - 1)
            if x < count - 1:
                s = s + plane(ref, h, x + 1)
            put(diag_ref, h, x, s)

    def restrict(lower, upper):
        s = lower + upper
        s = s + jnp.where(even_sub2, pltpu.roll(s, 7, 0), pltpu.roll(s, 1, 0))
        s = s + jnp.where(even_lane2, pltpu.roll(s, 127, 1), pltpu.roll(s, 1, 1))
        return 0.125 * s

    def slot(face, index):
        return OFFSETS[face] + index

    def message(store, turn, face):
        return store.at[turn, pl.ds(OFFSETS[face], TURN_SIZES[turn][face])]

    def pack_x(dest, fine, coarse=None):
        for face, x in ((0, 0), (1, NX - 1)):
            for h in HALVES:
                dest[slot(face, 2 * h) : slot(face, 2 * h) + 2] = plane(fine, h, x)
        if coarse is not None:
            for face, x in ((0, 0), (1, CX - 1)):
                p = [plane(coarse, h, x) for h in HALVES]
                dest[slot(face, 4)] = jnp.where(
                    even_sub2, jnp.where(even_lane2, p[0][0], p[1][0]), jnp.where(even_lane2, p[0][1], p[1][1]))

    def pack_face_y(dest, face, fine, coarse=None):
        row = (NY - 1) * (face - 2)
        for h in HALVES:
            dest[slot(face, h)] = fine[h, pl.ds(row, NX, stride=NY), :]
            if coarse is not None:
                dest[slot(face, 2), CX * h : CX * (h + 1), :] = coarse[h, pl.ds(row, CX, stride=NY), :]

    def pack_y(dest, fine, coarse=None):
        for face in AXES[1]:
            pack_face_y(dest, face, fine, coarse)

    def pack_z(dest, fine, coarse=None):
        for face, h, source_lane in ((4, 0, 0), (5, 1, 127)):
            packed = jnp.zeros((8, 128), F32)
            for ref, count, start in ((fine, NX, 0), (coarse, CX, 16)):
                if ref is None:
                    continue
                for x in range(count):
                    p = plane(ref, h, x)
                    for t in TILES:
                        m = start + 2 * x + t
                        packed = jnp.where(lane2 == m, pltpu.roll(p[t], (m - source_lane) % 128, 1), packed)
            dest[slot(face, 0)] = packed

    def fine_z(q, half, x, t):
        lanes = 2 * x + t
        column = q[slot(4 + half, 0)][:, lanes : lanes + 1]
        return jnp.where(lane2 == 127 * half, jnp.broadcast_to(column, (8, 128)), 0.0)

    def coarse_z(q, half, x, t):
        lanes = 16 + 2 * x + t
        column = q[slot(4 + half, 0)][:, lanes : lanes + 1]
        return jnp.where(lane2 // 2 == 63 * half, jnp.broadcast_to(column, (8, 128)), 0.0)

    def fine_y(q, half, x, t):
        return jnp.where(sub2 == 7 * t, jnp.broadcast_to(q[slot(2 + t, half), x : x + 1, :], (8, 128)), 0.0)

    def coarse_y(q, half, x, t):
        row = CX * half + x
        return jnp.where(sub2 // 2 == 3 * t, jnp.broadcast_to(q[slot(2 + t, 2), row : row + 1, :], (8, 128)), 0.0)

    def fine_xz(q, half, x, t):
        added = fine_z(q, half, x, t)
        if x == 0:
            added = added + q[slot(0, 2 * half + t)]
        if x == NX - 1:
            added = added + q[slot(1, 2 * half + t)]
        return added

    def coarse_plane(q, half, face, t):
        packed = q[slot(face, 4)]
        if half == 0:
            p = jnp.where(even_lane2, packed, pltpu.roll(packed, 1, 1))
        else:
            p = jnp.where(even_lane2, pltpu.roll(packed, 127, 1), packed)
        return jnp.where(even_sub2, p, pltpu.roll(p, 1, 0)) if t == 0 else jnp.where(even_sub2, pltpu.roll(p, 7, 0), p)

    def coarse_xz(q, half, x, t):
        added = coarse_z(q, half, x, t)
        if x == 0:
            added = added + coarse_plane(q, half, 0, t)
        if x == CX - 1:
            added = added + coarse_plane(q, half, 1, t)
        return added

    def peer(face):
        name, step = FACES[face]
        return {name: place[name] + step}

    def copy(turn, face):
        return pltpu.make_async_remote_copy(
            src_ref=message(sent, turn, face),
            dst_ref=message(received, turn, face ^ 1),
            send_sem=send_sem.at[turn, face],
            recv_sem=recv_sem.at[turn, face ^ 1],
            device_id=peer(face),
            device_id_type=MESH,
        )

    def arrival(turn, face):
        return pltpu.make_async_remote_copy(
            src_ref=message(sent, turn, face),
            dst_ref=message(received, turn, face),
            send_sem=send_sem.at[turn, face],
            recv_sem=recv_sem.at[turn, face],
            device_id=peer(face),
            device_id_type=MESH,
        )

    def send(turn, faces_):
        for face in faces_:
            @pl.when(present[face])
            def _():
                copy(turn, face).start()

    def wait(turn, faces_):
        for face in faces_:
            @pl.when(present[face])
            def _():
                arrival(turn, face).wait_recv()

    def edge_copy(k, landing):
        return pltpu.make_async_remote_copy(
            src_ref=edge_sent.at[k],
            dst_ref=edge_received.at[landing],
            send_sem=edge_send_sem.at[k],
            recv_sem=edge_recv_sem.at[landing],
            device_id={**peer(EDGES[k][0]), **peer(EDGES[k][1])},
            device_id_type=MESH,
        )

    edge_present = [jnp.logical_and(present[a], present[b]) for a, b in EDGES]

    def send_edges(ks):
        for k in ks:
            a, b = EDGES[k]

            @pl.when(edge_present[k])
            def _():
                edge_copy(k, EDGES.index((a ^ 1, b ^ 1))).start()

    def wait_edges(ks):
        for k in ks:
            @pl.when(edge_present[k])
            def _():
                edge_copy(k, k).wait_recv()

    def wait_sent_edges():
        for k in range(len(EDGES)):
            @pl.when(edge_present[k])
            def _():
                edge_copy(k, k).wait_send()

    def row(ref, *index):
        return jnp.broadcast_to(ref[index[0], index[1] : index[1] + 1, :], (8, 128))

    def column(value, lane_):
        return jnp.broadcast_to(value[:, lane_ : lane_ + 1], (8, 128))

    def pack_edges(ks, turn):
        cond, update = sent.at[0], sent.at[turn]
        for k in ks:
            a, b = EDGES[k]
            if a < 2 and b < 4:
                for h in HALVES:
                    for j, ref in ((0, cond), (2, update)):
                        x, i = (NX - 1) * a, CX * h + (CX - 1) * a
                        edge_sent[k, j + h : j + h + 1, :] = ref[slot(b, h), x : x + 1, :]
                        edge_sent[k, j + h + 4 : j + h + 5, :] = ref[slot(b, 2), i : i + 1, :]
            elif a < 2:
                c, u = cond[slot(b, 0)], update[slot(b, 0)]
                fine, coarse = 2 * (NX - 1) * a, 16 + 2 * (CX - 1) * a
                packed = pltpu.roll(u, (6 - coarse) % 128, 1)
                packed = jnp.where(lane2 < 6, pltpu.roll(c, (4 - coarse) % 128, 1), packed)
                packed = jnp.where(lane2 < 4, pltpu.roll(u, (2 - fine) % 128, 1), packed)
                edge_sent[k] = jnp.where(lane2 < 2, pltpu.roll(c, (-fine) % 128, 1) if fine else c, packed)
            else:
                h, t = b - 4, a - 2
                packed = pltpu.roll(update[slot(a, 2)], (35 - 127 * h) % 128, 1)
                packed = jnp.where(lane2 < 35, pltpu.roll(cond[slot(a, 2)], (34 - 127 * h) % 128, 1), packed)
                packed = jnp.where(lane2 < 34, pltpu.roll(update[slot(a, h)], (33 - 127 * h) % 128, 1), packed)
                packed = jnp.where(lane2 < 33, pltpu.roll(cond[slot(a, h)], (32 - 127 * h) % 128, 1), packed)
                rows = jnp.where(sub2 == 0, row(cond, slot(b, 0), 7 * t), row(update, slot(b, 0), 7 * t))
                edge_sent[k] = jnp.where(lane2 < 32, rows, packed)

    def add_edges(face, sides):
        def add(index, mask, c, u):
            i = slot(face, index)
            beside[i] = beside[i] + jnp.where(mask, (received[0, i] + c) * u, 0.0)

        for side in sides:
            k = EDGES.index((min(face, side), max(face, side)))
            if face < 2 and side < 4:
                t = side - 2
                r = [row(edge_received, k, j) for j in range(8)]
                for h in HALVES:
                    add(2 * h + t, sub2 == 7 * t, r[h], r[2 + h])
                add(4, sub2 == 7 * t, jnp.where(even_lane2, r[4], r[5]), jnp.where(even_lane2, r[6], r[7]))
            elif face < 2:
                h = side - 4
                lines = edge_received[k]
                r = [column(lines, j) for j in range(8)]
                for t in TILES:
                    add(2 * h + t, lane2 == 127 * h, r[t], r[2 + t])
                add(4, lane2 == 127 * h, jnp.where(even_sub2, r[4], r[5]), jnp.where(even_sub2, r[6], r[7]))
            elif face < 4 and side < 2:
                for h in HALVES:
                    add(h, sub2 == 7 * side, row(edge_received, k, h), row(edge_received, k, 2 + h))
                    add(2, sub2 == CX * h + (CX - 1) * side, row(edge_received, k, 4 + h), row(edge_received, k, 6 + h))
            elif face < 4:
                h = side - 4
                lines = edge_received[k]
                other = pltpu.roll(lines, 4, 0)
                add(h, lane2 == 127 * h, column(lines, 32), column(lines, 33))
                add(2, jnp.logical_and(lane2 // 2 == 63 * h, sub2 // 4 == h), column(other, 34), column(other, 35))
            elif side < 2:
                lines = edge_received[k]
                for t in TILES:
                    add(0, lane2 == 14 * side + t, column(lines, t), column(lines, 2 + t))
                    add(0, lane2 == 16 + 6 * side + t, column(lines, 4 + t), column(lines, 6 + t))
            else:
                t = side - 2
                shift = 1 if t else 127
                c, u = (pltpu.roll(row(edge_received, k, j), shift, 1) for j in (0, 1))
                fine = jnp.logical_and(sub2 == 7 * t, lane2 < 16)
                coarse = jnp.logical_and(sub2 // 2 == 3 * t, jnp.logical_and(lane2 >= 16, lane2 < 24))
                add(0, jnp.logical_and(jnp.logical_or(fine, coarse), lane2 % 2 == t), c, u)

    def neighbour_field(face):
        base = OFFSETS[face]
        for i in range(base, base + BOTH[face]):
            beside[i] = FRESH * received[4, i] * beside[i]
        if face < 2:
            for h in HALVES:
                for t in TILES:
                    i = slot(face, 2 * h + t)
                    beside[i] = received[3, i] + beside[i] + coarse_plane(beside, h, face, t)
        elif face < 4:
            for h in HALVES:
                spread = row(beside, slot(face, 2), CX * h)
                for x in range(1, CX):
                    spread = jnp.where(sub2 // 2 == x, row(beside, slot(face, 2), CX * h + x), spread)
                beside[slot(face, h)] = received[3, slot(face, h)] + beside[slot(face, h)] + spread
        else:
            i = slot(face, 0)
            value = beside[i]
            spread = jnp.zeros((8, 128), F32)
            for x in range(NX):
                spread = jnp.where(lane2 // 2 == x, pltpu.roll(value, (2 * x - 16 - 2 * (x // 2)) % 128, 1), spread)
            beside[i] = received[3, i] + value + spread

    def wait_sent(turn):
        for face in range(6):
            @pl.when(present[face])
            def _():
                copy(turn, face).wait_send()

    barrier = pltpu.get_barrier_semaphore()
    for face in (3, 2, 1, 0, 5, 4):
        @pl.when(present[face])
        def _():
            pl.semaphore_signal(barrier, inc=1, device_id=peer(face), device_id_type=MESH)

    loads = []
    for index, (hbm, ref) in enumerate(((cond_hbm, half_cond), (field_hbm, field), (source_hbm, source))):
        pair = []
        for h in HALVES:
            load = pltpu.make_async_copy(hbm.at[:, pl.ds(128 * h, 128)], ref.at[h], in_sem.at[index, h])
            load.start()
            pair.append(load)
        loads.append(pair)

    for face in range(6):
        @pl.when(jnp.logical_not(present[face]))
        def _():
            for turn in range(TURNS):
                count = TURN_SIZES[turn][face]
                received[turn, OFFSETS[face] : OFFSETS[face] + count] = jnp.zeros((count, 8, 128), F32)

    for k in range(len(EDGES)):
        @pl.when(jnp.logical_not(edge_present[k]))
        def _():
            edge_received[k] = jnp.zeros((8, 128), F32)

    for load in loads[0]:
        load.wait()
    for x in range(NX):
        for h in HALVES:
            put(half_cond, h, x, 0.5 * plane(half_cond, h, x))
    for x in range(CX):
        for h in HALVES:
            for t in TILES:
                put_part(coarse_half, h, x, t, restrict(part(half_cond, h, 2 * x, t), part(half_cond, h, 2 * x + 1, t)))
    for pack in (pack_y, pack_x):
        pack(sent.at[0], half_cond, coarse_half)
    pl.semaphore_wait(barrier, sum(p.astype(jnp.int32) for p in present))
    send(0, AXES[1])
    for load in loads[1]:
        load.wait()
    for axis, pack in ((1, pack_y), (0, pack_x), (2, pack_z)):
        if axis == 2:
            pack(sent.at[0], half_cond, coarse_half)
        if axis != 1:
            send(0, AXES[axis])
        pack(sent.at[1], field)
        send(1, AXES[axis])

    for x in range(NX):
        coefficients(half_cond, ky_lo, ky_hi, kz_lo, kz_hi, diag, x, NX, 1)
    for x in range(CX):
        coefficients(coarse_half, cky_lo, cky_hi, ckz_lo, ckz_hi, coarse_diag, x, CX, 2)
    for load in loads[2]:
        load.wait()

    def residual_part():
        for x in range(NX):
            total = fine_neighbours(field, x)
            for h in HALVES:
                put(partial, h, x, plane(source, h, x) - plane(diag, h, x) * plane(field, h, x) + total[h])

    residual_part()

    wait(0, (4, 5, 0, 1, 2, 3))
    for i in range(SLOTS):
        gains[i] = sent[0, i] + received[0, i]
    outside = received.at[0]
    for x in range(NX):
        for h in HALVES:
            for t in TILES:
                total = part(diag, h, x, t) + fine_xz(outside, h, x, t) + fine_y(outside, h, x, t)
                put_part(diag, h, x, t, total)
                put_part(inverse, h, x, t, 1.0 / total)
    for x in range(CX):
        for h in HALVES:
            for t in TILES:
                total = part(coarse_diag, h, x, t) + coarse_xz(outside, h, x, t) + coarse_y(outside, h, x, t)
                put_part(coarse_inverse, h, x, t, 1.0 / total)

    def add_near(ref):
        for x in range(NX):
            for h in HALVES:
                for t in TILES:
                    put_part(ref, h, x, t, part(ref, h, x, t) + fine_xz(faces, h, x, t))

    def smooth(x, t):
        for h in HALVES:
            pair = []
            for fx in (2 * x, 2 * x + 1):
                r = part(partial, h, fx, t) + fine_y(faces, h, fx, t)
                put_part(first, h, fx, t, FIRST_RATE * part(inverse, h, fx, t) * r)
                pair.append(r)
            put_part(coarse_first, h, x, t, 4.0 * FIRST_RATE * part(coarse_inverse, h, x, t) * restrict(*pair))

    def own_update():
        for x in range(CX):
            total = coarse_neighbours(coarse_first, x)
            coarse = [KEEP * plane(coarse_first, h, x) + FRESH * plane(coarse_inverse, h, x) * total[h] for h in HALVES]
            for fx in (2 * x, 2 * x + 1):
                total = fine_neighbours(first, fx)
                for h in HALVES:
                    fine = KEEP * plane(first, h, fx) + FRESH * plane(inverse, h, fx) * total[h]
                    put(partial, h, fx, plane(field, h, fx) + fine + coarse[h])

    def update_terms(turn, faces_):
        for face in faces_:
            for i in range(OFFSETS[face], OFFSETS[face] + BOTH[face]):
                faces[i] = scaled_gains[i] * received[turn, i]

    def finish(turn, last):
        wait(turn, near)
        update_terms(turn, near)
        for x in range(CX):
            for h in HALVES:
                for t in TILES:
                    coarse = coarse_xz(faces, h, x, t)
                    for fx in (2 * x, 2 * x + 1):
                        put_part(partial, h, fx, t, part(partial, h, fx, t) + coarse + fine_xz(faces, h, fx, t))
        for t in TILES:
            wait(turn, (2 + t,))
            update_terms(turn, (2 + t,))
            for x in range(CX):
                for h in HALVES:
                    coarse = coarse_y(faces, h, x, t)
                    for fx in (2 * x, 2 * x + 1):
                        value = part(partial, h, fx, t) + coarse + fine_y(faces, h, fx, t)
                        if last:
                            at = NY * fx + 8 * t
                            out[at : at + 8, 128 * h : 128 * (h + 1)] = value
                        else:
                            put_part(field, h, fx, t, value)

    near = (4, 5, 0, 1)
    every = near + (2, 3)

    def first_terms(faces_):
        for face in faces_:
            for i in range(OFFSETS[face], OFFSETS[face] + FINE[face]):
                faces[i] = gains[i] * received[1, i] - received[0, i] * sent[1, i]

    for axis, pack in ((1, pack_y), (0, pack_x)):
        pack(sent.at[4], inverse, coarse_inverse)
        send(4, AXES[axis])
    wait(1, near)
    first_terms(near)
    add_near(partial)
    for t in TILES:
        wait(1, (2 + t,))
        first_terms((2 + t,))
        for x in range(CX):
            smooth(x, t)
        pack_face_y(sent.at[2], 2 + t, first, coarse_first)
    pack_edges(range(4), 2)
    send_edges(range(4))
    pack_z(sent.at[2], first, coarse_first)
    pack_edges(range(4, 12), 2)
    send_edges((8, 9, 10, 11, 4, 5, 6, 7))
    send(2, AXES[1])
    pack_x(sent.at[2], first, coarse_first)
    send(2, near)

    own_update()
    pack_y(sent.at[3], partial)
    send(3, AXES[1])
    pack_x(sent.at[3], partial)
    send(3, AXES[0])
    pack_z(sent.at[3], partial)
    send(3, AXES[2])
    pack_z(sent.at[4], inverse, coarse_inverse)
    send(4, AXES[2])
    for i in range(SLOTS):
        scaled_gains[i] = FRESH * sent[4, i] * gains[i]
        beside[i] = gains[i] * sent[2, i]
    wait_sent(0)
    wait_sent(1)
    finish(2, False)
    residual_part()

    wait_edges(range(4, 12))
    for face in near:
        add_edges(face, (2, 3) if face >= 4 else (4, 5))
    for face in AXES[1]:
        add_edges(face, (4, 5))
    for face in AXES[2]:
        add_edges(face, (0, 1))
    wait(3, every)
    wait(4, every)
    def second_terms(faces_):
        for face in faces_:
            neighbour_field(face)
            for i in range(OFFSETS[face], OFFSETS[face] + FINE[face]):
                faces[i] = gains[i] * beside[i]

    second_terms(AXES[2])
    for x in range(NX):
        for h in HALVES:
            for t in TILES:
                put_part(partial, h, x, t, part(partial, h, x, t) + fine_z(faces, h, x, t))
    wait_edges(range(4))
    for face in AXES[1]:
        add_edges(face, (0, 1))
    for face in AXES[0]:
        add_edges(face, (2, 3))
    second_terms((2, 3, 0, 1))
    for face, x in ((0, 0), (1, NX - 1)):
        for h in HALVES:
            for t in TILES:
                put_part(partial, h, x, t, part(partial, h, x, t) + faces[slot(face, 2 * h + t)])
    for t in TILES:
        for x in range(CX):
            smooth(x, t)
        pack_face_y(sent.at[5], 2 + t, first, coarse_first)
        send(5, (2 + t,))
    pack_x(sent.at[5], first, coarse_first)
    send(5, AXES[0])
    pack_z(sent.at[5], first, coarse_first)
    send(5, AXES[2])
    own_update()
    for turn in (2, 3, 4):
        wait_sent(turn)
    wait_sent_edges()
    finish(5, True)
    wait_sent(TURNS - 1)


def block(source_term, conductivity, initial_field):
    def fine():
        return pltpu.VMEM((2, ROWS, 128), F32)

    def coarse():
        return pltpu.VMEM((2, CX * NY, 128), F32)

    hbm = pl.BlockSpec(memory_space=pltpu.HBM)
    result = pl.pallas_call(
        kernel,
        out_shape=pltpu.VMEM((ROWS, NZ), F32),
        in_specs=[hbm] * 3,
        out_specs=pl.BlockSpec(memory_space=pltpu.VMEM),
        scratch_shapes=[
            *(fine() for _ in range(11)),
            *(coarse() for _ in range(8)),
            *(pltpu.VMEM((SLOTS, 8, 128), F32) for _ in range(4)),
            *(pltpu.VMEM((len(EDGES), 8, 128), F32) for _ in range(2)),
            *(pltpu.VMEM((TURNS, SLOTS, 8, 128), F32) for _ in range(2)),
            pltpu.SemaphoreType.DMA((3, 2)),
            *(pltpu.SemaphoreType.DMA((TURNS, 6)) for _ in range(2)),
            *(pltpu.SemaphoreType.DMA((len(EDGES),)) for _ in range(2)),
        ],
        compiler_params=pltpu.CompilerParams(collective_id=0, has_side_effects=True),
    )(*(a.reshape(ROWS, NZ) for a in (source_term, conductivity, initial_field)))
    return result.reshape(NX, NY, NZ)


def solution(mesh):
    spec = P("gx", "gy", "grp")
    return jax.shard_map(block, mesh=mesh, in_specs=(spec,) * 3, out_specs=spec, check_vma=False)
```

```python
import functools

import jax
import jax.numpy as jnp
from jax import lax
from jax.experimental import pallas as pl
from jax.experimental.pallas import tpu as pltpu
from jax.sharding import PartitionSpec as P

MESH = pl.DeviceIdType.MESH
F32 = jnp.float32

NX, NY, NZ = 8, 16, 256
CX = NX // 2
ROWS = NX * NY
HALVES = (0, 1)
TILES = (0, 1)

FIRST_RATE = 0.8
KEEP = 60.0 / 41.0
FRESH = 40.0 / 41.0

FACES = (("gx", -1), ("gx", 1), ("gy", -1), ("gy", 1), ("grp", -1), ("grp", 1))
BOTH = (5, 5, 3, 3, 1, 1)
FINE = (4, 4, 2, 2, 1, 1)
TURN_SIZES = (BOTH, FINE, BOTH, FINE, BOTH, BOTH)
TURNS = len(TURN_SIZES)
OFFSETS = (0, 5, 10, 13, 16, 17)
SLOTS = 18
AXES = ((0, 1), (2, 3), (4, 5))
EDGES = [(a, b) for p, q in ((0, 1), (0, 2), (1, 2)) for a in AXES[p] for b in AXES[q]]


def iota(shape, dim):
    return lax.broadcasted_iota(jnp.int32, shape, dim)


def kernel(source_hbm, cond_hbm, field_hbm, out, source, half_cond, field, first, ky_lo, ky_hi, kz_lo, kz_hi,
           diag, inverse, partial, coarse_half, cky_lo, cky_hi, ckz_lo, ckz_hi, coarse_diag, coarse_inverse, coarse_first,
           faces, gains, scaled_gains, beside, edge_sent, edge_received, sent,
           received, in_sem, send_sem, recv_sem, edge_send_sem, edge_recv_sem):
    sub, lane = iota((2, 8, 128), 1), iota((2, 8, 128), 2)
    sub2, lane2 = iota((8, 128), 0), iota((8, 128), 1)
    even_sub2, even_lane2 = sub2 % 2 == 0, lane2 % 2 == 0
    zero = jnp.zeros((1, 8, 128), F32)

    place = {name: lax.axis_index(name) for name in ("grp", "gx", "gy")}
    size = {name: lax.axis_size(name) for name in ("grp", "gx", "gy")}
    present = []
    for name, step in FACES:
        present.append(place[name] > 0 if step < 0 else place[name] < size[name] - 1)

    def plane(ref, half, x):
        return ref[half, NY * x : NY * (x + 1), :].reshape(2, 8, 128)

    def put(ref, half, x, value):
        ref[half, NY * x : NY * (x + 1), :] = value.reshape(16, 128)

    def part(ref, half, x, t):
        return ref[half, NY * x + 8 * t : NY * x + 8 * t + 8, :]

    def put_part(ref, half, x, t, value):
        ref[half, NY * x + 8 * t : NY * x + 8 * t + 8, :] = value

    def y_lower(p, width=1):
        rolled = pltpu.roll(p, width, 1)
        return jnp.where(sub < width, jnp.concatenate([zero, rolled[:1]], axis=0), rolled)

    def y_upper(p, width=1):
        rolled = pltpu.roll(p, 8 - width, 1)
        return jnp.where(sub >= 8 - width, jnp.concatenate([rolled[1:], zero], axis=0), rolled)

    def z_lower(p0, p1, width=1):
        r0, r1 = pltpu.roll(p0, width, 2), pltpu.roll(p1, width, 2)
        return jnp.where(lane < width, 0.0, r0), jnp.where(lane < width, r0, r1)

    def z_upper(p0, p1, width=1):
        r0, r1 = pltpu.roll(p0, 128 - width, 2), pltpu.roll(p1, 128 - width, 2)
        return jnp.where(lane >= 128 - width, r1, r0), jnp.where(lane >= 128 - width, 0.0, r1)

    def neighbour_sum(ref, half_ref, kyl, kyh, kzl, kzh, x, count, width):
        p = [plane(ref, h, x) for h in HALVES]
        zl, zh = z_lower(p[0], p[1], width), z_upper(p[0], p[1], width)
        here = [plane(half_ref, h, x) for h in HALVES]
        total = []
        for h in HALVES:
            s = plane(kyl, h, x) * y_lower(p[h], width) + plane(kyh, h, x) * y_upper(p[h], width)
            s = s + (plane(kzl, h, x) * zl[h] + plane(kzh, h, x) * zh[h])
            if x > 0:
                s = s + (here[h] + plane(half_ref, h, x - 1)) * plane(ref, h, x - 1)
            if x < count - 1:
                s = s + (here[h] + plane(half_ref, h, x + 1)) * plane(ref, h, x + 1)
            total.append(s)
        return total

    def fine_neighbours(ref, x):
        return neighbour_sum(ref, half_cond, ky_lo, ky_hi, kz_lo, kz_hi, x, NX, 1)

    def coarse_neighbours(ref, x):
        return neighbour_sum(ref, coarse_half, cky_lo, cky_hi, ckz_lo, ckz_hi, x, CX, 2)

    def coefficients(ref, kyl, kyh, kzl, kzh, diag_ref, x, count, width):
        p = [plane(ref, h, x) for h in HALVES]
        zl, zh = z_lower(p[0], p[1], width), z_upper(p[0], p[1], width)
        for h in HALVES:
            yl, yh = y_lower(p[h], width), y_upper(p[h], width)
            put(kyl, h, x, p[h] + yl)
            put(kyh, h, x, p[h] + yh)
            put(kzl, h, x, p[h] + zl[h])
            put(kzh, h, x, p[h] + zh[h])
            s = 6.0 * p[h] + ((yl + yh) + (zl[h] + zh[h]))
            if x > 0:
                s = s + plane(ref, h, x - 1)
            if x < count - 1:
                s = s + plane(ref, h, x + 1)
            put(diag_ref, h, x, s)

    def restrict(lower, upper):
        s = lower + upper
        s = s + jnp.where(even_sub2, pltpu.roll(s, 7, 0), pltpu.roll(s, 1, 0))
        s = s + jnp.where(even_lane2, pltpu.roll(s, 127, 1), pltpu.roll(s, 1, 1))
        return 0.125 * s

    def slot(face, index):
        return OFFSETS[face] + index

    def message(store, turn, face):
        return store.at[turn, pl.ds(OFFSETS[face], TURN_SIZES[turn][face])]

    def pack_x(dest, fine, coarse=None):
        for face, x in ((0, 0), (1, NX - 1)):
            for h in HALVES:
                dest[slot(face, 2 * h) : slot(face, 2 * h) + 2] = plane(fine, h, x)
        if coarse is not None:
            for face, x in ((0, 0), (1, CX - 1)):
                p = [plane(coarse, h, x) for h in HALVES]
                dest[slot(face, 4)] = jnp.where(
                    even_sub2, jnp.where(even_lane2, p[0][0], p[1][0]), jnp.where(even_lane2, p[0][1], p[1][1]))

    def pack_face_y(dest, face, fine, coarse=None):
        row = (NY - 1) * (face - 2)
        for h in HALVES:
            dest[slot(face, h)] = fine[h, pl.ds(row, NX, stride=NY), :]
            if coarse is not None:
                dest[slot(face, 2), CX * h : CX * (h + 1), :] = coarse[h, pl.ds(row, CX, stride=NY), :]

    def pack_y(dest, fine, coarse=None):
        for face in AXES[1]:
            pack_face_y(dest, face, fine, coarse)

    def pack_z(dest, fine, coarse=None):
        for face, h, source_lane in ((4, 0, 0), (5, 1, 127)):
            packed = jnp.zeros((8, 128), F32)
            for ref, count, start in ((fine, NX, 0), (coarse, CX, 16)):
                if ref is None:
                    continue
                for x in range(count):
                    p = plane(ref, h, x)
                    for t in TILES:
                        m = start + 2 * x + t
                        packed = jnp.where(lane2 == m, pltpu.roll(p[t], (m - source_lane) % 128, 1), packed)
            dest[slot(face, 0)] = packed

    def fine_z(q, half, x, t):
        lanes = 2 * x + t
        column = q[slot(4 + half, 0)][:, lanes : lanes + 1]
        return jnp.where(lane2 == 127 * half, jnp.broadcast_to(column, (8, 128)), 0.0)

    def coarse_z(q, half, x, t):
        lanes = 16 + 2 * x + t
        column = q[slot(4 + half, 0)][:, lanes : lanes + 1]
        return jnp.where(lane2 // 2 == 63 * half, jnp.broadcast_to(column, (8, 128)), 0.0)

    def fine_y(q, half, x, t):
        return jnp.where(sub2 == 7 * t, jnp.broadcast_to(q[slot(2 + t, half), x : x + 1, :], (8, 128)), 0.0)

    def coarse_y(q, half, x, t):
        row = CX * half + x
        return jnp.where(sub2 // 2 == 3 * t, jnp.broadcast_to(q[slot(2 + t, 2), row : row + 1, :], (8, 128)), 0.0)

    def fine_xz(q, half, x, t):
        added = fine_z(q, half, x, t)
        if x == 0:
            added = added + q[slot(0, 2 * half + t)]
        if x == NX - 1:
            added = added + q[slot(1, 2 * half + t)]
        return added

    def coarse_plane(q, half, face, t):
        packed = q[slot(face, 4)]
        if half == 0:
            p = jnp.where(even_lane2, packed, pltpu.roll(packed, 1, 1))
        else:
            p = jnp.where(even_lane2, pltpu.roll(packed, 127, 1), packed)
        return jnp.where(even_sub2, p, pltpu.roll(p, 1, 0)) if t == 0 else jnp.where(even_sub2, pltpu.roll(p, 7, 0), p)

    def coarse_xz(q, half, x, t):
        added = coarse_z(q, half, x, t)
        if x == 0:
            added = added + coarse_plane(q, half, 0, t)
        if x == CX - 1:
            added = added + coarse_plane(q, half, 1, t)
        return added

    def peer(face):
        name, step = FACES[face]
        return {name: place[name] + step}

    def copy(turn, face):
        return pltpu.make_async_remote_copy(
            src_ref=message(sent, turn, face),
            dst_ref=message(received, turn, face ^ 1),
            send_sem=send_sem.at[turn, face],
            recv_sem=recv_sem.at[turn, face ^ 1],
            device_id=peer(face),
            device_id_type=MESH,
        )

    def arrival(turn, face):
        return pltpu.make_async_remote_copy(
            src_ref=message(sent, turn, face),
            dst_ref=message(received, turn, face),
            send_sem=send_sem.at[turn, face],
            recv_sem=recv_sem.at[turn, face],
            device_id=peer(face),
            device_id_type=MESH,
        )

    def send(turn, faces_):
        for face in faces_:
            @pl.when(present[face])
            def _():
                copy(turn, face).start()

    def wait(turn, faces_):
        for face in faces_:
            @pl.when(present[face])
            def _():
                arrival(turn, face).wait_recv()

    def edge_copy(k, landing):
        return pltpu.make_async_remote_copy(
            src_ref=edge_sent.at[k],
            dst_ref=edge_received.at[landing],
            send_sem=edge_send_sem.at[k],
            recv_sem=edge_recv_sem.at[landing],
            device_id={**peer(EDGES[k][0]), **peer(EDGES[k][1])},
            device_id_type=MESH,
        )

    edge_present = [jnp.logical_and(present[a], present[b]) for a, b in EDGES]

    def send_edges(ks):
        for k in ks:
            a, b = EDGES[k]

            @pl.when(edge_present[k])
            def _():
                edge_copy(k, EDGES.index((a ^ 1, b ^ 1))).start()

    def wait_edges(ks):
        for k in ks:
            @pl.when(edge_present[k])
            def _():
                edge_copy(k, k).wait_recv()

    def wait_sent_edges():
        for k in range(len(EDGES)):
            @pl.when(edge_present[k])
            def _():
                edge_copy(k, k).wait_send()

    def row(ref, *index):
        return jnp.broadcast_to(ref[index[0], index[1] : index[1] + 1, :], (8, 128))

    def column(value, lane_):
        return jnp.broadcast_to(value[:, lane_ : lane_ + 1], (8, 128))

    def pack_edges(ks, turn):
        cond, update = sent.at[0], sent.at[turn]
        for k in ks:
            a, b = EDGES[k]
            if a < 2 and b < 4:
                for h in HALVES:
                    for j, ref in ((0, cond), (2, update)):
                        x, i = (NX - 1) * a, CX * h + (CX - 1) * a
                        edge_sent[k, j + h : j + h + 1, :] = ref[slot(b, h), x : x + 1, :]
                        edge_sent[k, j + h + 4 : j + h + 5, :] = ref[slot(b, 2), i : i + 1, :]
            elif a < 2:
                c, u = cond[slot(b, 0)], update[slot(b, 0)]
                fine, coarse = 2 * (NX - 1) * a, 16 + 2 * (CX - 1) * a
                packed = pltpu.roll(u, (6 - coarse) % 128, 1)
                packed = jnp.where(lane2 < 6, pltpu.roll(c, (4 - coarse) % 128, 1), packed)
                packed = jnp.where(lane2 < 4, pltpu.roll(u, (2 - fine) % 128, 1), packed)
                edge_sent[k] = jnp.where(lane2 < 2, pltpu.roll(c, (-fine) % 128, 1) if fine else c, packed)
            else:
                h, t = b - 4, a - 2
                packed = pltpu.roll(update[slot(a, 2)], (35 - 127 * h) % 128, 1)
                packed = jnp.where(lane2 < 35, pltpu.roll(cond[slot(a, 2)], (34 - 127 * h) % 128, 1), packed)
                packed = jnp.where(lane2 < 34, pltpu.roll(update[slot(a, h)], (33 - 127 * h) % 128, 1), packed)
                packed = jnp.where(lane2 < 33, pltpu.roll(cond[slot(a, h)], (32 - 127 * h) % 128, 1), packed)
                rows = jnp.where(sub2 == 0, row(cond, slot(b, 0), 7 * t), row(update, slot(b, 0), 7 * t))
                edge_sent[k] = jnp.where(lane2 < 32, rows, packed)

    def add_edges(face, sides):
        def add(index, mask, c, u):
            i = slot(face, index)
            beside[i] = beside[i] + jnp.where(mask, (received[0, i] + c) * u, 0.0)

        for side in sides:
            k = EDGES.index((min(face, side), max(face, side)))
            if face < 2 and side < 4:
                t = side - 2
                r = [row(edge_received, k, j) for j in range(8)]
                for h in HALVES:
                    add(2 * h + t, sub2 == 7 * t, r[h], r[2 + h])
                add(4, sub2 == 7 * t, jnp.where(even_lane2, r[4], r[5]), jnp.where(even_lane2, r[6], r[7]))
            elif face < 2:
                h = side - 4
                lines = edge_received[k]
                r = [column(lines, j) for j in range(8)]
                for t in TILES:
                    add(2 * h + t, lane2 == 127 * h, r[t], r[2 + t])
                add(4, lane2 == 127 * h, jnp.where(even_sub2, r[4], r[5]), jnp.where(even_sub2, r[6], r[7]))
            elif face < 4 and side < 2:
                for h in HALVES:
                    add(h, sub2 == 7 * side, row(edge_received, k, h), row(edge_received, k, 2 + h))
                    add(2, sub2 == CX * h + (CX - 1) * side, row(edge_received, k, 4 + h), row(edge_received, k, 6 + h))
            elif face < 4:
                h = side - 4
                lines = edge_received[k]
                other = pltpu.roll(lines, 4, 0)
                add(h, lane2 == 127 * h, column(lines, 32), column(lines, 33))
                add(2, jnp.logical_and(lane2 // 2 == 63 * h, sub2 // 4 == h), column(other, 34), column(other, 35))
            elif side < 2:
                lines = edge_received[k]
                for t in TILES:
                    add(0, lane2 == 14 * side + t, column(lines, t), column(lines, 2 + t))
                    add(0, lane2 == 16 + 6 * side + t, column(lines, 4 + t), column(lines, 6 + t))
            else:
                t = side - 2
                shift = 1 if t else 127
                c, u = (pltpu.roll(row(edge_received, k, j), shift, 1) for j in (0, 1))
                fine = jnp.logical_and(sub2 == 7 * t, lane2 < 16)
                coarse = jnp.logical_and(sub2 // 2 == 3 * t, jnp.logical_and(lane2 >= 16, lane2 < 24))
                add(0, jnp.logical_and(jnp.logical_or(fine, coarse), lane2 % 2 == t), c, u)

    def neighbour_field(face):
        base = OFFSETS[face]
        for i in range(base, base + BOTH[face]):
            beside[i] = FRESH * received[4, i] * beside[i]
        if face < 2:
            for h in HALVES:
                for t in TILES:
                    i = slot(face, 2 * h + t)
                    beside[i] = received[3, i] + beside[i] + coarse_plane(beside, h, face, t)
        elif face < 4:
            for h in HALVES:
                spread = row(beside, slot(face, 2), CX * h)
                for x in range(1, CX):
                    spread = jnp.where(sub2 // 2 == x, row(beside, slot(face, 2), CX * h + x), spread)
                beside[slot(face, h)] = received[3, slot(face, h)] + beside[slot(face, h)] + spread
        else:
            i = slot(face, 0)
            value = beside[i]
            spread = jnp.zeros((8, 128), F32)
            for x in range(NX):
                spread = jnp.where(lane2 // 2 == x, pltpu.roll(value, (2 * x - 16 - 2 * (x // 2)) % 128, 1), spread)
            beside[i] = received[3, i] + value + spread

    def wait_sent(turn):
        for face in range(6):
            @pl.when(present[face])
            def _():
                copy(turn, face).wait_send()

    barrier = pltpu.get_barrier_semaphore()
    for face in (3, 2, 1, 0, 5, 4):
        @pl.when(present[face])
        def _():
            pl.semaphore_signal(barrier, inc=1, device_id=peer(face), device_id_type=MESH)

    loads = []
    for index, (hbm, ref) in enumerate(((cond_hbm, half_cond), (field_hbm, field), (source_hbm, source))):
        pair = []
        for h in HALVES:
            load = pltpu.make_async_copy(hbm.at[:, pl.ds(128 * h, 128)], ref.at[h], in_sem.at[index, h])
            load.start()
            pair.append(load)
        loads.append(pair)

    for face in range(6):
        @pl.when(jnp.logical_not(present[face]))
        def _():
            for turn in range(TURNS):
                count = TURN_SIZES[turn][face]
                received[turn, OFFSETS[face] : OFFSETS[face] + count] = jnp.zeros((count, 8, 128), F32)

    for k in range(len(EDGES)):
        @pl.when(jnp.logical_not(edge_present[k]))
        def _():
            edge_received[k] = jnp.zeros((8, 128), F32)

    for load in loads[0]:
        load.wait()
    for x in range(NX):
        for h in HALVES:
            put(half_cond, h, x, 0.5 * plane(half_cond, h, x))
    for x in range(CX):
        for h in HALVES:
            for t in TILES:
                put_part(coarse_half, h, x, t, restrict(part(half_cond, h, 2 * x, t), part(half_cond, h, 2 * x + 1, t)))
    for pack in (pack_y, pack_x):
        pack(sent.at[0], half_cond, coarse_half)
    pl.semaphore_wait(barrier, sum(p.astype(jnp.int32) for p in present))
    send(0, AXES[1])
    for load in loads[1]:
        load.wait()
    for axis, pack in ((1, pack_y), (0, pack_x), (2, pack_z)):
        if axis == 2:
            pack(sent.at[0], half_cond, coarse_half)
        if axis != 1:
            send(0, AXES[axis])
        pack(sent.at[1], field)
        send(1, AXES[axis])

    for x in range(NX):
        coefficients(half_cond, ky_lo, ky_hi, kz_lo, kz_hi, diag, x, NX, 1)
    for x in range(CX):
        coefficients(coarse_half, cky_lo, cky_hi, ckz_lo, ckz_hi, coarse_diag, x, CX, 2)
    for load in loads[2]:
        load.wait()

    def residual_part():
        for x in range(NX):
            total = fine_neighbours(field, x)
            for h in HALVES:
                put(partial, h, x, plane(source, h, x) - plane(diag, h, x) * plane(field, h, x) + total[h])

    residual_part()

    wait(0, (4, 5, 0, 1, 2, 3))
    for i in range(SLOTS):
        gains[i] = sent[0, i] + received[0, i]
    outside = received.at[0]
    for x in range(NX):
        for h in HALVES:
            for t in TILES:
                total = part(diag, h, x, t) + fine_xz(outside, h, x, t) + fine_y(outside, h, x, t)
                put_part(diag, h, x, t, total)
                put_part(inverse, h, x, t, 1.0 / total)
    for x in range(CX):
        for h in HALVES:
            for t in TILES:
                total = part(coarse_diag, h, x, t) + coarse_xz(outside, h, x, t) + coarse_y(outside, h, x, t)
                put_part(coarse_inverse, h, x, t, 1.0 / total)

    def add_near(ref):
        for x in range(NX):
            for h in HALVES:
                for t in TILES:
                    put_part(ref, h, x, t, part(ref, h, x, t) + fine_xz(faces, h, x, t))

    def smooth(x, t):
        for h in HALVES:
            pair = []
            for fx in (2 * x, 2 * x + 1):
                r = part(partial, h, fx, t) + fine_y(faces, h, fx, t)
                put_part(first, h, fx, t, FIRST_RATE * part(inverse, h, fx, t) * r)
                pair.append(r)
            put_part(coarse_first, h, x, t, 4.0 * FIRST_RATE * part(coarse_inverse, h, x, t) * restrict(*pair))

    def own_update():
        for x in range(CX):
            total = coarse_neighbours(coarse_first, x)
            coarse = [KEEP * plane(coarse_first, h, x) + FRESH * plane(coarse_inverse, h, x) * total[h] for h in HALVES]
            for fx in (2 * x, 2 * x + 1):
                total = fine_neighbours(first, fx)
                for h in HALVES:
                    fine = KEEP * plane(first, h, fx) + FRESH * plane(inverse, h, fx) * total[h]
                    put(partial, h, fx, plane(field, h, fx) + fine + coarse[h])

    def update_terms(turn, faces_):
        for face in faces_:
            for i in range(OFFSETS[face], OFFSETS[face] + BOTH[face]):
                faces[i] = scaled_gains[i] * received[turn, i]

    def finish(turn, last):
        wait(turn, near)
        update_terms(turn, near)
        for x in range(CX):
            for h in HALVES:
                for t in TILES:
                    coarse = coarse_xz(faces, h, x, t)
                    for fx in (2 * x, 2 * x + 1):
                        put_part(partial, h, fx, t, part(partial, h, fx, t) + coarse + fine_xz(faces, h, fx, t))
        for t in TILES:
            wait(turn, (2 + t,))
            update_terms(turn, (2 + t,))
            for x in range(CX):
                for h in HALVES:
                    coarse = coarse_y(faces, h, x, t)
                    for fx in (2 * x, 2 * x + 1):
                        value = part(partial, h, fx, t) + coarse + fine_y(faces, h, fx, t)
                        if last:
                            at = NY * fx + 8 * t
                            out[at : at + 8, 128 * h : 128 * (h + 1)] = value
                        else:
                            put_part(field, h, fx, t, value)

    near = (4, 5, 0, 1)
    every = near + (2, 3)

    def first_terms(faces_):
        for face in faces_:
            for i in range(OFFSETS[face], OFFSETS[face] + FINE[face]):
                faces[i] = gains[i] * received[1, i] - received[0, i] * sent[1, i]

    for axis, pack in ((1, pack_y), (0, pack_x)):
        pack(sent.at[4], inverse, coarse_inverse)
        send(4, AXES[axis])
    wait(1, near)
    first_terms(near)
    add_near(partial)
    for t in TILES:
        wait(1, (2 + t,))
        first_terms((2 + t,))
        for x in range(CX):
            smooth(x, t)
        pack_face_y(sent.at[2], 2 + t, first, coarse_first)
    pack_edges(range(4), 2)
    send_edges(range(4))
    pack_z(sent.at[2], first, coarse_first)
    pack_edges(range(4, 12), 2)
    send_edges((8, 9, 10, 11, 4, 5, 6, 7))
    send(2, AXES[1])
    pack_x(sent.at[2], first, coarse_first)
    send(2, near)

    own_update()
    pack_y(sent.at[3], partial)
    send(3, AXES[1])
    pack_x(sent.at[3], partial)
    send(3, AXES[0])
    pack_z(sent.at[3], partial)
    send(3, AXES[2])
    pack_z(sent.at[4], inverse, coarse_inverse)
    send(4, AXES[2])
    for i in range(SLOTS):
        scaled_gains[i] = FRESH * sent[4, i] * gains[i]
        beside[i] = gains[i] * sent[2, i]
    wait_sent(0)
    wait_sent(1)
    finish(2, False)
    residual_part()

    wait_edges(range(4, 12))
    for face in near:
        add_edges(face, (2, 3) if face >= 4 else (4, 5))
    for face in AXES[1]:
        add_edges(face, (4, 5))
    for face in AXES[2]:
        add_edges(face, (0, 1))
    wait(3, every)
    wait(4, every)
    def second_terms(faces_):
        for face in faces_:
            neighbour_field(face)
            for i in range(OFFSETS[face], OFFSETS[face] + FINE[face]):
                faces[i] = gains[i] * beside[i]

    second_terms(AXES[2])
    for x in range(NX):
        for h in HALVES:
            for t in TILES:
                put_part(partial, h, x, t, part(partial, h, x, t) + fine_z(faces, h, x, t))
    wait_edges(range(4))
    for face in AXES[1]:
        add_edges(face, (0, 1))
    for face in AXES[0]:
        add_edges(face, (2, 3))
    second_terms((2, 3, 0, 1))
    for face, x in ((0, 0), (1, NX - 1)):
        for h in HALVES:
            for t in TILES:
                put_part(partial, h, x, t, part(partial, h, x, t) + faces[slot(face, 2 * h + t)])
    for t in TILES:
        for x in range(CX):
            smooth(x, t)
        pack_face_y(sent.at[5], 2 + t, first, coarse_first)
        send(5, (2 + t,))
    pack_x(sent.at[5], first, coarse_first)
    send(5, AXES[0])
    pack_z(sent.at[5], first, coarse_first)
    send(5, AXES[2])
    own_update()
    for turn in (2, 3, 4):
        wait_sent(turn)
    wait_sent_edges()
    wait_sent(TURNS - 1)
    finish(5, True)


def block(source_term, conductivity, initial_field):
    def fine():
        return pltpu.VMEM((2, ROWS, 128), F32)

    def coarse():
        return pltpu.VMEM((2, CX * NY, 128), F32)

    hbm = pl.BlockSpec(memory_space=pltpu.HBM)
    result = pl.pallas_call(
        kernel,
        out_shape=pltpu.VMEM((ROWS, NZ), F32),
        in_specs=[hbm] * 3,
        out_specs=pl.BlockSpec(memory_space=pltpu.VMEM),
        scratch_shapes=[
            *(fine() for _ in range(11)),
            *(coarse() for _ in range(8)),
            *(pltpu.VMEM((SLOTS, 8, 128), F32) for _ in range(4)),
            *(pltpu.VMEM((len(EDGES), 8, 128), F32) for _ in range(2)),
            *(pltpu.VMEM((TURNS, SLOTS, 8, 128), F32) for _ in range(2)),
            pltpu.SemaphoreType.DMA((3, 2)),
            *(pltpu.SemaphoreType.DMA((TURNS, 6)) for _ in range(2)),
            *(pltpu.SemaphoreType.DMA((len(EDGES),)) for _ in range(2)),
        ],
        compiler_params=pltpu.CompilerParams(collective_id=0, has_side_effects=True),
    )(*(a.reshape(ROWS, NZ) for a in (source_term, conductivity, initial_field)))
    return result.reshape(NX, NY, NZ)


def solution(mesh):
    spec = P("gx", "gy", "grp")
    return jax.shard_map(block, mesh=mesh, in_specs=(spec,) * 3, out_specs=spec, check_vma=False)
```
